256 devices in a mesh: dp: 32 (over z, x_hi, core), space: 8 (over x_lo, y).
Axes of the slice: x: 4 (x_hi: 2, x_lo: 2; x = x_hi * 2 + x_lo), y: 4, z: 8, core: 2. Of those that a mesh axis runs over, the one named last changes fastest.
Arguments:
- volume: bfloat16 [256, 4, 32, 16, 128], P('dp', None, 'space'), may hold values from -8 to 8
- conv_kernel: bfloat16 [32, 108], replicated, may hold values from -0.625 to 0.625
- dense_weight: bfloat16 [512, 128], replicated, may hold values from -0.25 to 0.25
- cotangent: bfloat16 [256, 128], P(('dp', 'space')), may hold values from -6 to 6
Outputs:
- step_conv: float32 [32, 108], replicated
- step_dense: float32 [512, 128], P('space', 'dp')
The draws below stay inside these ranges and needn't reach their ends.
All inputs are finite; a program needn't handle non-finite values. Where the reference program divides by a largest or mean magnitude, that divisor is 1e-20 or more.
Results may differ from the reference program's by a relative error of at most 0.0099.
Values may be sent and summed in bfloat16 or wider, within the bound.
No kernel may reach another device: no remote copies, remote signals or barrier semaphores. Data moves between devices by JAX's collectives and lax.ppermute only.
A program may use at most 64 MiB of HBM per device.

```python
import jax
import jax.numpy as jnp
from jax import lax

CIN = 4
C = 32
H = 128
PC = 2
NS_STEPS = 8
XS = 4
NY = 16
NZ = 128
NB = 256
NX = 32
F = 512
N_SPACE = 8


def draw_volume(key, part):
    key_mean = jax.random.fold_in(key, 11)
    key_scale = jax.random.fold_in(key, 12)
    key_noise = jax.random.fold_in(key, 13)
    region = (NB, CIN, NX, 1, 1)
    offsets = jax.random.uniform(key_mean, region, jnp.float32, -1.0, 1.0)
    scales = jnp.exp(jax.random.uniform(key_scale, region, jnp.float32, -0.7, 0.7))
    noise = jax.random.normal(key_noise, (NB, CIN, NX, NY, NZ), jnp.float32)
    return jnp.clip(offsets + scales * noise, -8.0, 8.0).astype(jnp.bfloat16)


def levels(rng, shape, split, smallest, top_value):
    level = 1.0
    for axis_at, blocks in split:
        heights = jax.random.uniform(jax.random.fold_in(jax.random.fold_in(rng, 6), axis_at), (blocks,), jnp.float32, smallest / len(split), top_value / len(split))
        level = level * jnp.repeat(jnp.exp(heights), shape[axis_at] // blocks).reshape((-1,) + (1,) * (len(shape) - 1 - axis_at))
    return level


def scatter_about(key, extent, width, most, shards=(), held_as=jnp.bfloat16):
    result = jax.random.normal(key, extent, jnp.float32) * width
    if len(shards) > 0:
        result = levels(key, extent, shards, -0.22, 0.18) * result
    return jnp.clip(result, min=-most, max=most).astype(held_as)


def setup_inputs(seed: int = 0) -> dict:
    arg_keys = jax.random.split(jax.random.key(seed), 5)
    volume = draw_volume(jax.random.fold_in(arg_keys[4], 71), 0)
    conv_kernel = scatter_about(arg_keys[1], (C, CIN * 27), (CIN * 27) ** -0.5, 0.625)
    dense_weight = scatter_about(arg_keys[2], (F, H), F ** -0.5, 0.25)
    cotangent = scatter_about(arg_keys[3], (NB, H), 1.0, 6.0, ((0, 256),))
    return dict(volume=volume, conv_kernel=conv_kernel, dense_weight=dense_weight, cotangent=cotangent)


LEAK_SLOPE = 0.3
DAMPING = 0.1
KL_BOUND = 0.0001
LEARN_RATE = 0.01
HIGHEST = lax.Precision.HIGHEST
CONTRACT = (((1,), (1,)), ((), ()))
LEADING = (((0,), (0,)), ((), ()))

def patch_matrix(slab_rim):
    channels, planes_rim, height, length = slab_rim.shape
    planes = planes_rim - 2
    padded = jnp.pad(slab_rim, ((0, 0), (0, 0), (1, 1), (1, 1)))
    pieces = []
    for shift_x in range(3):
        for shift_y in range(3):
            for shift_z in range(3):
                pieces.append(padded[:, shift_x:shift_x + planes, shift_y:shift_y + height, shift_z:shift_z + length])
    return jnp.stack(pieces, axis=1).reshape(channels * 27, planes * height * length)

def damped_inverse(factor):
    factor_order = factor.shape[0]
    identity = jnp.eye(factor_order, dtype=jnp.float32)
    damped = factor + DAMPING * jnp.trace(factor) / factor_order * identity
    row_bound = jnp.max(lax.optimization_barrier(jnp.sum(jnp.abs(damped), axis=1)))
    iterate = identity / row_bound
    for newton_step in range(NS_STEPS):
        product = jnp.dot(damped, iterate, precision=HIGHEST)
        iterate = jnp.dot(iterate, 2.0 * identity - product, precision=HIGHEST)
    return iterate

def reference(volume, conv_kernel, dense_weight, cotangent):
    patch_rows = CIN * 27

    def forward_pass(moment_in, sample):
        slab_rim = jnp.pad(sample, ((0, 0), (1, 1), (0, 0), (0, 0)))
        patches = patch_matrix(slab_rim)
        before = jnp.dot(conv_kernel, patches, preferred_element_type=jnp.float32)
        active = jnp.where(before > 0, before, LEAK_SLOPE * before)
        shaped = active.reshape(C, N_SPACE, XS, PC, NY // PC, NZ)
        pooled = lax.optimization_barrier(jnp.mean(shaped, axis=(2, 4, 5))).transpose(1, 0, 2).reshape(-1).astype(jnp.bfloat16)
        gram = lax.dot_general(patches, patches, CONTRACT, preferred_element_type=jnp.float32)
        return (moment_in + gram, pooled)
    moment_in, features = lax.scan(forward_pass, jnp.zeros((patch_rows, patch_rows), jnp.float32), volume)
    feature_grad = lax.dot_general(cotangent, dense_weight, CONTRACT, preferred_element_type=jnp.float32).astype(jnp.bfloat16)

    def backward_pass(totals, pair):
        sample, region_grad = pair
        slab_rim = jnp.pad(sample, ((0, 0), (1, 1), (0, 0), (0, 0)))
        patches = patch_matrix(slab_rim)
        before = jnp.dot(conv_kernel, patches, preferred_element_type=jnp.float32)
        region_grid = region_grad.reshape(N_SPACE, C, PC).transpose(1, 0, 2).astype(jnp.float32)
        spread = jnp.broadcast_to(region_grid.reshape(C, N_SPACE, 1, PC, 1, 1), (C, N_SPACE, XS, PC, NY // PC, NZ)).reshape(C, -1)
        signal = (jnp.where(before > 0, 1.0, LEAK_SLOPE) * spread).astype(jnp.bfloat16)
        moment_out = totals[0] + lax.dot_general(signal, signal, CONTRACT, preferred_element_type=jnp.float32)
        gradient = totals[1] + lax.dot_general(signal, patches, CONTRACT, preferred_element_type=jnp.float32)
        return ((moment_out, gradient), None)
    start_totals = (jnp.zeros((C, C), jnp.float32), jnp.zeros((C, patch_rows), jnp.float32))
    (moment_out, conv_sum), unused = lax.scan(backward_pass, start_totals, (volume, feature_grad))
    cell_count = NB * NX * NY * NZ
    conv_in = moment_in / cell_count
    conv_out = moment_out / cell_count
    conv_grad = conv_sum / cell_count
    dense_in = lax.dot_general(features, features, LEADING, preferred_element_type=jnp.float32) / NB
    dense_out = lax.dot_general(cotangent, cotangent, LEADING, preferred_element_type=jnp.float32) / NB
    dense_grad = lax.dot_general(features, cotangent, LEADING, preferred_element_type=jnp.float32) / NB
    inv_conv_in = damped_inverse(conv_in)
    inv_conv_out = damped_inverse(conv_out)
    inv_dense_in = damped_inverse(dense_in)
    inv_dense_out = damped_inverse(dense_out)
    delta_conv = jnp.dot(jnp.dot(inv_conv_out, conv_grad, precision=HIGHEST), inv_conv_in, precision=HIGHEST)
    delta_dense = jnp.dot(jnp.dot(inv_dense_in, dense_grad, precision=HIGHEST), inv_dense_out, precision=HIGHEST)
    total = jnp.sum(delta_conv * conv_grad) + jnp.sum(delta_dense * dense_grad)
    scaling = jnp.minimum(1.0, jnp.sqrt(KL_BOUND / (LEARN_RATE * LEARN_RATE * total)))
    return (scaling * delta_conv, scaling * delta_dense)
```

```python
import functools

import jax
import jax.numpy as jnp
from jax import lax
from jax.experimental import pallas as pl
from jax.experimental.pallas import tpu as pltpu
from jax.sharding import PartitionSpec as P

PC = 2
NS_STEPS = 8

LEAK_SLOPE = 0.3
DAMPING = 0.1
KL_BOUND = 0.0001
LEARN_RATE = 0.01
HIGHEST = lax.Precision.HIGHEST
CONTRACT = (((1,), (1,)), ((), ()))
LEADING = (((0,), (0,)), ((), ()))
BOTH = ("dp", "space")
F32 = jnp.float32
BF16 = jnp.bfloat16


def exchange(x, axes):
    return lax.all_to_all(x, axes, split_axis=0, concat_axis=0, tiled=True)


def gather_from(x, axes, peers):
    return exchange(jnp.broadcast_to(x[None], (peers,) + x.shape), axes)


def conv_kernel_body(
    sizes, vol_ref, before_ref, after_ref, bands_ref, weight_ref, cot_ref,
    pool_ref, moments_ref, shifted, stacked, grads, acc, acc_out,
):
    channels, planes, height, length, filters, samples = sizes
    rim = planes + 2
    per_plane = channels * 9
    rows = rim * per_plane
    cells = height * length
    half = cells // PC
    top = planes * filters
    step = pl.program_id(0)

    @pl.when(step == 0)
    def _():
        shifted[...] = jnp.zeros_like(shifted)
        acc[...] = jnp.zeros_like(acc)
        acc_out[...] = jnp.zeros_like(acc_out)
        pool_ref[...] = jnp.zeros_like(pool_ref)
        grads[...] = lax.dot_general(
            weight_ref[...], cot_ref[...], CONTRACT, preferred_element_type=F32
        ).astype(BF16).astype(F32)

    lane = lax.broadcasted_iota(jnp.int32, (height, length), 1)
    for plane in range(rim):
        for channel in range(channels):
            if plane == 0:
                value = before_ref[0, channel, 0]
            elif plane == rim - 1:
                value = after_ref[0, channel, 0]
            else:
                value = vol_ref[0, channel, plane - 1]
            value = value.astype(F32)
            moved = (
                jnp.where(lane == 0, 0.0, pltpu.roll(value, 1, 1)),
                value,
                jnp.where(lane == length - 1, 0.0, pltpu.roll(value, length - 1, 1)),
            )
            for j in range(3):
                for k in range(3):
                    row = plane * per_plane + channel * 9 + j * 3 + k
                    shifted[pl.ds((2 - j) * rows + row, height, stride=rows), :] = moved[k]
    for y in range(height):
        stacked[top:, y * length:(y + 1) * length] = shifted[
            (y + 1) * rows:(y + 2) * rows, :
        ].astype(BF16)

    column = lax.broadcasted_iota(jnp.int32, (filters * PC, samples), 1)
    grad_all = jnp.sum(jnp.where(column == step, grads[...], 0.0), axis=1, keepdims=True)
    low_all = (LEAK_SLOPE * grad_all).astype(BF16).astype(F32)
    pooled = []
    for part in range(PC):
        lanes = slice(part * half, (part + 1) * half)
        pre = jnp.dot(bands_ref[...], stacked[top:, lanes], preferred_element_type=F32)
        active = jnp.where(pre > 0, pre, LEAK_SLOPE * pre)
        total = active[0:filters]
        for plane in range(1, planes):
            total = total + active[plane * filters:(plane + 1) * filters]
        pooled.append(jnp.sum(total, axis=1, keepdims=True))
        grad = jnp.concatenate([grad_all[part * filters:(part + 1) * filters]] * planes, axis=0)
        low = jnp.concatenate([low_all[part * filters:(part + 1) * filters]] * planes, axis=0)
        stacked[0:top, lanes] = jnp.where(pre > 0, grad, low).astype(BF16)
    pooled = jnp.concatenate(pooled, axis=0) * (1.0 / (planes * half))
    spot = lax.broadcasted_iota(jnp.int32, pool_ref.shape, 1)
    pool_ref[...] = jnp.where(spot == step, pooled, pool_ref[...])
    acc[:, :rows] += lax.dot_general(
        stacked[...], stacked[top:, :], CONTRACT, preferred_element_type=F32
    )
    acc_out[...] += lax.dot_general(
        stacked[0:top, :], stacked[0:top, :], CONTRACT, preferred_element_type=F32
    )

    @pl.when(step == pl.num_programs(0) - 1)
    def _():
        width = acc.shape[1]
        wide = 3 * per_plane
        moment_in = jnp.zeros((wide, 128), F32)
        gradient = jnp.zeros((filters, 128), F32)
        moment_out = jnp.zeros((filters, 128), F32)
        for plane in range(planes):
            start = plane * per_plane
            turn = (width - start) % width
            block = acc[top + start:top + start + wide, :]
            moment_in += (pltpu.roll(block, turn, 1) if turn else block)[:, :128]
            block = acc[plane * filters:(plane + 1) * filters, :]
            gradient += (pltpu.roll(block, turn, 1) if turn else block)[:, :128]
            block = acc_out[plane * filters:(plane + 1) * filters, :]
            turn = (top - plane * filters) % top
            moment_out += pltpu.roll(block, turn, 1) if turn else block
        moments_ref[...] = jnp.zeros_like(moments_ref)
        lane_in = lax.broadcasted_iota(jnp.int32, (wide, 128), 1)
        lane_out = lax.broadcasted_iota(jnp.int32, (filters, 128), 1)
        moments_ref[0:wide, :] = jnp.where(lane_in < wide, moment_in, 0.0)
        moments_ref[112:112 + filters, :] = jnp.where(lane_out < wide, gradient, 0.0)
        moments_ref[144:144 + filters, :] = jnp.where(lane_out < filters, moment_out, 0.0)


def conv_moments(volume, before, after, bands, weight, cot_group, filters, peers):
    samples, channels, planes, height, length = volume.shape
    per_plane = channels * 9
    rows = (planes + 2) * per_plane
    top = planes * filters
    sizes = (channels, planes, height, length, filters, samples)
    whole = lambda shape: pl.BlockSpec(shape, lambda b: (0,) * len(shape))
    return pl.pallas_call(
        functools.partial(conv_kernel_body, sizes),
        grid=(samples,),
        in_specs=[
            pl.BlockSpec((1, channels, planes, height, length), lambda b: (b, 0, 0, 0, 0)),
            pl.BlockSpec((1, channels, 1, height, length), lambda b: (b, 0, 0, 0, 0)),
            pl.BlockSpec((1, channels, 1, height, length), lambda b: (b, 0, 0, 0, 0)),
            whole(bands.shape),
            whole(weight.shape),
            whole(cot_group.shape),
        ],
        out_specs=[whole((filters * PC, 128)), whole((peers, 128))],
        out_shape=[
            jax.ShapeDtypeStruct((filters * PC, 128), F32),
            jax.ShapeDtypeStruct((peers, 128), F32),
        ],
        scratch_shapes=[
            pltpu.VMEM(((height + 2) * rows, length), F32),
            pltpu.VMEM((top + rows, height * length), BF16),
            pltpu.VMEM((filters * PC, samples), F32),
            pltpu.VMEM((top + rows, 256), F32),
            pltpu.VMEM((top, top), F32),
        ],
        compiler_params=pltpu.CompilerParams(vmem_limit_bytes=48 * 1024 * 1024),
    )(volume, before, after, bands, weight, cot_group)


def exact_dot(a, b):
    return jnp.dot(a, b, precision=HIGHEST, preferred_element_type=F32)


def unit(order):
    row = lax.broadcasted_iota(jnp.int32, (order, order), 0)
    column = lax.broadcasted_iota(jnp.int32, (order, order), 1)
    return row == column


def scalar_sum(x):
    return jnp.sum(jnp.sum(x, axis=0, keepdims=True), axis=1, keepdims=True)


def residual(factor, order):
    size = factor.shape[0]
    eye = unit(size)
    trace = scalar_sum(jnp.where(eye, factor, 0.0))
    damping = DAMPING * trace / order
    sums = jnp.sum(jnp.abs(factor), axis=0, keepdims=True) + damping
    bound = jnp.max(sums, axis=1, keepdims=True)
    inside = lax.broadcasted_iota(jnp.int32, (size, size), 0) < order
    start = jnp.where(jnp.logical_and(eye, inside), 1.0 - damping / bound, 0.0)
    return start - factor / bound, bound


def dense_kernel_body(slab_count, place_ref, feat_ref, cot_ref, delta_ref, total_ref, whole):
    groups, spaces, local, width = feat_ref.shape
    count = groups * local
    for slab in range(0, spaces, 2):
        pair = [
            feat_ref[:, slab + i].astype(F32).reshape(count, width) for i in range(2)
        ]
        whole[:, slab * width:(slab + 2) * width] = jnp.concatenate(pair, axis=1).astype(BF16)
    cot = cot_ref[...]
    feats = whole[...]
    scale = 1.0 / count
    gram = lax.dot_general(feats, feats, CONTRACT, preferred_element_type=F32) * scale
    dense_in = lax.dot_general(feats, feats, LEADING, preferred_element_type=F32) * scale
    dense_out = lax.dot_general(cot, cot, LEADING, preferred_element_type=F32) * scale
    order = spaces * width
    eye = unit(count)
    damping = DAMPING * scalar_sum(jnp.where(eye, gram, 0.0)) / order
    sums = jnp.sum(jnp.abs(dense_in), axis=0, keepdims=True) + damping
    bound = jnp.max(sums, axis=1, keepdims=True)
    left = jnp.where(eye, 1.0 - damping / bound, 0.0) - gram / bound
    right, bound_out = residual(dense_out, dense_out.shape[0])
    cot_wide = cot.astype(F32)
    held = cot_wide * (scale / bound / bound_out)
    for newton_step in range(NS_STEPS):
        held = held + exact_dot(left, held)
        held = held + exact_dot(held, right)
        if newton_step < NS_STEPS - 1:
            left = exact_dot(left, left)
            right = exact_dot(right, right)
    total_ref[...] = scalar_sum(held * exact_dot(gram, cot_wide))
    mine = feat_ref[:, place_ref[0]].astype(F32).reshape(count, width)
    delta_ref[...] = lax.dot_general(
        mine, held, LEADING, precision=HIGHEST, preferred_element_type=F32
    )


def dense_delta(place, feats, cot):
    groups, spaces, local, width = feats.shape
    count = groups * local
    outputs = cot.shape[1]
    vmem = pl.BlockSpec(memory_space=pltpu.VMEM)
    return pl.pallas_call(
        functools.partial(dense_kernel_body, spaces),
        in_specs=[pl.BlockSpec(memory_space=pltpu.SMEM), vmem, vmem],
        out_specs=[vmem, vmem],
        out_shape=[
            jax.ShapeDtypeStruct((width, outputs), F32),
            jax.ShapeDtypeStruct((1, 1), F32),
        ],
        scratch_shapes=[pltpu.VMEM((count, spaces * width), BF16)],
        compiler_params=pltpu.CompilerParams(vmem_limit_bytes=48 * 1024 * 1024),
    )(place, feats, cot)


def final_kernel_body(
    filters, patch_rows, cells, moments_ref, dense_ref, total_ref, order_ref,
    step_conv_ref, step_dense_ref,
):
    scale = 1.0 / cells
    pad = jnp.zeros((128 - 112, 128), F32)
    conv_in = jnp.concatenate([moments_ref[0:112, :], pad], axis=0) * scale
    conv_grad = moments_ref[112:112 + filters, :] * scale
    conv_out = moments_ref[144:144 + filters, 0:filters] * scale
    right, bound_in = residual(conv_in, patch_rows)
    left, bound_out = residual(conv_out, filters)
    held = conv_grad / bound_in / bound_out
    for newton_step in range(NS_STEPS):
        held = held + exact_dot(left, held)
        held = held + exact_dot(held, right)
        if newton_step < NS_STEPS - 1:
            left = exact_dot(left, left)
            right = exact_dot(right, right)
    total = scalar_sum(held * conv_grad) + total_ref[...]
    scaling = jnp.minimum(1.0, jnp.sqrt(KL_BOUND / (LEARN_RATE * LEARN_RATE * total)))
    moved = exact_dot(held, order_ref[...])
    step_conv_ref[...] = scaling * moved[:, 0:patch_rows]
    step_dense_ref[...] = scaling * dense_ref[...]


def final_steps(moments, dense_block, dense_total, order, filters, patch_rows, cells):
    vmem = pl.BlockSpec(memory_space=pltpu.VMEM)
    return pl.pallas_call(
        functools.partial(final_kernel_body, filters, patch_rows, cells),
        in_specs=[vmem] * 4,
        out_specs=[vmem] * 2,
        out_shape=[
            jax.ShapeDtypeStruct((filters, patch_rows), F32),
            jax.ShapeDtypeStruct(dense_block.shape, F32),
        ],
        compiler_params=pltpu.CompilerParams(vmem_limit_bytes=32 * 1024 * 1024),
    )(moments, dense_block, dense_total, order)


def column_order(channels):
    row = lax.broadcasted_iota(jnp.int32, (128, 128), 0)
    column = lax.broadcasted_iota(jnp.int32, (128, 128), 1)
    channel, rest = column // 27, column % 27
    source = (rest // 9) * (9 * channels) + channel * 9 + rest % 9
    return jnp.where(jnp.logical_and(row == source, column < 27 * channels), 1.0, 0.0)


def on_device(volume, conv_kernel, dense_weight, cotangent):
    spaces = lax.axis_size("space")
    groups = lax.axis_size("dp")
    peers = spaces * groups
    samples, channels, planes, height, length = volume.shape
    filters, patch_rows = conv_kernel.shape
    slab = filters * PC

    up = [(i, i + 1) for i in range(spaces - 1)]
    down = [(j, i) for i, j in up]
    before = lax.ppermute(volume[:, :, planes - 1:], "space", up)
    after = lax.ppermute(volume[:, :, :1], "space", down)
    cot_group = gather_from(cotangent[0], "space", spaces)
    cot_all = gather_from(cotangent, BOTH, peers).reshape(peers, -1)

    mixed = conv_kernel.reshape(filters, channels, 3, 9).transpose(0, 2, 1, 3)
    mixed = mixed.reshape(filters, patch_rows)
    spare = (planes + 2) * channels * 9 - patch_rows
    bands = jnp.concatenate(
        [
            jnp.pad(mixed, ((0, 0), (p * channels * 9, spare - p * channels * 9)))
            for p in range(planes)
        ],
        axis=0,
    )
    place = lax.axis_index("space")
    weight = lax.dynamic_slice_in_dim(dense_weight, place * slab, slab, 0)
    weight = weight.reshape(filters, PC, -1).transpose(1, 0, 2).reshape(slab, -1)

    pool, moments = conv_moments(
        volume, before, after, bands, weight, cot_group, filters, peers
    )
    pooled = pool[:, :samples].reshape(PC, filters, samples).transpose(2, 1, 0)
    pooled = pooled.reshape(samples, slab).astype(BF16)

    feats = gather_from(pooled, BOTH, peers).reshape(groups, spaces, samples, slab)
    partial = exchange(moments, BOTH)
    mine = jnp.sum(partial, axis=0)
    reduced = gather_from(mine, BOTH, peers)

    delta, dense_total = dense_delta(place.reshape(1), feats, cot_all)
    share = cotangent.shape[1] // groups
    dense_block = lax.dynamic_slice_in_dim(delta, lax.axis_index("dp") * share, share, 1)
    cells = samples * groups * planes * spaces * height * length
    return final_steps(
        reduced, dense_block, dense_total, column_order(channels), filters, patch_rows, cells
    )


def solution(mesh):
    placed = (P("dp", None, "space", None, None), P(), P(), P(BOTH, None))
    return jax.shard_map(
        on_device, mesh=mesh, in_specs=placed, out_specs=(P(), P("space", "dp")), check_vma=False
    )
```

```python
import functools

import jax
import jax.numpy as jnp
from jax import lax
from jax.experimental import pallas as pl
from jax.experimental.pallas import tpu as pltpu
from jax.sharding import PartitionSpec as P

PC = 2
NS_STEPS = 8

LEAK_SLOPE = 0.3
DAMPING = 0.1
KL_BOUND = 0.0001
LEARN_RATE = 0.01
HIGHEST = lax.Precision.HIGHEST
CONTRACT = (((1,), (1,)), ((), ()))
LEADING = (((0,), (0,)), ((), ()))
BOTH = ("dp", "space")
F32 = jnp.float32
BF16 = jnp.bfloat16
ROWS_IN = 112


def exchange(x, axes):
    return lax.all_to_all(x, axes, split_axis=0, concat_axis=0, tiled=True)


def gather_from(x, axes, peers):
    return exchange(jnp.broadcast_to(x[None], (peers,) + x.shape), axes)


def conv_kernel_body(
    sizes, vol_ref, before_ref, after_ref, bands_ref, weight_ref, cot_ref,
    feats_ref, moments_ref, pool_ref, shifted, stacked, grads, acc, acc_out,
):
    channels, planes, height, length, filters, samples = sizes
    rim = planes + 2
    per_plane = channels * 9
    rows = rim * per_plane
    cells = height * length
    half = cells // PC
    top = planes * filters
    step = pl.program_id(0)

    @pl.when(step == 0)
    def _():
        shifted[...] = jnp.zeros_like(shifted)
        acc[...] = jnp.zeros_like(acc)
        acc_out[...] = jnp.zeros_like(acc_out)
        pool_ref[...] = jnp.zeros_like(pool_ref)
        grads[...] = lax.dot_general(
            weight_ref[...], cot_ref[...], CONTRACT, preferred_element_type=F32
        ).astype(BF16).astype(F32)

    lane = lax.broadcasted_iota(jnp.int32, (height, length), 1)
    for plane in range(rim):
        for channel in range(channels):
            if plane == 0:
                value = before_ref[0, channel, 0]
            elif plane == rim - 1:
                value = after_ref[0, channel, 0]
            else:
                value = vol_ref[0, channel, plane - 1]
            value = value.astype(F32)
            moved = (
                jnp.where(lane == 0, 0.0, pltpu.roll(value, 1, 1)),
                value,
                jnp.where(lane == length - 1, 0.0, pltpu.roll(value, length - 1, 1)),
            )
            for j in range(3):
                for k in range(3):
                    row = plane * per_plane + channel * 9 + j * 3 + k
                    shifted[pl.ds((2 - j) * rows + row, height, stride=rows), :] = moved[k]
    for y in range(height):
        stacked[top:, y * length:(y + 1) * length] = shifted[
            (y + 1) * rows:(y + 2) * rows, :
        ].astype(BF16)

    column = lax.broadcasted_iota(jnp.int32, (filters * PC, samples), 1)
    grad_all = jnp.sum(jnp.where(column == step, grads[...], 0.0), axis=1, keepdims=True)
    low_all = (LEAK_SLOPE * grad_all).astype(BF16).astype(F32)
    pooled = []
    for part in range(PC):
        lanes = slice(part * half, (part + 1) * half)
        pre = jnp.dot(bands_ref[...], stacked[top:, lanes], preferred_element_type=F32)
        active = jnp.where(pre > 0, pre, LEAK_SLOPE * pre)
        total = active[0:filters]
        for plane in range(1, planes):
            total = total + active[plane * filters:(plane + 1) * filters]
        pooled.append(jnp.sum(total, axis=1, keepdims=True))
        grad = jnp.concatenate([grad_all[part * filters:(part + 1) * filters]] * planes, axis=0)
        low = jnp.concatenate([low_all[part * filters:(part + 1) * filters]] * planes, axis=0)
        stacked[0:top, lanes] = jnp.where(pre > 0, grad, low).astype(BF16)
    pooled = jnp.concatenate(pooled, axis=0) * (1.0 / (planes * half))
    spot = lax.broadcasted_iota(jnp.int32, pool_ref.shape, 1)
    pool_ref[...] = jnp.where(spot == step, pooled, pool_ref[...])
    acc[0:top + rows, :rows] += lax.dot_general(
        stacked[...], stacked[top:, :], CONTRACT, preferred_element_type=F32
    )
    acc_out[...] += lax.dot_general(
        stacked[0:top, :], stacked[0:top, :], CONTRACT, preferred_element_type=F32
    )

    @pl.when(step == pl.num_programs(0) - 1)
    def _():
        width = acc.shape[1]
        wide = 3 * per_plane
        moment_in = jnp.zeros((ROWS_IN, 128), F32)
        gradient = jnp.zeros((filters, 128), F32)
        moment_out = jnp.zeros((filters, 128), F32)
        for plane in range(planes):
            start = plane * per_plane
            turn = (width - start) % width
            block = acc[top + start:top + start + ROWS_IN, :]
            moment_in += (pltpu.roll(block, turn, 1) if turn else block)[:, :128]
            block = acc[plane * filters:(plane + 1) * filters, :]
            gradient += (pltpu.roll(block, turn, 1) if turn else block)[:, :128]
            block = acc_out[plane * filters:(plane + 1) * filters, :]
            turn = (top - plane * filters) % top
            moment_out += pltpu.roll(block, turn, 1) if turn else block
        row_in = lax.broadcasted_iota(jnp.int32, (ROWS_IN, 128), 0)
        lane_in = lax.broadcasted_iota(jnp.int32, (ROWS_IN, 128), 1)
        moment_in = jnp.where(jnp.maximum(row_in, lane_in) < wide, moment_in, 0.0)
        lane_out = lax.broadcasted_iota(jnp.int32, (filters, 128), 1)
        gradient = jnp.where(lane_out < wide, gradient, 0.0)
        packed = jnp.concatenate(
            [
                moment_in[:, :64],
                moment_in[64:, 64:],
                gradient[:, :64],
                gradient[:, 64:],
                moment_out[:, :64],
            ],
            axis=0,
        )
        high = packed.astype(BF16)
        low = (packed - high.astype(F32)).astype(BF16)
        moments_ref[...] = jnp.concatenate([high, low], axis=1)
        feats_ref[...] = jnp.transpose(pool_ref[...])[:samples].astype(BF16)


def conv_moments(volume, before, after, bands, weight, cot_group, filters, peers):
    samples, channels, planes, height, length = volume.shape
    per_plane = channels * 9
    rows = (planes + 2) * per_plane
    top = planes * filters
    sizes = (channels, planes, height, length, filters, samples)
    whole = lambda shape: pl.BlockSpec(shape, lambda b: (0,) * len(shape))
    return pl.pallas_call(
        functools.partial(conv_kernel_body, sizes),
        grid=(samples,),
        in_specs=[
            pl.BlockSpec((1, channels, planes, height, length), lambda b: (b, 0, 0, 0, 0)),
            pl.BlockSpec((1, channels, 1, height, length), lambda b: (b, 0, 0, 0, 0)),
            pl.BlockSpec((1, channels, 1, height, length), lambda b: (b, 0, 0, 0, 0)),
            whole(bands.shape),
            whole(weight.shape),
            whole(cot_group.shape),
        ],
        out_specs=[whole((samples, filters * PC)), whole((peers, 128))],
        out_shape=[
            jax.ShapeDtypeStruct((samples, filters * PC), BF16),
            jax.ShapeDtypeStruct((peers, 128), BF16),
        ],
        scratch_shapes=[
            pltpu.VMEM((filters * PC, 128), F32),
            pltpu.VMEM(((height + 2) * rows, length), F32),
            pltpu.VMEM((top + rows, height * length), BF16),
            pltpu.VMEM((filters * PC, samples), F32),
            pltpu.VMEM((top + rows + 8, 256), F32),
            pltpu.VMEM((top, top), F32),
        ],
        compiler_params=pltpu.CompilerParams(vmem_limit_bytes=48 * 1024 * 1024),
    )(volume, before, after, bands, weight, cot_group)


def exact_dot(a, b):
    return jnp.dot(a, b, precision=HIGHEST, preferred_element_type=F32)


def unit(order):
    row = lax.broadcasted_iota(jnp.int32, (order, order), 0)
    column = lax.broadcasted_iota(jnp.int32, (order, order), 1)
    return row == column


def scalar_sum(x):
    return jnp.sum(jnp.sum(x, axis=0, keepdims=True), axis=1, keepdims=True)


def residual(factor, order):
    size = factor.shape[0]
    eye = unit(size)
    trace = scalar_sum(jnp.where(eye, factor, 0.0))
    damping = DAMPING * trace / order
    sums = jnp.sum(jnp.abs(factor), axis=0, keepdims=True) + damping
    bound = jnp.max(sums, axis=1, keepdims=True)
    inside = lax.broadcasted_iota(jnp.int32, (size, size), 0) < order
    start = jnp.where(jnp.logical_and(eye, inside), 1.0 - damping / bound, 0.0)
    return start - factor / bound, bound


def dense_kernel_body(slab_count, place_ref, feat_ref, cot_ref, delta_ref, total_ref, whole):
    groups, spaces, local, width = feat_ref.shape
    count = groups * local
    for slab in range(0, spaces, 2):
        pair = [
            feat_ref[:, slab + i].astype(F32).reshape(count, width) for i in range(2)
        ]
        whole[:, slab * width:(slab + 2) * width] = jnp.concatenate(pair, axis=1).astype(BF16)
    cot = cot_ref[...]
    feats = whole[...]
    scale = 1.0 / count
    gram = lax.dot_general(feats, feats, CONTRACT, preferred_element_type=F32) * scale
    dense_in = lax.dot_general(feats, feats, LEADING, preferred_element_type=F32) * scale
    dense_out = lax.dot_general(cot, cot, LEADING, preferred_element_type=F32) * scale
    order = spaces * width
    eye = unit(count)
    damping = DAMPING * scalar_sum(jnp.where(eye, gram, 0.0)) / order
    sums = jnp.sum(jnp.abs(dense_in), axis=0, keepdims=True) + damping
    bound = jnp.max(sums, axis=1, keepdims=True)
    left = jnp.where(eye, 1.0 - damping / bound, 0.0) - gram / bound
    right, bound_out = residual(dense_out, dense_out.shape[0])
    cot_wide = cot.astype(F32)
    held = cot_wide * (scale / bound / bound_out)
    for newton_step in range(NS_STEPS):
        held = held + exact_dot(left, held)
        held = held + exact_dot(held, right)
        if newton_step < NS_STEPS - 1:
            left = exact_dot(left, left)
            right = exact_dot(right, right)
    total_ref[...] = scalar_sum(held * exact_dot(gram, cot_wide))
    mine = feat_ref[:, place_ref[0]].astype(F32).reshape(count, width)
    source = lax.broadcasted_iota(jnp.int32, (width, width), 0)
    target = lax.broadcasted_iota(jnp.int32, (width, width), 1)
    spot = (target % PC) * (width // PC) + target // PC
    pick = jnp.where(source == spot, 1.0, 0.0).astype(BF16)
    mine = jnp.dot(mine.astype(BF16), pick, preferred_element_type=F32)
    delta_ref[...] = lax.dot_general(
        mine, held, LEADING, precision=HIGHEST, preferred_element_type=F32
    )


def dense_delta(place, feats, cot):
    groups, spaces, local, width = feats.shape
    count = groups * local
    outputs = cot.shape[1]
    vmem = pl.BlockSpec(memory_space=pltpu.VMEM)
    return pl.pallas_call(
        functools.partial(dense_kernel_body, spaces),
        in_specs=[pl.BlockSpec(memory_space=pltpu.SMEM), vmem, vmem],
        out_specs=[vmem, vmem],
        out_shape=[
            jax.ShapeDtypeStruct((width, outputs), F32),
            jax.ShapeDtypeStruct((1, 1), F32),
        ],
        scratch_shapes=[pltpu.VMEM((count, spaces * width), BF16)],
        compiler_params=pltpu.CompilerParams(vmem_limit_bytes=48 * 1024 * 1024),
    )(place, feats, cot)


def final_kernel_body(
    filters, patch_rows, cells, moments_ref, dense_ref, total_ref, order_ref,
    step_conv_ref, step_dense_ref,
):
    scale = 1.0 / cells
    pad = jnp.zeros((128 - ROWS_IN, 64), F32)
    lower = jnp.concatenate([moments_ref[64:ROWS_IN, :], pad], axis=0)
    corner = jnp.concatenate([moments_ref[ROWS_IN:2 * ROWS_IN - 64, :], pad], axis=0)
    upper = jnp.concatenate([moments_ref[0:64, :], jnp.transpose(lower)], axis=1)
    lower = jnp.concatenate([lower, corner], axis=1)
    conv_in = jnp.concatenate([upper, lower], axis=0) * scale
    first = 2 * ROWS_IN - 64
    conv_grad = jnp.concatenate(
        [moments_ref[first:first + filters, :], moments_ref[first + filters:first + 2 * filters, :]],
        axis=1,
    ) * scale
    conv_out = moments_ref[first + 2 * filters:first + 3 * filters, 0:filters] * scale
    right, bound_in = residual(conv_in, patch_rows)
    left, bound_out = residual(conv_out, filters)
    held = conv_grad / bound_in / bound_out
    for newton_step in range(NS_STEPS):
        held = held + exact_dot(left, held)
        held = held + exact_dot(held, right)
        if newton_step < NS_STEPS - 1:
            left = exact_dot(left, left)
            right = exact_dot(right, right)
    total = scalar_sum(held * conv_grad) + total_ref[...]
    scaling = jnp.minimum(1.0, jnp.sqrt(KL_BOUND / (LEARN_RATE * LEARN_RATE * total)))
    moved = exact_dot(held, order_ref[...])
    step_conv_ref[...] = scaling * moved[:, 0:patch_rows]
    step_dense_ref[...] = scaling * dense_ref[...]


def final_steps(moments, dense_block, dense_total, order, filters, patch_rows, cells):
    vmem = pl.BlockSpec(memory_space=pltpu.VMEM)
    return pl.pallas_call(
        functools.partial(final_kernel_body, filters, patch_rows, cells),
        in_specs=[vmem] * 4,
        out_specs=[vmem] * 2,
        out_shape=[
            jax.ShapeDtypeStruct((filters, patch_rows), F32),
            jax.ShapeDtypeStruct(dense_block.shape, F32),
        ],
        compiler_params=pltpu.CompilerParams(vmem_limit_bytes=32 * 1024 * 1024),
    )(moments, dense_block, dense_total, order)


def column_order(channels):
    row = lax.broadcasted_iota(jnp.int32, (128, 128), 0)
    column = lax.broadcasted_iota(jnp.int32, (128, 128), 1)
    channel, rest = column // 27, column % 27
    source = (rest // 9) * (9 * channels) + channel * 9 + rest % 9
    return jnp.where(jnp.logical_and(row == source, column < 27 * channels), 1.0, 0.0)


def on_device(volume, conv_kernel, dense_weight, cotangent):
    spaces = lax.axis_size("space")
    groups = lax.axis_size("dp")
    peers = spaces * groups
    samples, channels, planes, height, length = volume.shape
    filters, patch_rows = conv_kernel.shape
    slab = filters * PC

    up = [(i, i + 1) for i in range(spaces - 1)]
    down = [(j, i) for i, j in up]
    before = lax.ppermute(volume[:, :, planes - 1:], "space", up)
    after = lax.ppermute(volume[:, :, :1], "space", down)
    cot_group = gather_from(cotangent[0], "space", spaces)

    mixed = conv_kernel.reshape(filters, channels, 3, 9).transpose(0, 2, 1, 3)
    mixed = mixed.reshape(filters, patch_rows)
    spare = (planes + 2) * channels * 9 - patch_rows
    bands = jnp.concatenate(
        [
            jnp.pad(mixed, ((0, 0), (p * channels * 9, spare - p * channels * 9)))
            for p in range(planes)
        ],
        axis=0,
    )
    place = lax.axis_index("space")
    weight = lax.dynamic_slice_in_dim(dense_weight, place * slab, slab, 0)
    weight = weight.reshape(filters, PC, -1).transpose(1, 0, 2).reshape(slab, -1)

    pooled, moments = conv_moments(
        volume, before, after, bands, weight, cot_group, filters, peers
    )
    own = jnp.concatenate([pooled.reshape(1, samples * slab), cotangent], axis=1)
    sent = jnp.concatenate([jnp.broadcast_to(own, (peers, own.shape[1])), moments], axis=1)
    got = exchange(sent, BOTH)
    feats = got[:, :samples * slab].reshape(groups, spaces, samples, slab)
    cot_all = got[:, samples * slab:own.shape[1]]
    parts = got[:, own.shape[1]:].astype(F32)
    mine = jnp.sum(parts[:, :64] + parts[:, 64:], axis=0)
    reduced = gather_from(mine, BOTH, peers)

    delta, dense_total = dense_delta(place.reshape(1), feats, cot_all)
    share = cotangent.shape[1] // groups
    dense_block = lax.dynamic_slice_in_dim(delta, lax.axis_index("dp") * share, share, 1)
    cells = samples * groups * planes * spaces * height * length
    return final_steps(
        reduced, dense_block, dense_total, column_order(channels), filters, patch_rows, cells
    )


def solution(mesh):
    placed = (P("dp", None, "space", None, None), P(), P(), P(BOTH, None))
    return jax.shard_map(
        on_device, mesh=mesh, in_specs=placed, out_specs=(P(), P("space", "dp")), check_vma=False
    )
```

```python
import functools

import jax
import jax.numpy as jnp
from jax import lax
from jax.experimental import pallas as pl
from jax.experimental.pallas import tpu as pltpu
from jax.sharding import PartitionSpec as P

PC = 2
NS_STEPS = 8

LEAK_SLOPE = 0.3
DAMPING = 0.1
KL_BOUND = 0.0001
LEARN_RATE = 0.01
HIGHEST = lax.Precision.HIGHEST
CONTRACT = (((1,), (1,)), ((), ()))
LEADING = (((0,), (0,)), ((), ()))
BOTH = ("dp", "space")
F32 = jnp.float32
BF16 = jnp.bfloat16
ROWS_IN = 112


def exchange(x, axes):
    return lax.all_to_all(x, axes, split_axis=0, concat_axis=0, tiled=True)


def gather_from(x, axes, peers):
    return exchange(jnp.broadcast_to(x[None], (peers,) + x.shape), axes)


def conv_kernel_body(
    sizes, vol_ref, before_ref, after_ref, bands_ref, weight_ref, cot_ref, own_ref,
    sent_ref, pool_ref, shifted, stacked, grads, acc, acc_out,
):
    channels, planes, height, length, filters, samples = sizes
    rim = planes + 2
    per_plane = channels * 9
    rows = rim * per_plane
    cells = height * length
    half = cells // PC
    top = planes * filters
    step = pl.program_id(0)

    @pl.when(step == 0)
    def _():
        shifted[...] = jnp.zeros_like(shifted)
        acc[...] = jnp.zeros_like(acc)
        acc_out[...] = jnp.zeros_like(acc_out)
        pool_ref[...] = jnp.zeros_like(pool_ref)
        grads[...] = lax.dot_general(
            weight_ref[...], cot_ref[...], CONTRACT, preferred_element_type=F32
        ).astype(BF16).astype(F32)

    lane = lax.broadcasted_iota(jnp.int32, (height, length), 1)
    for plane in range(rim):
        for channel in range(channels):
            if plane == 0:
                value = before_ref[0, channel, 0]
            elif plane == rim - 1:
                value = after_ref[0, channel, 0]
            else:
                value = vol_ref[0, channel, plane - 1]
            value = value.astype(F32)
            moved = (
                jnp.where(lane == 0, 0.0, pltpu.roll(value, 1, 1)),
                value,
                jnp.where(lane == length - 1, 0.0, pltpu.roll(value, length - 1, 1)),
            )
            for j in range(3):
                for k in range(3):
                    row = plane * per_plane + channel * 9 + j * 3 + k
                    shifted[pl.ds((2 - j) * rows + row, height, stride=rows), :] = moved[k]
    for y in range(height):
        stacked[top:, y * length:(y + 1) * length] = shifted[
            (y + 1) * rows:(y + 2) * rows, :
        ].astype(BF16)

    column = lax.broadcasted_iota(jnp.int32, (filters * PC, samples), 1)
    grad_all = jnp.sum(jnp.where(column == step, grads[...], 0.0), axis=1, keepdims=True)
    low_all = (LEAK_SLOPE * grad_all).astype(BF16).astype(F32)
    pooled = []
    for part in range(PC):
        lanes = slice(part * half, (part + 1) * half)
        pre = jnp.dot(bands_ref[...], stacked[top:, lanes], preferred_element_type=F32)
        active = jnp.where(pre > 0, pre, LEAK_SLOPE * pre)
        total = active[0:filters]
        for plane in range(1, planes):
            total = total + active[plane * filters:(plane + 1) * filters]
        pooled.append(jnp.sum(total, axis=1, keepdims=True))
        grad = jnp.concatenate([grad_all[part * filters:(part + 1) * filters]] * planes, axis=0)
        low = jnp.concatenate([low_all[part * filters:(part + 1) * filters]] * planes, axis=0)
        stacked[0:top, lanes] = jnp.where(pre > 0, grad, low).astype(BF16)
    pooled = jnp.concatenate(pooled, axis=0) * (1.0 / (planes * half))
    spot = lax.broadcasted_iota(jnp.int32, pool_ref.shape, 1)
    pool_ref[...] = jnp.where(spot == step, pooled, pool_ref[...])
    acc[0:top + rows, :rows] += lax.dot_general(
        stacked[...], stacked[top:, :], CONTRACT, preferred_element_type=F32
    )
    acc_out[...] += lax.dot_general(
        stacked[0:top, :], stacked[0:top, :], CONTRACT, preferred_element_type=F32
    )

    @pl.when(step == pl.num_programs(0) - 1)
    def _():
        width = acc.shape[1]
        wide = 3 * per_plane
        moment_in = jnp.zeros((ROWS_IN, 128), F32)
        gradient = jnp.zeros((filters, 128), F32)
        moment_out = jnp.zeros((filters, 128), F32)
        for plane in range(planes):
            start = plane * per_plane
            turn = (width - start) % width
            block = acc[top + start:top + start + ROWS_IN, :]
            moment_in += (pltpu.roll(block, turn, 1) if turn else block)[:, :128]
            block = acc[plane * filters:(plane + 1) * filters, :]
            gradient += (pltpu.roll(block, turn, 1) if turn else block)[:, :128]
            block = acc_out[plane * filters:(plane + 1) * filters, :]
            turn = (top - plane * filters) % top
            moment_out += pltpu.roll(block, turn, 1) if turn else block
        row_in = lax.broadcasted_iota(jnp.int32, (ROWS_IN, 128), 0)
        lane_in = lax.broadcasted_iota(jnp.int32, (ROWS_IN, 128), 1)
        moment_in = jnp.where(jnp.maximum(row_in, lane_in) < wide, moment_in, 0.0)
        lane_out = lax.broadcasted_iota(jnp.int32, (filters, 128), 1)
        gradient = jnp.where(lane_out < wide, gradient, 0.0)
        packed = jnp.concatenate(
            [
                moment_in[:, :64],
                moment_in[64:, 64:],
                gradient[:, :64],
                gradient[:, 64:],
                moment_out[:, :64],
            ],
            axis=0,
        )
        groups = sent_ref.shape[0]
        sent_ref[:, 0:8, :] = in_halves(packed).reshape(groups, 8, 128)
        feats = jnp.transpose(pool_ref[...])[:samples]
        own = own_ref[...].astype(F32)
        own = jnp.concatenate([own[:, :64], own[:, 64:], jnp.zeros((samples - 2, 64), F32)], axis=0)
        both = jnp.concatenate([feats, own], axis=1).astype(BF16)
        sent_ref[:, 8:16, :] = jnp.broadcast_to(both[None], (groups, samples, 128))


def in_halves(x):
    high = x.astype(BF16)
    low = (x - high.astype(F32)).astype(BF16)
    return jnp.concatenate([high, low], axis=1)


def from_halves(x):
    wide = x.astype(F32)
    return wide[..., :64] + wide[..., 64:]


def conv_moments(volume, before, after, bands, weight, cot_group, own, filters, groups):
    samples, channels, planes, height, length = volume.shape
    per_plane = channels * 9
    rows = (planes + 2) * per_plane
    top = planes * filters
    sizes = (channels, planes, height, length, filters, samples)
    whole = lambda shape: pl.BlockSpec(shape, lambda b: (0,) * len(shape))
    return pl.pallas_call(
        functools.partial(conv_kernel_body, sizes),
        grid=(samples,),
        in_specs=[
            pl.BlockSpec((1, channels, planes, height, length), lambda b: (b, 0, 0, 0, 0)),
            pl.BlockSpec((1, channels, 1, height, length), lambda b: (b, 0, 0, 0, 0)),
            pl.BlockSpec((1, channels, 1, height, length), lambda b: (b, 0, 0, 0, 0)),
            whole(bands.shape),
            whole(weight.shape),
            whole(cot_group.shape),
            whole(own.shape),
        ],
        out_specs=whole((groups, 16, 128)),
        out_shape=jax.ShapeDtypeStruct((groups, 16, 128), BF16),
        scratch_shapes=[
            pltpu.VMEM((filters * PC, 128), F32),
            pltpu.VMEM(((height + 2) * rows, length), F32),
            pltpu.VMEM((top + rows, height * length), BF16),
            pltpu.VMEM((filters * PC, samples), F32),
            pltpu.VMEM((top + rows + 8, 256), F32),
            pltpu.VMEM((top, top), F32),
        ],
        compiler_params=pltpu.CompilerParams(vmem_limit_bytes=48 * 1024 * 1024),
    )(volume, before, after, bands, weight, cot_group, own)


def middle_body(got_ref, sent_ref):
    groups = got_ref.shape[0]
    pairs = groups // 2
    rows = pairs * 8
    chunk = jnp.sum(from_halves(got_ref[:, 0:8, :]), axis=0)
    wide = got_ref[:, 8:16, :].astype(F32)
    feats = wide[:, :, :64]
    feats = jnp.concatenate([feats[:pairs], feats[pairs:]], axis=2).reshape(rows, 128)
    cots = jnp.concatenate([wide[:, 0, 64:], wide[:, 1, 64:]], axis=1)
    feats = feats.astype(BF16)
    cots = cots.astype(BF16)
    chunk = in_halves(chunk)
    for peer in range(sent_ref.shape[0]):
        sent_ref[peer, 0:rows, :] = feats
        sent_ref[peer, rows:rows + groups, :] = cots
        sent_ref[peer, rows + groups:, :] = chunk


def middle(got, spaces):
    groups = got.shape[0]
    vmem = pl.BlockSpec(memory_space=pltpu.VMEM)
    return pl.pallas_call(
        middle_body,
        in_specs=[vmem],
        out_specs=vmem,
        out_shape=jax.ShapeDtypeStruct((spaces, groups * 5 + 8, 128), BF16),
        compiler_params=pltpu.CompilerParams(vmem_limit_bytes=8 * 1024 * 1024),
    )(got)


def spread_body(got_ref, sent_ref):
    chunk = jnp.sum(from_halves(got_ref[...]), axis=0)
    sent_ref[...] = jnp.broadcast_to(in_halves(chunk)[None], sent_ref.shape)


def spread(got, groups):
    spaces, rows, lanes = got.shape
    return pl.pallas_call(
        spread_body,
        grid=(1,),
        in_specs=[pl.BlockSpec((spaces, 8, lanes), lambda i: (0, rows // 8 - 1, 0))],
        out_specs=pl.BlockSpec((groups, 8, lanes), lambda i: (0, 0, 0)),
        out_shape=jax.ShapeDtypeStruct((groups, 8, lanes), BF16),
        compiler_params=pltpu.CompilerParams(vmem_limit_bytes=8 * 1024 * 1024),
    )(got)


def exact_dot(a, b):
    return jnp.dot(a, b, precision=HIGHEST, preferred_element_type=F32)


def unit(order):
    row = lax.broadcasted_iota(jnp.int32, (order, order), 0)
    column = lax.broadcasted_iota(jnp.int32, (order, order), 1)
    return row == column


def scalar_sum(x):
    return jnp.sum(jnp.sum(x, axis=0, keepdims=True), axis=1, keepdims=True)


def residual(factor, order):
    size = factor.shape[0]
    eye = unit(size)
    trace = scalar_sum(jnp.where(eye, factor, 0.0))
    damping = DAMPING * trace / order
    sums = jnp.sum(jnp.abs(factor), axis=0, keepdims=True) + damping
    bound = jnp.max(sums, axis=1, keepdims=True)
    inside = lax.broadcasted_iota(jnp.int32, (size, size), 0) < order
    start = jnp.where(jnp.logical_and(eye, inside), 1.0 - damping / bound, 0.0)
    return start - factor / bound, bound


def dense_kernel_body(groups, place_ref, got_ref, delta_ref, total_ref, whole, cots):
    spaces = got_ref.shape[0]
    width = 64
    count = groups * 8
    half = count // 2

    def slab_of(index):
        both = got_ref[index].astype(F32)[:half]
        return jnp.concatenate([both[:, :width], both[:, width:]], axis=0)

    for slab in range(0, spaces, 2):
        pair = jnp.concatenate([slab_of(slab), slab_of(slab + 1)], axis=1)
        whole[:, slab * width:(slab + 2) * width] = pair.astype(BF16)
    for slab in range(spaces):
        cots[pl.ds(slab, groups, stride=spaces), :] = got_ref[
            slab, half:half + groups, :
        ].astype(F32)
    cot_wide = cots[...]
    cot = cot_wide.astype(BF16)
    feats = whole[...]
    scale = 1.0 / count
    gram = lax.dot_general(feats, feats, CONTRACT, preferred_element_type=F32) * scale
    dense_in = lax.dot_general(feats, feats, LEADING, preferred_element_type=F32) * scale
    dense_out = lax.dot_general(cot, cot, LEADING, preferred_element_type=F32) * scale
    order = spaces * width
    eye = unit(count)
    damping = DAMPING * scalar_sum(jnp.where(eye, gram, 0.0)) / order
    sums = jnp.sum(jnp.abs(dense_in), axis=0, keepdims=True) + damping
    bound = jnp.max(sums, axis=1, keepdims=True)
    left = jnp.where(eye, 1.0 - damping / bound, 0.0) - gram / bound
    right, bound_out = residual(dense_out, dense_out.shape[0])
    held = cot_wide * (scale / bound / bound_out)
    for newton_step in range(NS_STEPS):
        held = held + exact_dot(left, held)
        held = held + exact_dot(held, right)
        if newton_step < NS_STEPS - 1:
            left = exact_dot(left, left)
            right = exact_dot(right, right)
    total_ref[...] = scalar_sum(held * exact_dot(gram, cot_wide))
    mine = slab_of(place_ref[0])
    source = lax.broadcasted_iota(jnp.int32, (width, width), 0)
    target = lax.broadcasted_iota(jnp.int32, (width, width), 1)
    spot = (target % PC) * (width // PC) + target // PC
    pick = jnp.where(source == spot, 1.0, 0.0).astype(BF16)
    mine = jnp.dot(mine.astype(BF16), pick, preferred_element_type=F32)
    delta_ref[...] = lax.dot_general(
        held, mine, LEADING, precision=HIGHEST, preferred_element_type=F32
    )


def dense_delta(place, got, groups, outputs):
    spaces = got.shape[0]
    vmem = pl.BlockSpec(memory_space=pltpu.VMEM)
    return pl.pallas_call(
        functools.partial(dense_kernel_body, groups),
        in_specs=[pl.BlockSpec(memory_space=pltpu.SMEM), vmem],
        out_specs=[vmem, vmem],
        out_shape=[
            jax.ShapeDtypeStruct((outputs, 64), F32),
            jax.ShapeDtypeStruct((1, 1), F32),
        ],
        scratch_shapes=[
            pltpu.VMEM((groups * 8, spaces * 64), BF16),
            pltpu.VMEM((groups * 8, outputs), F32),
        ],
        compiler_params=pltpu.CompilerParams(vmem_limit_bytes=48 * 1024 * 1024),
    )(place, got)


def final_kernel_body(
    filters, patch_rows, cells, got_ref, dense_ref, total_ref, order_ref,
    step_conv_ref, step_dense_ref,
):
    scale = 1.0 / cells
    moments = from_halves(got_ref[...]).reshape(-1, 64)
    pad = jnp.zeros((128 - ROWS_IN, 64), F32)
    lower = jnp.concatenate([moments[64:ROWS_IN], pad], axis=0)
    corner = jnp.concatenate([moments[ROWS_IN:2 * ROWS_IN - 64], pad], axis=0)
    upper = jnp.concatenate([moments[0:64], jnp.transpose(lower)], axis=1)
    lower = jnp.concatenate([lower, corner], axis=1)
    conv_in = jnp.concatenate([upper, lower], axis=0) * scale
    first = 2 * ROWS_IN - 64
    conv_grad = jnp.concatenate(
        [moments[first:first + filters], moments[first + filters:first + 2 * filters]],
        axis=1,
    ) * scale
    conv_out = moments[first + 2 * filters:first + 3 * filters, 0:filters] * scale
    right, bound_in = residual(conv_in, patch_rows)
    left, bound_out = residual(conv_out, filters)
    held = conv_grad / bound_in / bound_out
    inverse = jnp.where(unit(128), 1.0, 0.0) + right
    for newton_step in range(NS_STEPS):
        held = held + exact_dot(left, held)
        if newton_step < NS_STEPS - 1:
            left = exact_dot(left, left)
            right = exact_dot(right, right)
            inverse = inverse + exact_dot(inverse, right)
    held = exact_dot(held, inverse)
    total = scalar_sum(held * conv_grad) + total_ref[...]
    scaling = jnp.minimum(1.0, jnp.sqrt(KL_BOUND / (LEARN_RATE * LEARN_RATE * total)))
    moved = exact_dot(held, order_ref[...])
    step_conv_ref[...] = scaling * moved[:, 0:patch_rows]
    step_dense_ref[...] = scaling * dense_ref[...]


def final_steps(moments, dense_block, dense_total, order, filters, patch_rows, cells):
    vmem = pl.BlockSpec(memory_space=pltpu.VMEM)
    return pl.pallas_call(
        functools.partial(final_kernel_body, filters, patch_rows, cells),
        in_specs=[vmem] * 4,
        out_specs=[vmem] * 2,
        out_shape=[
            jax.ShapeDtypeStruct((filters, patch_rows), F32),
            jax.ShapeDtypeStruct(dense_block.shape, F32),
        ],
        compiler_params=pltpu.CompilerParams(vmem_limit_bytes=32 * 1024 * 1024),
    )(moments, dense_block, dense_total, order)


def column_order(channels):
    row = lax.broadcasted_iota(jnp.int32, (128, 128), 0)
    column = lax.broadcasted_iota(jnp.int32, (128, 128), 1)
    channel, rest = column // 27, column % 27
    source = (rest // 9) * (9 * channels) + channel * 9 + rest % 9
    return jnp.where(jnp.logical_and(row == source, column < 27 * channels), 1.0, 0.0)


def on_device(volume, conv_kernel, dense_weight, cotangent):
    spaces = lax.axis_size("space")
    groups = lax.axis_size("dp")
    samples, channels, planes, height, length = volume.shape
    filters, patch_rows = conv_kernel.shape
    slab = filters * PC

    up = [(i, i + 1) for i in range(spaces - 1)]
    down = [(j, i) for i, j in up]
    before = lax.ppermute(volume[:, :, planes - 1:], "space", up)
    after = lax.ppermute(volume[:, :, :1], "space", down)
    cot_group = gather_from(cotangent[0], "space", spaces)

    mixed = conv_kernel.reshape(filters, channels, 3, 9).transpose(0, 2, 1, 3)
    mixed = mixed.reshape(filters, patch_rows)
    spare = (planes + 2) * channels * 9 - patch_rows
    bands = jnp.concatenate(
        [
            jnp.pad(mixed, ((0, 0), (p * channels * 9, spare - p * channels * 9)))
            for p in range(planes)
        ],
        axis=0,
    )
    place = lax.axis_index("space")
    weight = lax.dynamic_slice_in_dim(dense_weight, place * slab, slab, 0)
    weight = weight.reshape(filters, PC, -1).transpose(1, 0, 2).reshape(slab, -1)

    sent = conv_moments(
        volume, before, after, bands, weight, cot_group, cotangent, filters, groups
    )
    got = exchange(middle(exchange(sent, "dp"), spaces), "space")
    reduced = exchange(spread(got, groups), "dp")
    delta, dense_total = dense_delta(place.reshape(1), got, groups, cotangent.shape[1])
    share = cotangent.shape[1] // groups
    dense_block = lax.dynamic_slice_in_dim(delta, lax.axis_index("dp") * share, share, 0)
    cells = samples * groups * planes * spaces * height * length
    step_conv, step_dense = final_steps(
        reduced, dense_block, dense_total, column_order(channels), filters, patch_rows, cells
    )
    return step_conv, step_dense.T


def solution(mesh):
    placed = (P("dp", None, "space", None, None), P(), P(), P(BOTH, None))
    return jax.shard_map(
        on_device, mesh=mesh, in_specs=placed, out_specs=(P(), P("space", "dp")), check_vma=False
    )
```

```python
import functools

import jax
import jax.numpy as jnp
from jax import lax
from jax.experimental import pallas as pl
from jax.experimental.pallas import tpu as pltpu
from jax.sharding import PartitionSpec as P

PC = 2
NS_STEPS = 8

LEAK_SLOPE = 0.3
DAMPING = 0.1
KL_BOUND = 0.0001
LEARN_RATE = 0.01
HIGHEST = lax.Precision.HIGHEST
CONTRACT = (((1,), (1,)), ((), ()))
LEADING = (((0,), (0,)), ((), ()))
DP = ("z", "xh", "core")
SPACE = ("xl", "y")
COLUMN = ("z", "core")
PLANE = ("xh", "xl", "y")
F32 = jnp.float32
BF16 = jnp.bfloat16
ROWS_IN = 112


def exchange(x, axes):
    return lax.all_to_all(x, axes, split_axis=0, concat_axis=0, tiled=True)


def gather_from(x, axes, peers):
    return exchange(jnp.broadcast_to(x[None], (peers,) + x.shape), axes)


def conv_kernel_body(
    sizes, vol_ref, before_ref, after_ref, bands_ref, weight_ref, cot_ref, own_ref,
    sent_ref, pool_ref, shifted, stacked, grads, acc, acc_out,
):
    channels, planes, height, length, filters, samples = sizes
    rim = planes + 2
    per_plane = channels * 9
    rows = rim * per_plane
    cells = height * length
    half = cells // PC
    top = planes * filters
    step = pl.program_id(0)

    @pl.when(step == 0)
    def _():
        shifted[...] = jnp.zeros_like(shifted)
        acc[...] = jnp.zeros_like(acc)
        acc_out[...] = jnp.zeros_like(acc_out)
        pool_ref[...] = jnp.zeros_like(pool_ref)
        grads[...] = lax.dot_general(
            weight_ref[...], cot_ref[...], CONTRACT, preferred_element_type=F32
        ).astype(BF16).astype(F32)

    lane = lax.broadcasted_iota(jnp.int32, (height, length), 1)
    for plane in range(rim):
        for channel in range(channels):
            if plane == 0:
                value = before_ref[0, channel, 0]
            elif plane == rim - 1:
                value = after_ref[0, channel, 0]
            else:
                value = vol_ref[0, channel, plane - 1]
            value = value.astype(F32)
            moved = (
                jnp.where(lane == 0, 0.0, pltpu.roll(value, 1, 1)),
                value,
                jnp.where(lane == length - 1, 0.0, pltpu.roll(value, length - 1, 1)),
            )
            for j in range(3):
                for k in range(3):
                    row = plane * per_plane + channel * 9 + j * 3 + k
                    shifted[pl.ds((2 - j) * rows + row, height, stride=rows), :] = moved[k]
    for y in range(height):
        stacked[top:, y * length:(y + 1) * length] = shifted[
            (y + 1) * rows:(y + 2) * rows, :
        ].astype(BF16)

    column = lax.broadcasted_iota(jnp.int32, (filters * PC, samples), 1)
    grad_all = jnp.sum(jnp.where(column == step, grads[...], 0.0), axis=1, keepdims=True)
    low_all = (LEAK_SLOPE * grad_all).astype(BF16).astype(F32)
    pooled = []
    for part in range(PC):
        lanes = slice(part * half, (part + 1) * half)
        pre = jnp.dot(bands_ref[...], stacked[top:, lanes], preferred_element_type=F32)
        active = jnp.where(pre > 0, pre, LEAK_SLOPE * pre)
        total = active[0:filters]
        for plane in range(1, planes):
            total = total + active[plane * filters:(plane + 1) * filters]
        pooled.append(jnp.sum(total, axis=1, keepdims=True))
        grad = jnp.concatenate([grad_all[part * filters:(part + 1) * filters]] * planes, axis=0)
        low = jnp.concatenate([low_all[part * filters:(part + 1) * filters]] * planes, axis=0)
        stacked[0:top, lanes] = jnp.where(pre > 0, grad, low).astype(BF16)
    pooled = jnp.concatenate(pooled, axis=0) * (1.0 / (planes * half))
    spot = lax.broadcasted_iota(jnp.int32, pool_ref.shape, 1)
    pool_ref[...] = jnp.where(spot == step, pooled, pool_ref[...])
    acc[0:top + rows, :rows] += lax.dot_general(
        stacked[...], stacked[top:, :], CONTRACT, preferred_element_type=F32
    )
    acc_out[...] += lax.dot_general(
        stacked[0:top, :], stacked[0:top, :], CONTRACT, preferred_element_type=F32
    )

    @pl.when(step == pl.num_programs(0) - 1)
    def _():
        width = acc.shape[1]
        wide = 3 * per_plane
        moment_in = jnp.zeros((ROWS_IN, 128), F32)
        gradient = jnp.zeros((filters, 128), F32)
        moment_out = jnp.zeros((filters, 128), F32)
        for plane in range(planes):
            start = plane * per_plane
            turn = (width - start) % width
            block = acc[top + start:top + start + ROWS_IN, :]
            moment_in += (pltpu.roll(block, turn, 1) if turn else block)[:, :128]
            block = acc[plane * filters:(plane + 1) * filters, :]
            gradient += (pltpu.roll(block, turn, 1) if turn else block)[:, :128]
            block = acc_out[plane * filters:(plane + 1) * filters, :]
            turn = (top - plane * filters) % top
            moment_out += pltpu.roll(block, turn, 1) if turn else block
        row_in = lax.broadcasted_iota(jnp.int32, (ROWS_IN, 128), 0)
        lane_in = lax.broadcasted_iota(jnp.int32, (ROWS_IN, 128), 1)
        moment_in = jnp.where(jnp.maximum(row_in, lane_in) < wide, moment_in, 0.0)
        lane_out = lax.broadcasted_iota(jnp.int32, (filters, 128), 1)
        gradient = jnp.where(lane_out < wide, gradient, 0.0)
        packed = jnp.concatenate(
            [
                moment_in[:, :64],
                moment_in[64:, 64:],
                gradient[:, :64],
                gradient[:, 64:],
                moment_out[:, :64],
            ],
            axis=0,
        )
        groups = sent_ref.shape[0]
        share = packed.shape[0] // groups
        sent_ref[:, 0:share, :] = in_halves(packed).reshape(groups, share, 128)
        feats = jnp.transpose(pool_ref[...])[:samples]
        own = own_ref[...].astype(F32)
        own = jnp.concatenate([own[:, :64], own[:, 64:], jnp.zeros((samples - 2, 64), F32)], axis=0)
        both = jnp.concatenate([feats, own], axis=1).astype(BF16)
        sent_ref[:, share:, :] = jnp.broadcast_to(both[None], (groups, samples, 128))


def in_halves(x):
    high = x.astype(BF16)
    low = (x - high.astype(F32)).astype(BF16)
    return jnp.concatenate([high, low], axis=1)


def from_halves(x):
    wide = x.astype(F32)
    return wide[..., :64] + wide[..., 64:]


def conv_moments(volume, before, after, bands, weight, cot_group, own, filters, groups):
    samples, channels, planes, height, length = volume.shape
    per_plane = channels * 9
    rows = (planes + 2) * per_plane
    top = planes * filters
    sizes = (channels, planes, height, length, filters, samples)
    whole = lambda shape: pl.BlockSpec(shape, lambda b: (0,) * len(shape))
    return pl.pallas_call(
        functools.partial(conv_kernel_body, sizes),
        grid=(samples,),
        in_specs=[
            pl.BlockSpec((1, channels, planes, height, length), lambda b: (b, 0, 0, 0, 0)),
            pl.BlockSpec((1, channels, 1, height, length), lambda b: (b, 0, 0, 0, 0)),
            pl.BlockSpec((1, channels, 1, height, length), lambda b: (b, 0, 0, 0, 0)),
            whole(bands.shape),
            whole(weight.shape),
            whole(cot_group.shape),
            whole(own.shape),
        ],
        out_specs=whole((groups, 256 // groups + samples, 128)),
        out_shape=jax.ShapeDtypeStruct((groups, 256 // groups + samples, 128), BF16),
        scratch_shapes=[
            pltpu.VMEM((filters * PC, 128), F32),
            pltpu.VMEM(((height + 2) * rows, length), F32),
            pltpu.VMEM((top + rows, height * length), BF16),
            pltpu.VMEM((filters * PC, samples), F32),
            pltpu.VMEM((top + rows + 8, 256), F32),
            pltpu.VMEM((top, top), F32),
        ],
        compiler_params=pltpu.CompilerParams(vmem_limit_bytes=48 * 1024 * 1024),
    )(volume, before, after, bands, weight, cot_group, own)


def middle_body(got_ref, sent_ref):
    groups = got_ref.shape[0]
    pairs = groups // 2
    rows = pairs * 8
    share = got_ref.shape[1] - 8
    chunk = jnp.sum(from_halves(got_ref[:, 0:share, :]), axis=0)
    wide = got_ref[:, share:, :].astype(F32)
    feats = wide[:, :, :64]
    feats = jnp.concatenate([feats[:pairs], feats[pairs:]], axis=2).reshape(rows, 128)
    cots = jnp.concatenate([wide[:, 0, 64:], wide[:, 1, 64:]], axis=1)
    feats = feats.astype(BF16)
    cots = cots.astype(BF16)
    chunk = in_halves(chunk)
    for peer in range(sent_ref.shape[0]):
        sent_ref[peer, 0:rows, :] = feats
        sent_ref[peer, rows:rows + groups, :] = cots
        sent_ref[peer, rows + groups:, :] = chunk


def middle(got, peers):
    groups, rows, lanes = got.shape
    vmem = pl.BlockSpec(memory_space=pltpu.VMEM)
    return pl.pallas_call(
        middle_body,
        in_specs=[vmem],
        out_specs=vmem,
        out_shape=jax.ShapeDtypeStruct((peers, groups * 5 + rows - 8, lanes), BF16),
        compiler_params=pltpu.CompilerParams(vmem_limit_bytes=8 * 1024 * 1024),
    )(got)


def spread_body(got_ref, sent_ref):
    chunk = jnp.sum(from_halves(got_ref[...]), axis=0)
    sent_ref[...] = jnp.broadcast_to(in_halves(chunk)[None], sent_ref.shape)


def spread(got, groups):
    peers, rows, lanes = got.shape
    share = 256 // groups
    return pl.pallas_call(
        spread_body,
        grid=(1,),
        in_specs=[pl.BlockSpec((peers, share, lanes), lambda i: (0, rows // share - 1, 0))],
        out_specs=pl.BlockSpec((groups, share, lanes), lambda i: (0, 0, 0)),
        out_shape=jax.ShapeDtypeStruct((groups, share, lanes), BF16),
        compiler_params=pltpu.CompilerParams(vmem_limit_bytes=8 * 1024 * 1024),
    )(got)


def exact_dot(a, b):
    return jnp.dot(a, b, precision=HIGHEST, preferred_element_type=F32)


def unit(order):
    row = lax.broadcasted_iota(jnp.int32, (order, order), 0)
    column = lax.broadcasted_iota(jnp.int32, (order, order), 1)
    return row == column


def scalar_sum(x):
    return jnp.sum(jnp.sum(x, axis=0, keepdims=True), axis=1, keepdims=True)


def residual(factor, order):
    size = factor.shape[0]
    eye = unit(size)
    trace = scalar_sum(jnp.where(eye, factor, 0.0))
    damping = DAMPING * trace / order
    sums = jnp.sum(jnp.abs(factor), axis=0, keepdims=True) + damping
    bound = jnp.max(sums, axis=1, keepdims=True)
    inside = lax.broadcasted_iota(jnp.int32, (size, size), 0) < order
    start = jnp.where(jnp.logical_and(eye, inside), 1.0 - damping / bound, 0.0)
    return start - factor / bound, bound


def dense_kernel_body(groups, spaces, place_ref, got_ref, delta_ref, total_ref, whole, cots):
    parts = got_ref.shape[0] // spaces
    width = 64
    block = groups * 8
    count = parts * block
    half = block // 2

    def slab_of(index):
        pieces = []
        for part in range(parts):
            both = got_ref[part * spaces + index].astype(F32)[:half]
            pieces += [both[:, :width], both[:, width:]]
        return jnp.concatenate(pieces, axis=0)

    for slab in range(0, spaces, 2):
        pair = jnp.concatenate([slab_of(slab), slab_of(slab + 1)], axis=1)
        whole[:, slab * width:(slab + 2) * width] = pair.astype(BF16)
    for part in range(parts):
        for slab in range(spaces):
            cots[pl.ds(part * block + slab, groups, stride=spaces), :] = got_ref[
                part * spaces + slab, half:half + groups, :
            ].astype(F32)
    cot_wide = cots[...]
    cot = cot_wide.astype(BF16)
    feats = whole[...]
    scale = 1.0 / count
    gram = lax.dot_general(feats, feats, CONTRACT, preferred_element_type=F32) * scale
    dense_in = lax.dot_general(feats, feats, LEADING, preferred_element_type=F32) * scale
    dense_out = lax.dot_general(cot, cot, LEADING, preferred_element_type=F32) * scale
    order = spaces * width
    eye = unit(count)
    damping = DAMPING * scalar_sum(jnp.where(eye, gram, 0.0)) / order
    sums = jnp.sum(jnp.abs(dense_in), axis=0, keepdims=True) + damping
    bound = jnp.max(sums, axis=1, keepdims=True)
    left = jnp.where(eye, 1.0 - damping / bound, 0.0) - gram / bound
    right, bound_out = residual(dense_out, dense_out.shape[0])
    held = cot_wide * (scale / bound / bound_out)
    for newton_step in range(NS_STEPS):
        held = held + exact_dot(left, held)
        held = held + exact_dot(held, right)
        if newton_step < NS_STEPS - 1:
            left = exact_dot(left, left)
            right = exact_dot(right, right)
    total_ref[...] = scalar_sum(held * exact_dot(gram, cot_wide))
    mine = slab_of(place_ref[0])
    source = lax.broadcasted_iota(jnp.int32, (width, width), 0)
    target = lax.broadcasted_iota(jnp.int32, (width, width), 1)
    spot = (target % PC) * (width // PC) + target // PC
    pick = jnp.where(source == spot, 1.0, 0.0).astype(BF16)
    mine = jnp.dot(mine.astype(BF16), pick, preferred_element_type=F32)
    delta_ref[...] = lax.dot_general(
        held, mine, LEADING, precision=HIGHEST, preferred_element_type=F32
    )


def dense_delta(place, got, groups, spaces, outputs):
    count = groups * 8 * (got.shape[0] // spaces)
    vmem = pl.BlockSpec(memory_space=pltpu.VMEM)
    return pl.pallas_call(
        functools.partial(dense_kernel_body, groups, spaces),
        in_specs=[pl.BlockSpec(memory_space=pltpu.SMEM), vmem],
        out_specs=[vmem, vmem],
        out_shape=[
            jax.ShapeDtypeStruct((outputs, 64), F32),
            jax.ShapeDtypeStruct((1, 1), F32),
        ],
        scratch_shapes=[
            pltpu.VMEM((count, spaces * 64), BF16),
            pltpu.VMEM((count, outputs), F32),
        ],
        compiler_params=pltpu.CompilerParams(vmem_limit_bytes=48 * 1024 * 1024),
    )(place, got)


def final_kernel_body(
    filters, patch_rows, cells, got_ref, dense_ref, total_ref, order_ref,
    step_conv_ref, step_dense_ref,
):
    scale = 1.0 / cells
    moments = from_halves(got_ref[...]).reshape(-1, 64)
    pad = jnp.zeros((128 - ROWS_IN, 64), F32)
    lower = jnp.concatenate([moments[64:ROWS_IN], pad], axis=0)
    corner = jnp.concatenate([moments[ROWS_IN:2 * ROWS_IN - 64], pad], axis=0)
    upper = jnp.concatenate([moments[0:64], jnp.transpose(lower)], axis=1)
    lower = jnp.concatenate([lower, corner], axis=1)
    conv_in = jnp.concatenate([upper, lower], axis=0) * scale
    first = 2 * ROWS_IN - 64
    conv_grad = jnp.concatenate(
        [moments[first:first + filters], moments[first + filters:first + 2 * filters]],
        axis=1,
    ) * scale
    conv_out = moments[first + 2 * filters:first + 3 * filters, 0:filters] * scale
    right, bound_in = residual(conv_in, patch_rows)
    left, bound_out = residual(conv_out, filters)
    held = conv_grad / bound_in / bound_out
    inverse = jnp.where(unit(128), 1.0, 0.0) + right
    for newton_step in range(NS_STEPS):
        held = held + exact_dot(left, held)
        if newton_step < NS_STEPS - 1:
            left = exact_dot(left, left)
            right = exact_dot(right, right)
            inverse = inverse + exact_dot(inverse, right)
    held = exact_dot(held, inverse)
    total = scalar_sum(held * conv_grad) + total_ref[...]
    scaling = jnp.minimum(1.0, jnp.sqrt(KL_BOUND / (LEARN_RATE * LEARN_RATE * total)))
    moved = exact_dot(held, order_ref[...])
    step_conv_ref[...] = scaling * moved[:, 0:patch_rows]
    step_dense_ref[...] = scaling * dense_ref[...]


def final_steps(moments, dense_block, dense_total, order, filters, patch_rows, cells):
    vmem = pl.BlockSpec(memory_space=pltpu.VMEM)
    return pl.pallas_call(
        functools.partial(final_kernel_body, filters, patch_rows, cells),
        in_specs=[vmem] * 4,
        out_specs=[vmem] * 2,
        out_shape=[
            jax.ShapeDtypeStruct((filters, patch_rows), F32),
            jax.ShapeDtypeStruct(dense_block.shape, F32),
        ],
        compiler_params=pltpu.CompilerParams(vmem_limit_bytes=32 * 1024 * 1024),
    )(moments, dense_block, dense_total, order)


def column_order(channels):
    row = lax.broadcasted_iota(jnp.int32, (128, 128), 0)
    column = lax.broadcasted_iota(jnp.int32, (128, 128), 1)
    channel, rest = column // 27, column % 27
    source = (rest // 9) * (9 * channels) + channel * 9 + rest % 9
    return jnp.where(jnp.logical_and(row == source, column < 27 * channels), 1.0, 0.0)


def on_device(volume, conv_kernel, dense_weight, cotangent):
    spaces = lax.axis_size(SPACE)
    groups = lax.axis_size(DP)
    column = lax.axis_size(COLUMN)
    samples, channels, planes, height, length = volume.shape
    filters, patch_rows = conv_kernel.shape
    slab = filters * PC

    up = [(i, i + 1) for i in range(spaces - 1)]
    down = [(j, i) for i, j in up]
    before = lax.ppermute(volume[:, :, planes - 1:], SPACE, up)
    after = lax.ppermute(volume[:, :, :1], SPACE, down)
    cot_group = gather_from(cotangent[0], SPACE, spaces)

    mixed = conv_kernel.reshape(filters, channels, 3, 9).transpose(0, 2, 1, 3)
    mixed = mixed.reshape(filters, patch_rows)
    spare = (planes + 2) * channels * 9 - patch_rows
    bands = jnp.concatenate(
        [
            jnp.pad(mixed, ((0, 0), (p * channels * 9, spare - p * channels * 9)))
            for p in range(planes)
        ],
        axis=0,
    )
    place = lax.axis_index(SPACE)
    weight = lax.dynamic_slice_in_dim(dense_weight, place * slab, slab, 0)
    weight = weight.reshape(filters, PC, -1).transpose(1, 0, 2).reshape(slab, -1)

    sent = conv_moments(
        volume, before, after, bands, weight, cot_group, cotangent, filters, column
    )
    peers = spaces * groups // column
    got = exchange(middle(exchange(sent, COLUMN), peers), PLANE)
    reduced = exchange(spread(got, column), COLUMN)
    delta, dense_total = dense_delta(
        place.reshape(1), got, column, spaces, cotangent.shape[1]
    )
    share = cotangent.shape[1] // groups
    dense_block = lax.dynamic_slice_in_dim(delta, lax.axis_index(DP) * share, share, 0)
    cells = samples * groups * planes * spaces * height * length
    step_conv, step_dense = final_steps(
        reduced, dense_block, dense_total, column_order(channels), filters, patch_rows, cells
    )
    return step_conv, step_dense.T


def solution(mesh):
    fine = jax.sharding.Mesh(mesh.devices.reshape(-1, 2, 2, 2, 4), ("z", "xh", "core", "xl", "y"))
    placed = (P(DP, None, SPACE, None, None), P(), P(), P(DP + SPACE, None))
    return jax.shard_map(
        on_device, mesh=fine, in_specs=placed, out_specs=(P(), P(SPACE, DP)), check_vma=False
    )
```

```python
import functools

import jax
import jax.numpy as jnp
from jax import lax
from jax.experimental import pallas as pl
from jax.experimental.pallas import tpu as pltpu
from jax.sharding import PartitionSpec as P


PC = 2
NS_STEPS = 8

LEAK_SLOPE = 0.3
DAMPING = 0.1
KL_BOUND = 0.0001
LEARN_RATE = 0.01
CONTRACT = (((1,), (1,)), ((), ()))
LEADING = (((0,), (0,)), ((), ()))
DP = ("z", "xh", "core")
SPACE = ("xl", "y")
COLUMN = ("z", "core")
PLANE = ("xh", "xl", "y")
F32 = jnp.float32
BF16 = jnp.bfloat16
ROWS_IN = 112


def exchange(x, axes):
    return lax.all_to_all(x, axes, split_axis=0, concat_axis=0, tiled=True)


def gather_from(x, axes, peers):
    return exchange(jnp.broadcast_to(x[None], (peers,) + x.shape), axes)


def conv_kernel_body(
    sizes, vol_ref, before_ref, after_ref, bands_ref, weight_ref, cot_ref, own_ref,
    sent_ref, pool_ref, shifted, stacked, grads, acc, acc_out,
):
    channels, planes, height, length, filters, samples = sizes
    rim = planes + 2
    per_plane = channels * 9
    rows = rim * per_plane
    cells = height * length
    half = cells // PC
    top = planes * filters
    step = pl.program_id(0)

    @pl.when(step == 0)
    def _():
        shifted[...] = jnp.zeros_like(shifted)
        acc[...] = jnp.zeros_like(acc)
        acc_out[...] = jnp.zeros_like(acc_out)
        pool_ref[...] = jnp.zeros_like(pool_ref)
        grads[...] = lax.dot_general(
            weight_ref[...], cot_ref[...], CONTRACT, preferred_element_type=F32
        ).astype(BF16).astype(F32)

    lane = lax.broadcasted_iota(jnp.int32, (height, length), 1)
    for plane in range(rim):
        for channel in range(channels):
            if plane == 0:
                value = before_ref[0, channel, 0]
            elif plane == rim - 1:
                value = after_ref[0, channel, 0]
            else:
                value = vol_ref[0, channel, plane - 1]
            value = value.astype(F32)
            moved = (
                jnp.where(lane == 0, 0.0, pltpu.roll(value, 1, 1)),
                value,
                jnp.where(lane == length - 1, 0.0, pltpu.roll(value, length - 1, 1)),
            )
            for j in range(3):
                for k in range(3):
                    row = plane * per_plane + channel * 9 + j * 3 + k
                    shifted[pl.ds((2 - j) * rows + row, height, stride=rows), :] = moved[k]
    for y in range(height):
        stacked[top:, y * length:(y + 1) * length] = shifted[
            (y + 1) * rows:(y + 2) * rows, :
        ].astype(BF16)

    column = lax.broadcasted_iota(jnp.int32, (filters * PC, samples), 1)
    grad_all = jnp.sum(jnp.where(column == step, grads[...], 0.0), axis=1, keepdims=True)
    low_all = (LEAK_SLOPE * grad_all).astype(BF16).astype(F32)
    pooled = []
    for part in range(PC):
        lanes = slice(part * half, (part + 1) * half)
        pre = jnp.dot(bands_ref[...], stacked[top:, lanes], preferred_element_type=F32)
        active = jnp.where(pre > 0, pre, LEAK_SLOPE * pre)
        total = active[0:filters]
        for plane in range(1, planes):
            total = total + active[plane * filters:(plane + 1) * filters]
        pooled.append(jnp.sum(total, axis=1, keepdims=True))
        grad = jnp.concatenate([grad_all[part * filters:(part + 1) * filters]] * planes, axis=0)
        low = jnp.concatenate([low_all[part * filters:(part + 1) * filters]] * planes, axis=0)
        stacked[0:top, lanes] = jnp.where(pre > 0, grad, low).astype(BF16)
    pooled = jnp.concatenate(pooled, axis=0) * (1.0 / (planes * half))
    spot = lax.broadcasted_iota(jnp.int32, pool_ref.shape, 1)
    pool_ref[...] = jnp.where(spot == step, pooled, pool_ref[...])
    acc[0:top + rows, :rows] += lax.dot_general(
        stacked[...], stacked[top:, :], CONTRACT, preferred_element_type=F32
    )
    acc_out[...] += lax.dot_general(
        stacked[0:top, :], stacked[0:top, :], CONTRACT, preferred_element_type=F32
    )

    @pl.when(step == pl.num_programs(0) - 1)
    def _():
        width = acc.shape[1]
        wide = 3 * per_plane
        moment_in = jnp.zeros((ROWS_IN, 128), F32)
        gradient = jnp.zeros((filters, 128), F32)
        moment_out = jnp.zeros((filters, 128), F32)
        for plane in range(planes):
            start = plane * per_plane
            turn = (width - start) % width
            block = acc[top + start:top + start + ROWS_IN, :]
            moment_in += (pltpu.roll(block, turn, 1) if turn else block)[:, :128]
            block = acc[plane * filters:(plane + 1) * filters, :]
            gradient += (pltpu.roll(block, turn, 1) if turn else block)[:, :128]
            block = acc_out[plane * filters:(plane + 1) * filters, :]
            turn = (top - plane * filters) % top
            moment_out += pltpu.roll(block, turn, 1) if turn else block
        row_in = lax.broadcasted_iota(jnp.int32, (ROWS_IN, 128), 0)
        lane_in = lax.broadcasted_iota(jnp.int32, (ROWS_IN, 128), 1)
        moment_in = jnp.where(jnp.maximum(row_in, lane_in) < wide, moment_in, 0.0)
        lane_out = lax.broadcasted_iota(jnp.int32, (filters, 128), 1)
        gradient = jnp.where(lane_out < wide, gradient, 0.0)
        packed = jnp.concatenate(
            [
                moment_in[:, :64],
                moment_in[64:, 64:],
                gradient[:, :64],
                gradient[:, 64:],
                moment_out[:, :64],
            ],
            axis=0,
        )
        groups = sent_ref.shape[0]
        share = packed.shape[0] // groups
        sent_ref[:, 0:share, :] = in_halves(packed).reshape(groups, share, 128)
        feats = jnp.transpose(pool_ref[...])[:samples]
        own = own_ref[...].astype(F32)
        own = jnp.concatenate([own[:, :64], own[:, 64:], jnp.zeros((samples - 2, 64), F32)], axis=0)
        both = jnp.concatenate([feats, own], axis=1).astype(BF16)
        sent_ref[:, share:, :] = jnp.broadcast_to(both[None], (groups, samples, 128))


def in_halves(x):
    high = x.astype(BF16)
    low = (x - high.astype(F32)).astype(BF16)
    return jnp.concatenate([high, low], axis=1)


def from_halves(x):
    wide = x.astype(F32)
    return wide[..., :64] + wide[..., 64:]


def conv_moments(volume, before, after, bands, weight, cot_group, own, filters, groups):
    samples, channels, planes, height, length = volume.shape
    per_plane = channels * 9
    rows = (planes + 2) * per_plane
    top = planes * filters
    sizes = (channels, planes, height, length, filters, samples)
    whole = lambda shape: pl.BlockSpec(shape, lambda b: (0,) * len(shape))
    return pl.pallas_call(
        functools.partial(conv_kernel_body, sizes),
        grid=(samples,),
        in_specs=[
            pl.BlockSpec((1, channels, planes, height, length), lambda b: (b, 0, 0, 0, 0)),
            pl.BlockSpec((1, channels, 1, height, length), lambda b: (b, 0, 0, 0, 0)),
            pl.BlockSpec((1, channels, 1, height, length), lambda b: (b, 0, 0, 0, 0)),
            whole(bands.shape),
            whole(weight.shape),
            whole(cot_group.shape),
            whole(own.shape),
        ],
        out_specs=whole((groups, 256 // groups + samples, 128)),
        out_shape=jax.ShapeDtypeStruct((groups, 256 // groups + samples, 128), BF16),
        scratch_shapes=[
            pltpu.VMEM((filters * PC, 128), F32),
            pltpu.VMEM(((height + 2) * rows, length), F32),
            pltpu.VMEM((top + rows, height * length), BF16),
            pltpu.VMEM((filters * PC, samples), F32),
            pltpu.VMEM((top + rows + 8, 256), F32),
            pltpu.VMEM((top, top), F32),
        ],
        compiler_params=pltpu.CompilerParams(vmem_limit_bytes=48 * 1024 * 1024),
    )(volume, before, after, bands, weight, cot_group, own)


def middle_body(got_ref, sent_ref):
    groups = got_ref.shape[0]
    pairs = groups // 2
    rows = pairs * 8
    share = got_ref.shape[1] - 8
    chunk = jnp.sum(from_halves(got_ref[:, 0:share, :]), axis=0)
    wide = got_ref[:, share:, :].astype(F32)
    feats = wide[:, :, :64]
    feats = jnp.concatenate([feats[:pairs], feats[pairs:]], axis=2).reshape(rows, 128)
    cots = jnp.concatenate([wide[:, 0, 64:], wide[:, 1, 64:]], axis=1)
    feats = feats.astype(BF16)
    cots = cots.astype(BF16)
    chunk = in_halves(chunk)
    for peer in range(sent_ref.shape[0]):
        sent_ref[peer, 0:rows, :] = feats
        sent_ref[peer, rows:rows + groups, :] = cots
        sent_ref[peer, rows + groups:, :] = chunk


def middle(got, peers):
    groups, rows, lanes = got.shape
    vmem = pl.BlockSpec(memory_space=pltpu.VMEM)
    return pl.pallas_call(
        middle_body,
        in_specs=[vmem],
        out_specs=vmem,
        out_shape=jax.ShapeDtypeStruct((peers, groups * 5 + rows - 8, lanes), BF16),
        compiler_params=pltpu.CompilerParams(vmem_limit_bytes=8 * 1024 * 1024),
    )(got)


def spread_body(got_ref, sent_ref):
    chunk = jnp.sum(from_halves(got_ref[...]), axis=0)
    sent_ref[...] = jnp.broadcast_to(in_halves(chunk)[None], sent_ref.shape)


def spread(got, groups):
    peers, rows, lanes = got.shape
    share = 256 // groups
    return pl.pallas_call(
        spread_body,
        grid=(1,),
        in_specs=[pl.BlockSpec((peers, share, lanes), lambda i: (0, rows // share - 1, 0))],
        out_specs=pl.BlockSpec((groups, share, lanes), lambda i: (0, 0, 0)),
        out_shape=jax.ShapeDtypeStruct((groups, share, lanes), BF16),
        compiler_params=pltpu.CompilerParams(vmem_limit_bytes=8 * 1024 * 1024),
    )(got)


def parts_of(x):
    high = x.astype(BF16)
    return high, (x - high.astype(F32)).astype(BF16)


def split_dot(a, b):
    a_high, a_low = parts_of(a)
    b_high, b_low = parts_of(b)
    return jnp.dot(
        jnp.concatenate([a_high, a_high, a_low], axis=1),
        jnp.concatenate([b_high, b_low, b_high], axis=0),
        preferred_element_type=F32,
    )


def square_and_apply(left, held, last):
    order = left.shape[1]
    if last:
        both = held
    else:
        both = jnp.concatenate([left, held], axis=1)
    if both.shape[0] < order:
        rest = jnp.zeros((order - both.shape[0], both.shape[1]), F32)
        both = jnp.concatenate([both, rest], axis=0)
    product = split_dot(left, both)
    if last:
        return left, held + product
    return product[:, :order], held + product[:, order:]


def square_and_extend(inverse, right, last):
    if last:
        return inverse + split_dot(inverse, right), right
    order = right.shape[0]
    product = split_dot(jnp.concatenate([inverse, right], axis=0), right)
    return inverse + product[:order], product[order:]


def two_sided(left, held, right):
    order = right.shape[0]
    inverse = jnp.where(unit(order), 1.0, 0.0) + right
    right = split_dot(right, right)
    for step in range(NS_STEPS):
        left, held = square_and_apply(left, held, step == NS_STEPS - 1)
        if step > 0:
            inverse, right = square_and_extend(inverse, right, step == NS_STEPS - 1)
    return split_dot(held, inverse)


def unit(order):
    row = lax.broadcasted_iota(jnp.int32, (order, order), 0)
    column = lax.broadcasted_iota(jnp.int32, (order, order), 1)
    return row == column


def scalar_sum(x):
    return jnp.sum(jnp.sum(x, axis=0, keepdims=True), axis=1, keepdims=True)


def residual(factor, order):
    size = factor.shape[0]
    eye = unit(size)
    trace = scalar_sum(jnp.where(eye, factor, 0.0))
    damping = DAMPING * trace / order
    sums = jnp.sum(jnp.abs(factor), axis=0, keepdims=True) + damping
    bound = jnp.max(sums, axis=1, keepdims=True)
    inside = lax.broadcasted_iota(jnp.int32, (size, size), 0) < order
    start = jnp.where(jnp.logical_and(eye, inside), 1.0 - damping / bound, 0.0)
    return start - factor / bound, bound


def dense_kernel_body(groups, spaces, place_ref, got_ref, delta_ref, total_ref, whole, cots):
    parts = got_ref.shape[0] // spaces
    width = 64
    block = groups * 8
    count = parts * block
    half = block // 2

    def slab_of(index):
        pieces = []
        for part in range(parts):
            both = got_ref[part * spaces + index].astype(F32)[:half]
            pieces += [both[:, :width], both[:, width:]]
        return jnp.concatenate(pieces, axis=0)

    for slab in range(0, spaces, 2):
        pair = jnp.concatenate([slab_of(slab), slab_of(slab + 1)], axis=1)
        whole[:, slab * width:(slab + 2) * width] = pair.astype(BF16)
    for part in range(parts):
        for slab in range(spaces):
            cots[pl.ds(part * block + slab, groups, stride=spaces), :] = got_ref[
                part * spaces + slab, half:half + groups, :
            ].astype(F32)
    cot_wide = cots[...]
    cot = cot_wide.astype(BF16)
    feats = whole[...]
    scale = 1.0 / count
    gram = lax.dot_general(feats, feats, CONTRACT, preferred_element_type=F32) * scale
    dense_in = lax.dot_general(feats, feats, LEADING, preferred_element_type=F32) * scale
    dense_out = lax.dot_general(cot, cot, LEADING, preferred_element_type=F32) * scale
    order = spaces * width
    eye = unit(count)
    damping = DAMPING * scalar_sum(jnp.where(eye, gram, 0.0)) / order
    sums = jnp.sum(jnp.abs(dense_in), axis=0, keepdims=True) + damping
    bound = jnp.max(sums, axis=1, keepdims=True)
    left = jnp.where(eye, 1.0 - damping / bound, 0.0) - gram / bound
    right, bound_out = residual(dense_out, dense_out.shape[0])
    held = two_sided(left, cot_wide * (scale / bound / bound_out), right)
    total_ref[...] = scalar_sum(held * split_dot(gram, cot_wide))
    mine = slab_of(place_ref[0])
    source = lax.broadcasted_iota(jnp.int32, (width, width), 0)
    target = lax.broadcasted_iota(jnp.int32, (width, width), 1)
    spot = (target % PC) * (width // PC) + target // PC
    pick = jnp.where(source == spot, 1.0, 0.0).astype(BF16)
    mine = jnp.dot(mine.astype(BF16), pick, preferred_element_type=F32).astype(BF16)
    high, low = parts_of(held)
    delta_ref[...] = lax.dot_general(
        jnp.concatenate([high, low], axis=0),
        jnp.concatenate([mine, mine], axis=0),
        LEADING,
        preferred_element_type=F32,
    )


def dense_delta(place, got, groups, spaces, outputs):
    count = groups * 8 * (got.shape[0] // spaces)
    vmem = pl.BlockSpec(memory_space=pltpu.VMEM)
    return pl.pallas_call(
        functools.partial(dense_kernel_body, groups, spaces),
        in_specs=[pl.BlockSpec(memory_space=pltpu.SMEM), vmem],
        out_specs=[vmem, vmem],
        out_shape=[
            jax.ShapeDtypeStruct((outputs, 64), F32),
            jax.ShapeDtypeStruct((1, 1), F32),
        ],
        scratch_shapes=[
            pltpu.VMEM((count, spaces * 64), BF16),
            pltpu.VMEM((count, outputs), F32),
        ],
        compiler_params=pltpu.CompilerParams(vmem_limit_bytes=48 * 1024 * 1024),
    )(place, got)


def final_kernel_body(
    filters, patch_rows, cells, got_ref, dense_ref, total_ref, order_ref,
    step_conv_ref, step_dense_ref,
):
    scale = 1.0 / cells
    moments = from_halves(got_ref[...]).reshape(-1, 64)
    pad = jnp.zeros((128 - ROWS_IN, 64), F32)
    lower = jnp.concatenate([moments[64:ROWS_IN], pad], axis=0)
    corner = jnp.concatenate([moments[ROWS_IN:2 * ROWS_IN - 64], pad], axis=0)
    upper = jnp.concatenate([moments[0:64], jnp.transpose(lower)], axis=1)
    lower = jnp.concatenate([lower, corner], axis=1)
    conv_in = jnp.concatenate([upper, lower], axis=0) * scale
    first = 2 * ROWS_IN - 64
    conv_grad = jnp.concatenate(
        [moments[first:first + filters], moments[first + filters:first + 2 * filters]],
        axis=1,
    ) * scale
    conv_out = moments[first + 2 * filters:first + 3 * filters]
    conv_out = jnp.concatenate([conv_out, jnp.zeros((filters, 64), F32)], axis=1)
    conv_out = jnp.concatenate([conv_out, jnp.zeros((128 - filters, 128), F32)], axis=0) * scale
    right, bound_in = residual(conv_in, patch_rows)
    left, bound_out = residual(conv_out, filters)
    held = two_sided(left[0:filters], conv_grad / bound_in / bound_out, right)
    total = scalar_sum(held * conv_grad) + total_ref[...]
    scaling = jnp.minimum(1.0, jnp.sqrt(KL_BOUND / (LEARN_RATE * LEARN_RATE * total)))
    moved = split_dot(held, order_ref[...])
    step_conv_ref[...] = scaling * moved[:, 0:patch_rows]
    step_dense_ref[...] = scaling * dense_ref[...]


def final_steps(moments, dense_block, dense_total, order, filters, patch_rows, cells):
    vmem = pl.BlockSpec(memory_space=pltpu.VMEM)
    return pl.pallas_call(
        functools.partial(final_kernel_body, filters, patch_rows, cells),
        in_specs=[vmem] * 4,
        out_specs=[vmem] * 2,
        out_shape=[
            jax.ShapeDtypeStruct((filters, patch_rows), F32),
            jax.ShapeDtypeStruct(dense_block.shape, F32),
        ],
        compiler_params=pltpu.CompilerParams(vmem_limit_bytes=32 * 1024 * 1024),
    )(moments, dense_block, dense_total, order)


def column_order(channels):
    row = lax.broadcasted_iota(jnp.int32, (128, 128), 0)
    column = lax.broadcasted_iota(jnp.int32, (128, 128), 1)
    channel, rest = column // 27, column % 27
    source = (rest // 9) * (9 * channels) + channel * 9 + rest % 9
    return jnp.where(jnp.logical_and(row == source, column < 27 * channels), 1.0, 0.0)


def on_device(volume, conv_kernel, dense_weight, cotangent):
    spaces = lax.axis_size(SPACE)
    groups = lax.axis_size(DP)
    column = lax.axis_size(COLUMN)
    samples, channels, planes, height, length = volume.shape
    filters, patch_rows = conv_kernel.shape
    slab = filters * PC

    up = [(i, i + 1) for i in range(spaces - 1)]
    down = [(j, i) for i, j in up]
    cot_group = gather_from(cotangent[0], SPACE, spaces)
    before = lax.ppermute(volume[:, :, planes - 1:], SPACE, up)
    after = lax.ppermute(volume[:, :, :1], SPACE, down)

    mixed = conv_kernel.reshape(filters, channels, 3, 9).transpose(0, 2, 1, 3)
    mixed = mixed.reshape(filters, patch_rows)
    spare = (planes + 2) * channels * 9 - patch_rows
    bands = jnp.concatenate(
        [
            jnp.pad(mixed, ((0, 0), (p * channels * 9, spare - p * channels * 9)))
            for p in range(planes)
        ],
        axis=0,
    )
    place = lax.axis_index(SPACE)
    weight = lax.dynamic_slice_in_dim(dense_weight, place * slab, slab, 0)
    weight = weight.reshape(filters, PC, -1).transpose(1, 0, 2).reshape(slab, -1)

    sent = conv_moments(
        volume, before, after, bands, weight, cot_group, cotangent, filters, column
    )
    peers = spaces * groups // column
    got = exchange(middle(exchange(sent, COLUMN), peers), PLANE)
    reduced = exchange(spread(got, column), COLUMN)
    delta, dense_total = dense_delta(
        place.reshape(1), got, column, spaces, cotangent.shape[1]
    )
    share = cotangent.shape[1] // groups
    dense_block = lax.dynamic_slice_in_dim(delta, lax.axis_index(DP) * share, share, 0)
    cells = samples * groups * planes * spaces * height * length
    step_conv, step_dense = final_steps(
        reduced, dense_block, dense_total, column_order(channels), filters, patch_rows, cells
    )
    return step_conv, step_dense.T


def solution(mesh):
    fine = jax.sharding.Mesh(mesh.devices.reshape(-1, 2, 2, 2, 4), ("z", "xh", "core", "xl", "y"))
    placed = (P(DP, None, SPACE, None, None), P(), P(), P(DP + SPACE, None))
    return jax.shard_map(
        on_device, mesh=fine, in_specs=placed, out_specs=(P(), P(SPACE, DP)), check_vma=False
    )
```

```python
import functools

import jax
import jax.numpy as jnp
from jax import lax
from jax.experimental import pallas as pl
from jax.experimental.pallas import tpu as pltpu
from jax.sharding import PartitionSpec as P


PC = 2
NS_STEPS = 8

LEAK_SLOPE = 0.3
DAMPING = 0.1
KL_BOUND = 0.0001
LEARN_RATE = 0.01
CONTRACT = (((1,), (1,)), ((), ()))
LEADING = (((0,), (0,)), ((), ()))
DP = ("z", "xh", "core")
SPACE = ("xl", "y")
COLUMN = ("z", "core")
PLANE = ("xh", "xl", "y")
F32 = jnp.float32
BF16 = jnp.bfloat16
ROWS_IN = 112


def exchange(x, axes):
    return lax.all_to_all(x, axes, split_axis=0, concat_axis=0, tiled=True)


def gather_from(x, axes, peers):
    return exchange(jnp.broadcast_to(x[None], (peers,) + x.shape), axes)


def turned(x, by):
    return pltpu.roll(x, x.shape[1] - by, 1) if by else x


def conv_kernel_body(
    sizes, vol_ref, before_ref, after_ref, bands_ref,
    pool_ref, sums_ref, gram_ref, shift_a, shift_b, stack_a, stack_b, wide_a, wide_b,
):
    channels, planes, height, length, filters, samples = sizes
    rim = planes + 2
    group = rim * channels * 3
    rows = 3 * group
    half = height * length // PC
    top = planes * filters
    base = top + 16
    step = pl.program_id(0)

    def build(sample, shifted, stacked):
        lane = lax.broadcasted_iota(jnp.int32, (height, length), 1)
        for plane in range(rim):
            for channel in range(channels):
                if plane == 0:
                    value = before_ref[sample, channel, 0]
                elif plane == rim - 1:
                    value = after_ref[sample, channel, 0]
                else:
                    value = vol_ref[sample, channel, plane - 1]
                value = value.astype(F32)
                moved = (
                    jnp.where(lane == 0, 0.0, pltpu.roll(value, 1, 1)),
                    value,
                    jnp.where(lane == length - 1, 0.0, pltpu.roll(value, length - 1, 1)),
                )
                for k in range(3):
                    row = group + (plane * channels + channel) * 3 + k
                    shifted[pl.ds(row, height, stride=group), :] = moved[k]
        for y in range(height):
            stacked[base:, y * length:(y + 1) * length] = shifted[
                y * group:y * group + rows, :
            ].astype(BF16)

    def consume(sample, stacked, wide):
        slot = sample * PC
        pooled = []
        for part in range(PC):
            total = jnp.zeros((filters, 128), F32)
            for piece in range(2):
                first = part * half + piece * (half // 2)
                lanes = slice(first, first + half // 2)
                pre = jnp.dot(bands_ref[...], stacked[base:, lanes], preferred_element_type=F32)
                stacked[0:top, lanes] = jnp.where(pre > 0, 1.0, 0.0).astype(BF16)
                active = jnp.where(pre > 0, pre, LEAK_SLOPE * pre)
                for plane in range(planes):
                    for at in range(0, half // 2, 128):
                        total += active[plane * filters:(plane + 1) * filters, at:at + 128]
            pooled.append(jnp.sum(total, axis=1, keepdims=True))
            lanes = slice(part * half, (part + 1) * half)
            gram = lax.dot_general(
                stacked[:base + group, lanes], stacked[base:, lanes], CONTRACT,
                preferred_element_type=F32,
            )
            wide[part, :, :rows] = gram[:top + 8]
            gram_ref[:, :rows] += gram[base:]
            square = lax.dot_general(
                stacked[:base, lanes], stacked[:top, lanes], CONTRACT,
                preferred_element_type=F32,
            )
            for first, last in ((0, filters), (top, top + 8)):
                patch = jnp.zeros((last - first, 256), F32)
                mask = jnp.zeros((last - first, top), F32)
                for plane in range(planes):
                    at = slice(first, last)
                    if first == 0:
                        at = slice(plane * filters, (plane + 1) * filters)
                    patch += turned(wide[part, at, :], plane * channels * 3)
                    mask += turned(square[at], plane * filters)
                to = slice(0, filters) if first == 0 else slice(filters, filters + 8)
                sums_ref[slot + part, to, :256] = patch
                sums_ref[slot + part, to, 256:] = mask
        for side, y in ((0, height - 1), (1, 0)):
            edge = stacked[base + group:base + 2 * group, y * length:(y + 1) * length]
            gram_ref[:, 256 + side * 128:256 + side * 128 + group] += lax.dot_general(
                edge, edge, CONTRACT, preferred_element_type=F32
            )
        pooled = jnp.concatenate(pooled, axis=0) * (1.0 / (planes * half))
        spot = lax.broadcasted_iota(jnp.int32, pool_ref.shape, 1)
        pool_ref[...] = jnp.where(spot == sample, pooled, pool_ref[...])

    @pl.when(step == 0)
    def _():
        shift_a[...] = jnp.zeros_like(shift_a)
        shift_b[...] = jnp.zeros_like(shift_b)
        ones = jnp.ones((16, height * length), BF16)
        stack_a[top:base, :] = ones
        stack_b[top:base, :] = ones
        gram_ref[...] = jnp.zeros_like(gram_ref)
        pool_ref[...] = jnp.zeros_like(pool_ref)
        build(0, shift_a, stack_a)

    build(2 * step + 1, shift_b, stack_b)
    consume(2 * step, stack_a, wide_a)
    build(jnp.minimum(2 * step + 2, samples - 1), shift_a, stack_a)
    consume(2 * step + 1, stack_b, wide_b)


def conv_sums(volume, before, after, bands, filters):
    samples, channels, planes, height, length = volume.shape
    group = (planes + 2) * channels * 3
    top = planes * filters
    stack = top + 16 + 3 * group
    sizes = (channels, planes, height, length, filters, samples)
    vmem = pl.BlockSpec(memory_space=pltpu.VMEM)
    return pl.pallas_call(
        functools.partial(conv_kernel_body, sizes),
        grid=(samples // 2,),
        in_specs=[vmem] * 4,
        out_specs=[vmem] * 3,
        out_shape=[
            jax.ShapeDtypeStruct((filters * PC, 128), F32),
            jax.ShapeDtypeStruct((samples * PC, filters + 8, 256 + top), F32),
            jax.ShapeDtypeStruct((group, 512), F32),
        ],
        scratch_shapes=[
            pltpu.VMEM(((height + 2) * group, length), F32),
            pltpu.VMEM(((height + 2) * group, length), F32),
            pltpu.VMEM((stack, height * length), BF16),
            pltpu.VMEM((stack, height * length), BF16),
            pltpu.VMEM((PC, top + 8, 256), F32),
            pltpu.VMEM((PC, top + 8, 256), F32),
        ],
        compiler_params=pltpu.CompilerParams(vmem_limit_bytes=24 * 1024 * 1024),
    )(volume, before, after, bands)


def moments_body(
    sizes, pool_ref, sums_ref, gram_ref, weight_ref, cot_ref, own_ref, sent_ref, held, turned_up,
):
    channels, planes, cells, filters, samples = sizes
    inner = channels * 3
    group = (planes + 2) * inner
    wide = 3 * 3 * inner
    part_rows = 3 * inner
    lanes_of = lambda shape: lax.broadcasted_iota(jnp.int32, shape, 1)

    def compact(x):
        lane = lanes_of(x.shape)
        out = jnp.where(lane < part_rows, x, 0.0)
        for j in range(1, 3):
            here = jnp.logical_and(lane >= j * part_rows, lane < (j + 1) * part_rows)
            out = jnp.where(here, turned(x, j * (group - part_rows)), out)
        return out[:, :128]

    cots = cot_ref[...]
    gradient = jnp.zeros((filters, 256), F32)
    moment_out = jnp.zeros((filters, 128), F32)
    cross = jnp.zeros((filters, 128), F32)
    for part in range(PC):
        weight = weight_ref[part * filters:(part + 1) * filters, :]
        grad_down = lax.dot_general(weight, cots, CONTRACT, preferred_element_type=F32)
        weight = jnp.concatenate([weight, jnp.zeros((128 - filters, 128), BF16)], axis=0)
        grad_over = lax.dot_general(cots, weight, CONTRACT, preferred_element_type=F32)
        grad_down = grad_down.astype(BF16).astype(F32)
        grad_over = grad_over.astype(BF16).astype(F32)
        low_down = (LEAK_SLOPE * grad_down).astype(BF16).astype(F32)
        low_over = (LEAK_SLOPE * grad_over).astype(BF16).astype(F32)
        gap_down = grad_down - low_down
        gap_over = grad_over - low_over
        for sample in range(samples):
            slot = sample * PC + part
            gap = gap_down[:, sample:sample + 1]
            low = low_down[:, sample:sample + 1]
            across = gap_over[sample:sample + 1, :]
            gradient += gap * sums_ref[slot, :filters, :256]
            gradient += low * sums_ref[slot, filters:filters + 1, :256]
            moment_out += gap * sums_ref[slot, :filters, 256:] * across
            cross += low * (
                across * sums_ref[slot, filters:filters + 1, 256:]
                + (0.5 * cells) * low_over[sample:sample + 1, :]
            )
    lane = lanes_of(cross.shape)
    cross = jnp.where(lane < filters, cross, 0.0)
    tall = jnp.concatenate([cross, jnp.zeros((128 - filters, 128), F32)], axis=0)
    moment_out = jnp.where(lane < filters, moment_out, 0.0)
    moment_out += cross + jnp.transpose(tall)[:filters]

    blocks = jnp.zeros((part_rows, 512), F32)
    for plane in range(planes):
        start = plane * inner
        blocks += turned(gram_ref[start:start + part_rows, :], start)
    first = compact(blocks[:, :256])
    lane = lanes_of(first.shape)
    second = first + jnp.where(lane < part_rows, blocks[:, 256:384], 0.0)
    third = second - jnp.where(lane < part_rows, blocks[:, 384:], 0.0)
    turned_up[...] = jnp.zeros_like(turned_up)
    turned_up[0:part_rows, :] = first
    turned_up[...] = jnp.transpose(turned_up[...])
    held[...] = jnp.zeros_like(held)
    held[0:part_rows, :] = first
    above = turned_up[part_rows:2 * part_rows, :]
    row = jnp.where(lane < part_rows, above, pltpu.roll(second, part_rows, 1))
    held[part_rows:2 * part_rows, :] = jnp.where(lane < wide, row, 0.0)
    row = jnp.where(
        lane < 2 * part_rows,
        pltpu.roll(above, part_rows, 1),
        pltpu.roll(third, 2 * part_rows, 1),
    )
    row = jnp.where(lane < part_rows, turned_up[2 * part_rows:wide, :], row)
    held[2 * part_rows:wide, :] = jnp.where(lane < wide, row, 0.0)
    moment_in = held[...]
    gradient = compact(gradient)
    packed = jnp.concatenate(
        [
            moment_in[:, :64],
            moment_in[64:, 64:],
            gradient[:, :64],
            gradient[:, 64:],
            moment_out[:, :64],
        ],
        axis=0,
    )
    groups = sent_ref.shape[0]
    share = packed.shape[0] // groups
    sent_ref[:, 0:share, :] = in_halves(packed).reshape(groups, share, 128)
    feats = jnp.transpose(pool_ref[...])[:samples]
    own = own_ref[...].astype(F32)
    own = jnp.concatenate([own[:, :64], own[:, 64:], jnp.zeros((samples - 2, 64), F32)], axis=0)
    both = jnp.concatenate([feats, own], axis=1).astype(BF16)
    sent_ref[:, share:, :] = jnp.broadcast_to(both[None], (groups, samples, 128))


def conv_moments(sizes, sums, weight, cot_group, own, groups):
    samples = sizes[-1]
    rows = 256 // groups + samples
    vmem = pl.BlockSpec(memory_space=pltpu.VMEM)
    return pl.pallas_call(
        functools.partial(moments_body, sizes),
        in_specs=[vmem] * 6,
        out_specs=vmem,
        out_shape=jax.ShapeDtypeStruct((groups, rows, 128), BF16),
        scratch_shapes=[pltpu.VMEM((ROWS_IN, 128), F32), pltpu.VMEM((128, 128), F32)],
        compiler_params=pltpu.CompilerParams(vmem_limit_bytes=16 * 1024 * 1024),
    )(*sums, weight, cot_group, own)


def in_halves(x):
    high = x.astype(BF16)
    low = (x - high.astype(F32)).astype(BF16)
    return jnp.concatenate([high, low], axis=1)


def from_halves(x):
    wide = x.astype(F32)
    return wide[..., :64] + wide[..., 64:]


def middle_body(got_ref, sent_ref):
    groups = got_ref.shape[0]
    pairs = groups // 2
    rows = pairs * 8
    share = got_ref.shape[1] - 8
    chunk = jnp.sum(from_halves(got_ref[:, 0:share, :]), axis=0)
    wide = got_ref[:, share:, :].astype(F32)
    feats = wide[:, :, :64]
    feats = jnp.concatenate([feats[:pairs], feats[pairs:]], axis=2).reshape(rows, 128)
    cots = jnp.concatenate([wide[:, 0, 64:], wide[:, 1, 64:]], axis=1)
    feats = feats.astype(BF16)
    cots = cots.astype(BF16)
    chunk = in_halves(chunk)
    for peer in range(sent_ref.shape[0]):
        sent_ref[peer, 0:rows, :] = feats
        sent_ref[peer, rows:rows + groups, :] = cots
        sent_ref[peer, rows + groups:, :] = chunk


def middle(got, peers):
    groups, rows, lanes = got.shape
    vmem = pl.BlockSpec(memory_space=pltpu.VMEM)
    return pl.pallas_call(
        middle_body,
        in_specs=[vmem],
        out_specs=vmem,
        out_shape=jax.ShapeDtypeStruct((peers, groups * 5 + rows - 8, lanes), BF16),
        compiler_params=pltpu.CompilerParams(vmem_limit_bytes=8 * 1024 * 1024),
    )(got)


def spread_body(got_ref, sent_ref):
    chunk = jnp.sum(from_halves(got_ref[...]), axis=0)
    sent_ref[...] = jnp.broadcast_to(in_halves(chunk)[None], sent_ref.shape)


def spread(got, groups):
    peers, rows, lanes = got.shape
    share = 256 // groups
    return pl.pallas_call(
        spread_body,
        grid=(1,),
        in_specs=[pl.BlockSpec((peers, share, lanes), lambda i: (0, rows // share - 1, 0))],
        out_specs=pl.BlockSpec((groups, share, lanes), lambda i: (0, 0, 0)),
        out_shape=jax.ShapeDtypeStruct((groups, share, lanes), BF16),
        compiler_params=pltpu.CompilerParams(vmem_limit_bytes=8 * 1024 * 1024),
    )(got)


def parts_of(x):
    high = x.astype(BF16)
    return high, (x - high.astype(F32)).astype(BF16)


def split_dot(a, b):
    a_high, a_low = parts_of(a)
    b_high, b_low = parts_of(b)
    return jnp.dot(
        jnp.concatenate([a_high, a_high, a_low], axis=1),
        jnp.concatenate([b_high, b_low, b_high], axis=0),
        preferred_element_type=F32,
    )


def square_and_apply(left, held, last):
    order = left.shape[1]
    if last:
        both = held
    else:
        both = jnp.concatenate([left, held], axis=1)
    if both.shape[0] < order:
        rest = jnp.zeros((order - both.shape[0], both.shape[1]), F32)
        both = jnp.concatenate([both, rest], axis=0)
    product = split_dot(left, both)
    if last:
        return left, held + product
    return product[:, :order], held + product[:, order:]


def square_and_extend(inverse, right, last):
    if last:
        return inverse + split_dot(inverse, right), right
    order = right.shape[0]
    product = split_dot(jnp.concatenate([inverse, right], axis=0), right)
    return inverse + product[:order], product[order:]


def two_sided(left, held, right):
    order = right.shape[0]
    inverse = jnp.where(unit(order), 1.0, 0.0) + right
    right = split_dot(right, right)
    for step in range(NS_STEPS):
        left, held = square_and_apply(left, held, step == NS_STEPS - 1)
        if step > 0:
            inverse, right = square_and_extend(inverse, right, step == NS_STEPS - 1)
    return split_dot(held, inverse)


def unit(order):
    row = lax.broadcasted_iota(jnp.int32, (order, order), 0)
    column = lax.broadcasted_iota(jnp.int32, (order, order), 1)
    return row == column


def scalar_sum(x):
    return jnp.sum(jnp.sum(x, axis=0, keepdims=True), axis=1, keepdims=True)


def residual(factor, order):
    size = factor.shape[0]
    eye = unit(size)
    trace = scalar_sum(jnp.where(eye, factor, 0.0))
    damping = DAMPING * trace / order
    sums = jnp.sum(jnp.abs(factor), axis=0, keepdims=True) + damping
    bound = jnp.max(sums, axis=1, keepdims=True)
    inside = lax.broadcasted_iota(jnp.int32, (size, size), 0) < order
    start = jnp.where(jnp.logical_and(eye, inside), 1.0 - damping / bound, 0.0)
    return start - factor / bound, bound


def dense_kernel_body(groups, spaces, place_ref, got_ref, delta_ref, total_ref, whole, cots):
    parts = got_ref.shape[0] // spaces
    width = 64
    block = groups * 8
    count = parts * block
    half = block // 2

    def slab_of(index):
        pieces = []
        for part in range(parts):
            both = got_ref[part * spaces + index].astype(F32)[:half]
            pieces += [both[:, :width], both[:, width:]]
        return jnp.concatenate(pieces, axis=0)

    for slab in range(0, spaces, 2):
        pair = jnp.concatenate([slab_of(slab), slab_of(slab + 1)], axis=1)
        whole[:, slab * width:(slab + 2) * width] = pair.astype(BF16)
    for part in range(parts):
        for slab in range(spaces):
            cots[pl.ds(part * block + slab, groups, stride=spaces), :] = got_ref[
                part * spaces + slab, half:half + groups, :
            ].astype(F32)
    cot_wide = cots[...]
    cot = cot_wide.astype(BF16)
    feats = whole[...]
    scale = 1.0 / count
    gram = lax.dot_general(feats, feats, CONTRACT, preferred_element_type=F32) * scale
    dense_in = lax.dot_general(feats, feats, LEADING, preferred_element_type=F32) * scale
    dense_out = lax.dot_general(cot, cot, LEADING, preferred_element_type=F32) * scale
    order = spaces * width
    eye = unit(count)
    damping = DAMPING * scalar_sum(jnp.where(eye, gram, 0.0)) / order
    sums = jnp.sum(jnp.abs(dense_in), axis=0, keepdims=True) + damping
    bound = jnp.max(sums, axis=1, keepdims=True)
    left = jnp.where(eye, 1.0 - damping / bound, 0.0) - gram / bound
    right, bound_out = residual(dense_out, dense_out.shape[0])
    held = two_sided(left, cot_wide * (scale / bound / bound_out), right)
    total_ref[...] = scalar_sum(held * split_dot(gram, cot_wide))
    mine = slab_of(place_ref[0])
    source = lax.broadcasted_iota(jnp.int32, (width, width), 0)
    target = lax.broadcasted_iota(jnp.int32, (width, width), 1)
    spot = (target % PC) * (width // PC) + target // PC
    pick = jnp.where(source == spot, 1.0, 0.0).astype(BF16)
    mine = jnp.dot(mine.astype(BF16), pick, preferred_element_type=F32).astype(BF16)
    high, low = parts_of(held)
    delta_ref[...] = lax.dot_general(
        jnp.concatenate([high, low], axis=0),
        jnp.concatenate([mine, mine], axis=0),
        LEADING,
        preferred_element_type=F32,
    )


def dense_delta(place, got, groups, spaces, outputs):
    count = groups * 8 * (got.shape[0] // spaces)
    vmem = pl.BlockSpec(memory_space=pltpu.VMEM)
    return pl.pallas_call(
        functools.partial(dense_kernel_body, groups, spaces),
        in_specs=[pl.BlockSpec(memory_space=pltpu.SMEM), vmem],
        out_specs=[vmem, vmem],
        out_shape=[
            jax.ShapeDtypeStruct((outputs, 64), F32),
            jax.ShapeDtypeStruct((1, 1), F32),
        ],
        scratch_shapes=[
            pltpu.VMEM((count, spaces * 64), BF16),
            pltpu.VMEM((count, outputs), F32),
        ],
        compiler_params=pltpu.CompilerParams(vmem_limit_bytes=48 * 1024 * 1024),
    )(place, got)


def final_kernel_body(
    filters, patch_rows, cells, got_ref, dense_ref, total_ref, order_ref,
    step_conv_ref, step_dense_ref,
):
    scale = 1.0 / cells
    moments = from_halves(got_ref[...]).reshape(-1, 64)
    pad = jnp.zeros((128 - ROWS_IN, 64), F32)
    lower = jnp.concatenate([moments[64:ROWS_IN], pad], axis=0)
    corner = jnp.concatenate([moments[ROWS_IN:2 * ROWS_IN - 64], pad], axis=0)
    upper = jnp.concatenate([moments[0:64], jnp.transpose(lower)], axis=1)
    lower = jnp.concatenate([lower, corner], axis=1)
    conv_in = jnp.concatenate([upper, lower], axis=0) * scale
    first = 2 * ROWS_IN - 64
    conv_grad = jnp.concatenate(
        [moments[first:first + filters], moments[first + filters:first + 2 * filters]],
        axis=1,
    ) * scale
    conv_out = moments[first + 2 * filters:first + 3 * filters]
    conv_out = jnp.concatenate([conv_out, jnp.zeros((filters, 64), F32)], axis=1)
    conv_out = jnp.concatenate([conv_out, jnp.zeros((128 - filters, 128), F32)], axis=0) * scale
    right, bound_in = residual(conv_in, patch_rows)
    left, bound_out = residual(conv_out, filters)
    held = two_sided(left[0:filters], conv_grad / bound_in / bound_out, right)
    total = scalar_sum(held * conv_grad) + total_ref[...]
    scaling = jnp.minimum(1.0, jnp.sqrt(KL_BOUND / (LEARN_RATE * LEARN_RATE * total)))
    moved = split_dot(held, order_ref[...])
    step_conv_ref[...] = scaling * moved[:, 0:patch_rows]
    step_dense_ref[...] = scaling * dense_ref[...]


def final_steps(moments, dense_block, dense_total, order, filters, patch_rows, cells):
    vmem = pl.BlockSpec(memory_space=pltpu.VMEM)
    return pl.pallas_call(
        functools.partial(final_kernel_body, filters, patch_rows, cells),
        in_specs=[vmem] * 4,
        out_specs=[vmem] * 2,
        out_shape=[
            jax.ShapeDtypeStruct((filters, patch_rows), F32),
            jax.ShapeDtypeStruct(dense_block.shape, F32),
        ],
        compiler_params=pltpu.CompilerParams(vmem_limit_bytes=32 * 1024 * 1024),
    )(moments, dense_block, dense_total, order)


def column_order(channels):
    row = lax.broadcasted_iota(jnp.int32, (128, 128), 0)
    column = lax.broadcasted_iota(jnp.int32, (128, 128), 1)
    channel, i, j, k = column // 27, column // 9 % 3, column // 3 % 3, column % 3
    source = ((j * 3 + i) * channels + channel) * 3 + k
    return jnp.where(jnp.logical_and(row == source, column < 27 * channels), 1.0, 0.0)


def on_device(volume, conv_kernel, dense_weight, cotangent):
    spaces = lax.axis_size(SPACE)
    groups = lax.axis_size(DP)
    column = lax.axis_size(COLUMN)
    samples, channels, planes, height, length = volume.shape
    filters, patch_rows = conv_kernel.shape
    slab = filters * PC

    up = [(i, i + 1) for i in range(spaces - 1)]
    down = [(j, i) for i, j in up]
    before = lax.ppermute(volume[:, :, planes - 1:], SPACE, up)
    after = lax.ppermute(volume[:, :, :1], SPACE, down)
    cot_group = gather_from(cotangent[0], SPACE, spaces)

    mixed = conv_kernel.reshape(filters, channels, 3, 3, 3).transpose(0, 3, 2, 1, 4)
    mixed = mixed.reshape(filters, 3, channels * 9)
    inner = channels * 3
    spare = (planes - 1) * inner
    bands = jnp.concatenate(
        [
            jnp.pad(mixed, ((0, 0), (0, 0), (p * inner, spare - p * inner)))
            for p in range(planes)
        ],
        axis=0,
    ).reshape(planes * filters, -1)
    place = lax.axis_index(SPACE)
    weight = lax.dynamic_slice_in_dim(dense_weight, place * slab, slab, 0)
    weight = weight.reshape(filters, PC, -1).transpose(1, 0, 2).reshape(slab, -1)

    sums = conv_sums(volume, before, after, bands, filters)
    sizes = (channels, planes, planes * height * length // PC, filters, samples)
    sent = conv_moments(sizes, sums, weight, cot_group, cotangent, column)
    peers = spaces * groups // column
    got = exchange(middle(exchange(sent, COLUMN), peers), PLANE)
    reduced = exchange(spread(got, column), COLUMN)
    delta, dense_total = dense_delta(
        place.reshape(1), got, column, spaces, cotangent.shape[1]
    )
    share = cotangent.shape[1] // groups
    dense_block = lax.dynamic_slice_in_dim(delta, lax.axis_index(DP) * share, share, 0)
    cells = samples * groups * planes * spaces * height * length
    step_conv, step_dense = final_steps(
        reduced, dense_block, dense_total, column_order(channels), filters, patch_rows, cells
    )
    return step_conv, step_dense.T


def solution(mesh):
    fine = jax.sharding.Mesh(mesh.devices.reshape(-1, 2, 2, 2, 4), ("z", "xh", "core", "xl", "y"))
    placed = (P(DP, None, SPACE, None, None), P(), P(), P(DP + SPACE, None))
    return jax.shard_map(
        on_device, mesh=fine, in_specs=placed, out_specs=(P(), P(SPACE, DP)), check_vma=False
    )
```

```python
import functools

import jax
import jax.numpy as jnp
from jax import lax
from jax.experimental import pallas as pl
from jax.experimental.pallas import tpu as pltpu
from jax.sharding import PartitionSpec as P


PC = 2
NS_STEPS = 8

LEAK_SLOPE = 0.3
DAMPING = 0.1
KL_BOUND = 0.0001
LEARN_RATE = 0.01
CONTRACT = (((1,), (1,)), ((), ()))
LEADING = (((0,), (0,)), ((), ()))
DP = ("z", "xh", "core")
SPACE = ("xl", "y")
COLUMN = ("z", "core")
PLANE = ("xh", "xl", "y")
F32 = jnp.float32
BF16 = jnp.bfloat16
ROWS_IN = 112


def exchange(x, axes):
    return lax.all_to_all(x, axes, split_axis=0, concat_axis=0, tiled=True)


def gather_from(x, axes, peers):
    return exchange(jnp.broadcast_to(x[None], (peers,) + x.shape), axes)


def turned(x, by):
    return pltpu.roll(x, x.shape[1] - by, 1) if by else x


def conv_kernel_body(
    sizes, vol_ref, before_ref, after_ref, bands_ref,
    pool_ref, sums_ref, gram_ref, shift_a, shift_b, stack_a, stack_b, wide_a, wide_b,
):
    channels, planes, height, length, filters, samples = sizes
    rim = planes + 2
    group = rim * channels * 3
    rows = 3 * group
    half = height * length // PC
    top = planes * filters
    base = top + 16
    step = pl.program_id(0)

    def build(sample, shifted, stacked):
        lane = lax.broadcasted_iota(jnp.int32, (height, length), 1)
        for plane in range(rim):
            for channel in range(channels):
                if plane == 0:
                    value = before_ref[sample, channel, 0]
                elif plane == rim - 1:
                    value = after_ref[sample, channel, 0]
                else:
                    value = vol_ref[sample, channel, plane - 1]
                value = value.astype(F32)
                moved = (
                    jnp.where(lane == 0, 0.0, pltpu.roll(value, 1, 1)),
                    value,
                    jnp.where(lane == length - 1, 0.0, pltpu.roll(value, length - 1, 1)),
                )
                for k in range(3):
                    row = group + (plane * channels + channel) * 3 + k
                    shifted[pl.ds(row, height, stride=group), :] = moved[k]
        for y in range(height):
            stacked[base:, y * length:(y + 1) * length] = shifted[
                y * group:y * group + rows, :
            ].astype(BF16)

    def consume(sample, stacked, wide):
        slot = sample * PC
        pooled = []
        for part in range(PC):
            total = jnp.zeros((filters, 128), F32)
            for piece in range(2):
                first = part * half + piece * (half // 2)
                lanes = slice(first, first + half // 2)
                pre = jnp.dot(bands_ref[...], stacked[base:, lanes], preferred_element_type=F32)
                stacked[0:top, lanes] = jnp.where(pre > 0, 1.0, 0.0).astype(BF16)
                active = jnp.where(pre > 0, pre, LEAK_SLOPE * pre)
                for plane in range(planes):
                    for at in range(0, half // 2, 128):
                        total += active[plane * filters:(plane + 1) * filters, at:at + 128]
            pooled.append(jnp.sum(total, axis=1, keepdims=True))
            lanes = slice(part * half, (part + 1) * half)
            gram = lax.dot_general(
                stacked[:base + group, lanes], stacked[base:, lanes], CONTRACT,
                preferred_element_type=F32,
            )
            wide[part, :, :rows] = gram[:top + 8]
            gram_ref[:, :rows] += gram[base:]
            square = lax.dot_general(
                stacked[:base, lanes], stacked[:top, lanes], CONTRACT,
                preferred_element_type=F32,
            )
            for first, last in ((0, filters), (top, top + 8)):
                patch = jnp.zeros((last - first, 256), F32)
                mask = jnp.zeros((last - first, top), F32)
                for plane in range(planes):
                    at = slice(first, last)
                    if first == 0:
                        at = slice(plane * filters, (plane + 1) * filters)
                    patch += turned(wide[part, at, :], plane * channels * 3)
                    mask += turned(square[at], plane * filters)
                to = slice(0, filters) if first == 0 else slice(filters, filters + 8)
                sums_ref[slot + part, to, :256] = patch
                sums_ref[slot + part, to, 256:] = mask
        for side, y in ((0, height - 1), (1, 0)):
            edge = stacked[base + group:base + 2 * group, y * length:(y + 1) * length]
            gram_ref[:, 256 + side * 128:256 + side * 128 + group] += lax.dot_general(
                edge, edge, CONTRACT, preferred_element_type=F32
            )
        pooled = jnp.concatenate(pooled, axis=0) * (1.0 / (planes * half))
        spot = lax.broadcasted_iota(jnp.int32, pool_ref.shape, 1)
        pool_ref[...] = jnp.where(spot == sample, pooled, pool_ref[...])

    @pl.when(step == 0)
    def _():
        shift_a[...] = jnp.zeros_like(shift_a)
        shift_b[...] = jnp.zeros_like(shift_b)
        ones = jnp.ones((16, height * length), BF16)
        stack_a[top:base, :] = ones
        stack_b[top:base, :] = ones
        gram_ref[...] = jnp.zeros_like(gram_ref)
        pool_ref[...] = jnp.zeros_like(pool_ref)
        build(0, shift_a, stack_a)

    build(2 * step + 1, shift_b, stack_b)
    consume(2 * step, stack_a, wide_a)
    build(jnp.minimum(2 * step + 2, samples - 1), shift_a, stack_a)
    consume(2 * step + 1, stack_b, wide_b)


def conv_sums(volume, before, after, bands, filters):
    samples, channels, planes, height, length = volume.shape
    group = (planes + 2) * channels * 3
    top = planes * filters
    stack = top + 16 + 3 * group
    sizes = (channels, planes, height, length, filters, samples)
    vmem = pl.BlockSpec(memory_space=pltpu.VMEM)
    return pl.pallas_call(
        functools.partial(conv_kernel_body, sizes),
        grid=(samples // 2,),
        in_specs=[vmem] * 4,
        out_specs=[vmem] * 3,
        out_shape=[
            jax.ShapeDtypeStruct((filters * PC, 128), F32),
            jax.ShapeDtypeStruct((samples * PC, filters + 8, 256 + top), F32),
            jax.ShapeDtypeStruct((group, 512), F32),
        ],
        scratch_shapes=[
            pltpu.VMEM(((height + 2) * group, length), F32),
            pltpu.VMEM(((height + 2) * group, length), F32),
            pltpu.VMEM((stack, height * length), BF16),
            pltpu.VMEM((stack, height * length), BF16),
            pltpu.VMEM((PC, top + 8, 256), F32),
            pltpu.VMEM((PC, top + 8, 256), F32),
        ],
        compiler_params=pltpu.CompilerParams(vmem_limit_bytes=24 * 1024 * 1024),
    )(volume, before, after, bands)


def moments_body(
    sizes, pool_ref, sums_ref, gram_ref, weight_ref, cot_ref, own_ref, sent_ref, held, turned_up,
):
    channels, planes, cells, filters, samples = sizes
    inner = channels * 3
    group = (planes + 2) * inner
    wide = 3 * 3 * inner
    part_rows = 3 * inner
    lanes_of = lambda shape: lax.broadcasted_iota(jnp.int32, shape, 1)

    def compact(x):
        lane = lanes_of(x.shape)
        out = jnp.where(lane < part_rows, x, 0.0)
        for j in range(1, 3):
            here = jnp.logical_and(lane >= j * part_rows, lane < (j + 1) * part_rows)
            out = jnp.where(here, turned(x, j * (group - part_rows)), out)
        return out[:, :128]

    cots = cot_ref[...]
    gradient = jnp.zeros((filters, 256), F32)
    moment_out = jnp.zeros((filters, 128), F32)
    cross = jnp.zeros((filters, 128), F32)
    for part in range(PC):
        weight = weight_ref[part * filters:(part + 1) * filters, :]
        grad_down = lax.dot_general(weight, cots, CONTRACT, preferred_element_type=F32)
        weight = jnp.concatenate([weight, jnp.zeros((128 - filters, 128), BF16)], axis=0)
        grad_over = lax.dot_general(cots, weight, CONTRACT, preferred_element_type=F32)
        grad_down = grad_down.astype(BF16).astype(F32)
        grad_over = grad_over.astype(BF16).astype(F32)
        low_down = (LEAK_SLOPE * grad_down).astype(BF16).astype(F32)
        low_over = (LEAK_SLOPE * grad_over).astype(BF16).astype(F32)
        gap_down = grad_down - low_down
        gap_over = grad_over - low_over
        for sample in range(samples):
            slot = sample * PC + part
            gap = gap_down[:, sample:sample + 1]
            low = low_down[:, sample:sample + 1]
            across = gap_over[sample:sample + 1, :]
            gradient += gap * sums_ref[slot, :filters, :256]
            gradient += low * sums_ref[slot, filters:filters + 1, :256]
            moment_out += gap * sums_ref[slot, :filters, 256:] * across
            cross += low * (
                across * sums_ref[slot, filters:filters + 1, 256:]
                + (0.5 * cells) * low_over[sample:sample + 1, :]
            )
    lane = lanes_of(cross.shape)
    cross = jnp.where(lane < filters, cross, 0.0)
    tall = jnp.concatenate([cross, jnp.zeros((128 - filters, 128), F32)], axis=0)
    moment_out = jnp.where(lane < filters, moment_out, 0.0)
    moment_out += cross + jnp.transpose(tall)[:filters]

    blocks = jnp.zeros((part_rows, 512), F32)
    for plane in range(planes):
        start = plane * inner
        blocks += turned(gram_ref[start:start + part_rows, :], start)
    first = compact(blocks[:, :256])
    lane = lanes_of(first.shape)
    second = first + jnp.where(lane < part_rows, blocks[:, 256:384], 0.0)
    third = second - jnp.where(lane < part_rows, blocks[:, 384:], 0.0)
    turned_up[...] = jnp.zeros_like(turned_up)
    turned_up[0:part_rows, :] = first
    turned_up[...] = jnp.transpose(turned_up[...])
    held[...] = jnp.zeros_like(held)
    held[0:part_rows, :] = first
    above = turned_up[part_rows:2 * part_rows, :]
    row = jnp.where(lane < part_rows, above, pltpu.roll(second, part_rows, 1))
    held[part_rows:2 * part_rows, :] = jnp.where(lane < wide, row, 0.0)
    row = jnp.where(
        lane < 2 * part_rows,
        pltpu.roll(above, part_rows, 1),
        pltpu.roll(third, 2 * part_rows, 1),
    )
    row = jnp.where(lane < part_rows, turned_up[2 * part_rows:wide, :], row)
    held[2 * part_rows:wide, :] = jnp.where(lane < wide, row, 0.0)
    moment_in = held[...]
    gradient = compact(gradient)
    packed = jnp.concatenate(
        [
            moment_in[:, :64],
            moment_in[64:, 64:],
            gradient[:, :64],
            gradient[:, 64:],
            moment_out[:, :64],
        ],
        axis=0,
    )
    groups = sent_ref.shape[0]
    share = packed.shape[0] // groups
    sent_ref[:, 0:share, :] = in_halves(packed).reshape(groups, share, 128)
    feats = jnp.transpose(pool_ref[...])[:samples]
    own = own_ref[...].astype(F32)
    own = jnp.concatenate([own[:, :64], own[:, 64:], jnp.zeros((samples - 2, 64), F32)], axis=0)
    both = jnp.concatenate([feats, own], axis=1).astype(BF16)
    sent_ref[:, share:, :] = jnp.broadcast_to(both[None], (groups, samples, 128))


def conv_moments(sizes, sums, weight, cot_group, own, groups):
    samples = sizes[-1]
    rows = 256 // groups + samples
    vmem = pl.BlockSpec(memory_space=pltpu.VMEM)
    return pl.pallas_call(
        functools.partial(moments_body, sizes),
        in_specs=[vmem] * 6,
        out_specs=vmem,
        out_shape=jax.ShapeDtypeStruct((groups, rows, 128), BF16),
        scratch_shapes=[pltpu.VMEM((ROWS_IN, 128), F32), pltpu.VMEM((128, 128), F32)],
        compiler_params=pltpu.CompilerParams(vmem_limit_bytes=16 * 1024 * 1024),
    )(*sums, weight, cot_group, own)


def in_halves(x):
    high = x.astype(BF16)
    low = (x - high.astype(F32)).astype(BF16)
    return jnp.concatenate([high, low], axis=1)


def from_halves(x):
    wide = x.astype(F32)
    return wide[..., :64] + wide[..., 64:]


def middle_body(core_ref, got_ref, sent_ref):
    depth, cores, rows, _ = got_ref.shape
    share = rows - 8
    chunk = jnp.sum(from_halves(got_ref[:, 0, 0:share, :]), axis=0)
    for core in range(1, cores):
        chunk += jnp.sum(from_halves(got_ref[:, core, 0:share, :]), axis=0)
    wide = got_ref[:, core_ref[0], share:, :].astype(F32)
    pairs = depth // 2
    feats = wide[:, :, :64]
    feats = jnp.concatenate([feats[:pairs], feats[pairs:]], axis=2).reshape(pairs * 8, 128)
    cots = jnp.concatenate([wide[:, 0, 64:], wide[:, 1, 64:]], axis=1)
    feats = feats.astype(BF16)
    cots = cots.astype(BF16)
    chunk = in_halves(chunk)
    for peer in range(sent_ref.shape[0]):
        sent_ref[peer, 0:share, :] = chunk
        sent_ref[peer, share:share + pairs * 8, :] = feats
        sent_ref[peer, share + pairs * 8:, :] = cots


def middle(core, got, peers):
    depth, _, rows, lanes = got.shape
    vmem = pl.BlockSpec(memory_space=pltpu.VMEM)
    return pl.pallas_call(
        middle_body,
        in_specs=[pl.BlockSpec(memory_space=pltpu.SMEM), vmem],
        out_specs=vmem,
        out_shape=jax.ShapeDtypeStruct((peers, rows - 8 + depth * 5, lanes), BF16),
        compiler_params=pltpu.CompilerParams(vmem_limit_bytes=8 * 1024 * 1024),
    )(core, got)


def spread_body(got_ref, sent_ref):
    chunk = jnp.sum(from_halves(got_ref[...]), axis=0)
    sent_ref[...] = jnp.broadcast_to(in_halves(chunk)[None], sent_ref.shape)


def spread(got, groups):
    peers, _, lanes = got.shape
    share = 256 // groups
    return pl.pallas_call(
        spread_body,
        grid=(1,),
        in_specs=[pl.BlockSpec((peers, share, lanes), lambda i: (0, 0, 0))],
        out_specs=pl.BlockSpec((groups, share, lanes), lambda i: (0, 0, 0)),
        out_shape=jax.ShapeDtypeStruct((groups, share, lanes), BF16),
        compiler_params=pltpu.CompilerParams(vmem_limit_bytes=8 * 1024 * 1024),
    )(got)


def parts_of(x):
    high = x.astype(BF16)
    return high, (x - high.astype(F32)).astype(BF16)


def split_dot(a, b):
    a_high, a_low = parts_of(a)
    b_high, b_low = parts_of(b)
    return jnp.dot(
        jnp.concatenate([a_high, a_high, a_low], axis=1),
        jnp.concatenate([b_high, b_low, b_high], axis=0),
        preferred_element_type=F32,
    )


def square_and_apply(left, held, last):
    order = left.shape[1]
    if last:
        both = held
    else:
        both = jnp.concatenate([left, held], axis=1)
    if both.shape[0] < order:
        rest = jnp.zeros((order - both.shape[0], both.shape[1]), F32)
        both = jnp.concatenate([both, rest], axis=0)
    product = split_dot(left, both)
    if last:
        return left, held + product
    return product[:, :order], held + product[:, order:]


def square_and_extend(inverse, right, last):
    if last:
        return inverse + split_dot(inverse, right), right
    order = right.shape[0]
    product = split_dot(jnp.concatenate([inverse, right], axis=0), right)
    return inverse + product[:order], product[order:]


def two_sided(left, held, right):
    order = right.shape[0]
    inverse = jnp.where(unit(order), 1.0, 0.0) + right
    right = split_dot(right, right)
    for step in range(NS_STEPS):
        left, held = square_and_apply(left, held, step == NS_STEPS - 1)
        if step > 0:
            inverse, right = square_and_extend(inverse, right, step == NS_STEPS - 1)
    return split_dot(held, inverse)


def unit(order):
    row = lax.broadcasted_iota(jnp.int32, (order, order), 0)
    column = lax.broadcasted_iota(jnp.int32, (order, order), 1)
    return row == column


def scalar_sum(x):
    return jnp.sum(jnp.sum(x, axis=0, keepdims=True), axis=1, keepdims=True)


def residual(factor, order):
    size = factor.shape[0]
    eye = unit(size)
    trace = scalar_sum(jnp.where(eye, factor, 0.0))
    damping = DAMPING * trace / order
    sums = jnp.sum(jnp.abs(factor), axis=0, keepdims=True) + damping
    bound = jnp.max(sums, axis=1, keepdims=True)
    inside = lax.broadcasted_iota(jnp.int32, (size, size), 0) < order
    start = jnp.where(jnp.logical_and(eye, inside), 1.0 - damping / bound, 0.0)
    return start - factor / bound, bound


def dense_kernel_body(
    depth, spaces, place_ref, own_ref, other_ref, delta_ref, whole, cots,
):
    parts = own_ref.shape[0] // spaces
    width = 64
    block = depth * 8
    half = block // 2
    share = own_ref.shape[1] - other_ref.shape[1]
    count = parts * 2 * block
    lower = place_ref[1] == 0

    def both_cores(index):
        own = own_ref[index].astype(F32)[share:]
        other = other_ref[index].astype(F32)
        return jnp.where(lower, own, other), jnp.where(lower, other, own)

    def slab_of(index):
        pieces = []
        for part in range(parts):
            for rows in both_cores(part * spaces + index):
                pieces += [rows[:half, :width], rows[:half, width:]]
        return jnp.concatenate(pieces, axis=0)

    for slab in range(0, spaces, 2):
        pair = jnp.concatenate([slab_of(slab), slab_of(slab + 1)], axis=1)
        whole[:, slab * width:(slab + 2) * width] = pair.astype(BF16)
    for part in range(parts):
        for slab in range(spaces):
            for core, rows in enumerate(both_cores(part * spaces + slab)):
                first = (part * 2 + core) * block + slab
                cots[pl.ds(first, depth, stride=spaces), :] = rows[half:]
    cot_wide = cots[...]
    cot = cot_wide.astype(BF16)
    feats = whole[...]
    scale = 1.0 / count
    gram = lax.dot_general(feats, feats, CONTRACT, preferred_element_type=F32) * scale
    dense_in = lax.dot_general(feats, feats, LEADING, preferred_element_type=F32) * scale
    dense_out = lax.dot_general(cot, cot, LEADING, preferred_element_type=F32) * scale
    order = spaces * width
    eye = unit(count)
    damping = DAMPING * scalar_sum(jnp.where(eye, gram, 0.0)) / order
    sums = jnp.sum(jnp.abs(dense_in), axis=0, keepdims=True) + damping
    bound = jnp.max(sums, axis=1, keepdims=True)
    left = jnp.where(eye, 1.0 - damping / bound, 0.0) - gram / bound
    right, bound_out = residual(dense_out, dense_out.shape[0])
    held = two_sided(left, cot_wide * (scale / bound / bound_out), right)
    total = scalar_sum(held * split_dot(gram, cot_wide))
    mine = slab_of(place_ref[0])
    source = lax.broadcasted_iota(jnp.int32, (width, width), 0)
    target = lax.broadcasted_iota(jnp.int32, (width, width), 1)
    spot = (target % PC) * (width // PC) + target // PC
    pick = jnp.where(source == spot, 1.0, 0.0).astype(BF16)
    mine = jnp.dot(mine.astype(BF16), pick, preferred_element_type=F32).astype(BF16)
    high, low = parts_of(held)
    outputs = cot_wide.shape[1]
    delta_ref[outputs:, :] = jnp.broadcast_to(total, (8, width))
    delta_ref[0:outputs, :] = lax.dot_general(
        jnp.concatenate([high, low], axis=0),
        jnp.concatenate([mine, mine], axis=0),
        LEADING,
        preferred_element_type=F32,
    )


def dense_delta(place, own, other, depth, spaces, outputs):
    count = depth * 16 * (own.shape[0] // spaces)
    vmem = pl.BlockSpec(memory_space=pltpu.VMEM)
    return pl.pallas_call(
        functools.partial(dense_kernel_body, depth, spaces),
        in_specs=[pl.BlockSpec(memory_space=pltpu.SMEM), vmem, vmem],
        out_specs=vmem,
        out_shape=jax.ShapeDtypeStruct((outputs + 8, 64), F32),
        scratch_shapes=[
            pltpu.VMEM((count, spaces * 64), BF16),
            pltpu.VMEM((count, outputs), F32),
        ],
        compiler_params=pltpu.CompilerParams(vmem_limit_bytes=48 * 1024 * 1024),
    )(place, own, other)


def final_kernel_body(
    filters, patch_rows, cells, place_ref, got_ref, delta_ref, order_ref,
    step_conv_ref, step_dense_ref,
):
    scale = 1.0 / cells
    moments = from_halves(got_ref[...]).reshape(-1, 64)
    pad = jnp.zeros((128 - ROWS_IN, 64), F32)
    lower = jnp.concatenate([moments[64:ROWS_IN], pad], axis=0)
    corner = jnp.concatenate([moments[ROWS_IN:2 * ROWS_IN - 64], pad], axis=0)
    upper = jnp.concatenate([moments[0:64], jnp.transpose(lower)], axis=1)
    lower = jnp.concatenate([lower, corner], axis=1)
    conv_in = jnp.concatenate([upper, lower], axis=0) * scale
    first = 2 * ROWS_IN - 64
    conv_grad = jnp.concatenate(
        [moments[first:first + filters], moments[first + filters:first + 2 * filters]],
        axis=1,
    ) * scale
    conv_out = moments[first + 2 * filters:first + 3 * filters]
    conv_out = jnp.concatenate([conv_out, jnp.zeros((filters, 64), F32)], axis=1)
    conv_out = jnp.concatenate([conv_out, jnp.zeros((128 - filters, 128), F32)], axis=0) * scale
    right, bound_in = residual(conv_in, patch_rows)
    left, bound_out = residual(conv_out, filters)
    held = two_sided(left[0:filters], conv_grad / bound_in / bound_out, right)
    total = scalar_sum(held * conv_grad) + delta_ref[delta_ref.shape[0] - 8:, 0:1][0:1]
    scaling = jnp.minimum(1.0, jnp.sqrt(KL_BOUND / (LEARN_RATE * LEARN_RATE * total)))
    moved = split_dot(held, order_ref[...])
    step_conv_ref[...] = scaling * moved[:, 0:patch_rows]
    first = place_ref[2] // 2 * 8
    window = delta_ref[pl.ds(pl.multiple_of(first, 8), 8), :]
    mine = jnp.where(place_ref[2] % 2 == 0, window[0:4], window[4:8])
    step_dense_ref[...] = scaling * mine


def final_steps(place, moments, delta, order, filters, patch_rows, cells):
    vmem = pl.BlockSpec(memory_space=pltpu.VMEM)
    return pl.pallas_call(
        functools.partial(final_kernel_body, filters, patch_rows, cells),
        in_specs=[pl.BlockSpec(memory_space=pltpu.SMEM)] + [vmem] * 3,
        out_specs=[vmem] * 2,
        out_shape=[
            jax.ShapeDtypeStruct((filters, patch_rows), F32),
            jax.ShapeDtypeStruct((4, delta.shape[1]), F32),
        ],
        compiler_params=pltpu.CompilerParams(vmem_limit_bytes=32 * 1024 * 1024),
    )(place, moments, delta, order)


def column_order(channels):
    row = lax.broadcasted_iota(jnp.int32, (128, 128), 0)
    column = lax.broadcasted_iota(jnp.int32, (128, 128), 1)
    channel, i, j, k = column // 27, column // 9 % 3, column // 3 % 3, column % 3
    source = ((j * 3 + i) * channels + channel) * 3 + k
    return jnp.where(jnp.logical_and(row == source, column < 27 * channels), 1.0, 0.0)


def on_device(volume, conv_kernel, dense_weight, cotangent):
    spaces = lax.axis_size(SPACE)
    groups = lax.axis_size(DP)
    column = lax.axis_size(COLUMN)
    samples, channels, planes, height, length = volume.shape
    filters, patch_rows = conv_kernel.shape
    slab = filters * PC

    up = [(i, i + 1) for i in range(spaces - 1)]
    down = [(j, i) for i, j in up]
    before = lax.ppermute(volume[:, :, planes - 1:], SPACE, up)
    after = lax.ppermute(volume[:, :, :1], SPACE, down)
    cot_group = gather_from(cotangent[0], SPACE, spaces)

    mixed = conv_kernel.reshape(filters, channels, 3, 3, 3).transpose(0, 3, 2, 1, 4)
    mixed = mixed.reshape(filters, 3, channels * 9)
    inner = channels * 3
    spare = (planes - 1) * inner
    bands = jnp.concatenate(
        [
            jnp.pad(mixed, ((0, 0), (0, 0), (p * inner, spare - p * inner)))
            for p in range(planes)
        ],
        axis=0,
    ).reshape(planes * filters, -1)
    place = lax.axis_index(SPACE)
    weight = lax.dynamic_slice_in_dim(dense_weight, place * slab, slab, 0)
    weight = weight.reshape(filters, PC, -1).transpose(1, 0, 2).reshape(slab, -1)

    sums = conv_sums(volume, before, after, bands, filters)
    sizes = (channels, planes, planes * height * length // PC, filters, samples)
    sent = conv_moments(sizes, sums, weight, cot_group, cotangent, column)
    peers = spaces * groups // column
    core = lax.axis_index("core")
    got = exchange(sent, COLUMN).reshape(column // 2, 2, -1, 128)
    got = exchange(middle(core.reshape(1), got, peers), PLANE)
    reduced = exchange(spread(got, column), COLUMN)
    other = lax.ppermute(got[:, 256 // column:], "core", [(0, 1), (1, 0)])
    places = jnp.stack([place, core, lax.axis_index(DP)])
    delta = dense_delta(places, got, other, column // 2, spaces, cotangent.shape[1])
    cells = samples * groups * planes * spaces * height * length
    step_conv, step_dense = final_steps(
        places, reduced, delta, column_order(channels), filters, patch_rows, cells
    )
    return step_conv, step_dense.T


def solution(mesh):
    fine = jax.sharding.Mesh(mesh.devices.reshape(-1, 2, 2, 2, 4), ("z", "xh", "core", "xl", "y"))
    placed = (P(DP, None, SPACE, None, None), P(), P(), P(DP + SPACE, None))
    return jax.shard_map(
        on_device, mesh=fine, in_specs=placed, out_specs=(P(), P(SPACE, DP)), check_vma=False
    )
```

```python
import functools

import jax
import jax.numpy as jnp
from jax import lax
from jax.experimental import pallas as pl
from jax.experimental.pallas import tpu as pltpu
from jax.sharding import PartitionSpec as P


PC = 2
NS_STEPS = 8

LEAK_SLOPE = 0.3
DAMPING = 0.1
KL_BOUND = 0.0001
LEARN_RATE = 0.01
CONTRACT = (((1,), (1,)), ((), ()))
LEADING = (((0,), (0,)), ((), ()))
DP = ("z", "xh", "core")
SPACE = ("xl", "y")
COLUMN = ("z", "core")
PLANE = ("xh", "xl", "y")
F32 = jnp.float32
BF16 = jnp.bfloat16
ROWS_IN = 112


def exchange(x, axes):
    return lax.all_to_all(x, axes, split_axis=0, concat_axis=0, tiled=True)


def gather_from(x, axes, peers):
    return exchange(jnp.broadcast_to(x[None], (peers,) + x.shape), axes)


def turned(x, by):
    return pltpu.roll(x, x.shape[1] - by, 1) if by else x


def conv_kernel_body(
    sizes, vol_ref, before_ref, after_ref, kernel_ref, pool_ref, sums_ref, gram_ref,
    shift_a, shift_b, stack_a, stack_b, wide_a, wide_b, edges, bands_ref, taken, done,
):
    channels, planes, height, length, filters, samples = sizes
    rim = planes + 2
    group = rim * channels * 3
    rows = 3 * group
    half = height * length // PC
    top = planes * filters
    base = top + 16
    step = pl.program_id(0)

    def build(sample, shifted, stacked):
        lane = lax.broadcasted_iota(jnp.int32, (height, length), 1)
        for plane in range(rim):
            for channel in range(channels):
                if plane == 0:
                    value = before_ref[sample, channel, 0]
                elif plane == rim - 1:
                    value = after_ref[sample, channel, 0]
                else:
                    value = vol_ref[sample, channel, plane - 1]
                value = value.astype(F32)
                moved = (
                    jnp.where(lane == 0, 0.0, pltpu.roll(value, 1, 1)),
                    value,
                    jnp.where(lane == length - 1, 0.0, pltpu.roll(value, length - 1, 1)),
                )
                for k in range(3):
                    row = group + (plane * channels + channel) * 3 + k
                    shifted[pl.ds(row, height, stride=group), :] = moved[k]
        for y in range(height):
            stacked[base:, y * length:(y + 1) * length] = shifted[
                y * group:y * group + rows, :
            ].astype(BF16)

    def consume(sample, stacked, wide):
        slot = sample * PC
        pooled = []
        for part in range(PC):
            total = jnp.zeros((filters, 128), F32)
            for piece in range(2):
                first = part * half + piece * (half // 2)
                lanes = slice(first, first + half // 2)
                pre = jnp.dot(bands_ref[...], stacked[base:, lanes], preferred_element_type=F32)
                stacked[0:top, lanes] = jnp.where(pre > 0, 1.0, 0.0).astype(BF16)
                active = jnp.where(pre > 0, pre, LEAK_SLOPE * pre)
                for plane in range(planes):
                    for at in range(0, half // 2, 128):
                        total += active[plane * filters:(plane + 1) * filters, at:at + 128]
            pooled.append(jnp.sum(total, axis=1, keepdims=True))
            lanes = slice(part * half, (part + 1) * half)
            gram = lax.dot_general(
                stacked[:base + group, lanes], stacked[base:, lanes], CONTRACT,
                preferred_element_type=F32,
            )
            wide[part, :, :rows] = gram[:top + 8]
            gram_ref[:, :rows] += gram[base:]
            square = lax.dot_general(
                stacked[:base, lanes], stacked[:top, lanes], CONTRACT,
                preferred_element_type=F32,
            )
            for first, last in ((0, filters), (top, top + 8)):
                patch = jnp.zeros((last - first, 256), F32)
                mask = jnp.zeros((last - first, top), F32)
                for plane in range(planes):
                    at = slice(first, last)
                    if first == 0:
                        at = slice(plane * filters, (plane + 1) * filters)
                    patch += turned(wide[part, at, :], plane * channels * 3)
                    mask += turned(square[at], plane * filters)
                to = slice(0, filters) if first == 0 else slice(filters, filters + 8)
                sums_ref[slot + part, to, :256] = patch
                sums_ref[slot + part, to, 256:] = mask
        spot = pl.ds(pl.multiple_of(sample * length, length), length)
        for side, y in ((0, height - 1), (1, 0)):
            edges[side, :, spot] = stacked[
                base + group:base + 2 * group, y * length:(y + 1) * length
            ]
        pooled = jnp.concatenate(pooled, axis=0) * (1.0 / (planes * half))
        spot = lax.broadcasted_iota(jnp.int32, pool_ref.shape, 1)
        pool_ref[...] = jnp.where(spot == sample, pooled, pool_ref[...])

    @pl.when(step == 0)
    def _():
        fetch = pltpu.make_async_copy(kernel_ref, taken, done)
        fetch.start()
        blank = jnp.zeros((group, length), F32)
        for shifted in (shift_a, shift_b):
            shifted[0:group, :] = blank
            shifted[(height + 1) * group:, :] = blank
        ones = jnp.ones((16, height * length), BF16)
        stack_a[top:base, :] = ones
        stack_b[top:base, :] = ones
        gram_ref[...] = jnp.zeros_like(gram_ref)
        pool_ref[...] = jnp.zeros_like(pool_ref)
        build(0, shift_a, stack_a)
        at = lax.broadcasted_iota(jnp.int32, (1, 256), 1)
        j, rest = at // group, at % group
        inner = channels * 3
        i, channel, k = rest // inner, rest % inner // 3, rest % 3
        used = jnp.logical_and(rest < 3 * inner, at < rows)
        source = jnp.where(used, channel * 27 + i * 9 + j * 3 + k, -1)
        row = lax.broadcasted_iota(jnp.int32, (kernel_ref.shape[1], 256), 0)
        pick = jnp.where(row == source, 1.0, 0.0).astype(BF16)
        fetch.wait()
        band = jnp.dot(taken[...], pick, preferred_element_type=F32)
        bands_ref[...] = jnp.concatenate(
            [band] + [pltpu.roll(band, plane * inner, 1) for plane in range(1, planes)], axis=0
        )[:, :rows].astype(BF16)

    build(2 * step + 1, shift_b, stack_b)
    consume(2 * step, stack_a, wide_a)
    build(jnp.minimum(2 * step + 2, samples - 1), shift_a, stack_a)
    consume(2 * step + 1, stack_b, wide_b)

    @pl.when(step == pl.num_programs(0) - 1)
    def _():
        for side in range(2):
            gram_ref[:, 256 + side * 128:256 + side * 128 + group] = lax.dot_general(
                edges[side], edges[side], CONTRACT, preferred_element_type=F32
            )


def conv_sums(volume, before, after, conv_kernel):
    samples, channels, planes, height, length = volume.shape
    filters = conv_kernel.shape[0]
    group = (planes + 2) * channels * 3
    top = planes * filters
    stack = top + 16 + 3 * group
    sizes = (channels, planes, height, length, filters, samples)
    vmem = pl.BlockSpec(memory_space=pltpu.VMEM)
    return pl.pallas_call(
        functools.partial(conv_kernel_body, sizes),
        grid=(samples // 2,),
        in_specs=[vmem] * 3 + [pl.BlockSpec(memory_space=pltpu.HBM)],
        out_specs=[vmem] * 3,
        out_shape=[
            jax.ShapeDtypeStruct((filters * PC, 128), F32),
            jax.ShapeDtypeStruct((samples * PC, filters + 8, 256 + top), F32),
            jax.ShapeDtypeStruct((group, 512), F32),
        ],
        scratch_shapes=[
            pltpu.VMEM(((height + 2) * group, length), F32),
            pltpu.VMEM(((height + 2) * group, length), F32),
            pltpu.VMEM((stack, height * length), BF16),
            pltpu.VMEM((stack, height * length), BF16),
            pltpu.VMEM((PC, top + 8, 256), F32),
            pltpu.VMEM((PC, top + 8, 256), F32),
            pltpu.VMEM((2, group, samples * length), BF16),
            pltpu.VMEM((top, 3 * group), BF16),
            pltpu.VMEM(conv_kernel.shape, BF16),
            pltpu.SemaphoreType.DMA(()),
        ],
        compiler_params=pltpu.CompilerParams(vmem_limit_bytes=24 * 1024 * 1024),
    )(volume, before, after, conv_kernel)


def moments_body(
    sizes, pool_ref, sums_ref, gram_ref, weight_ref, cot_ref, own_ref, sent_ref, held, turned_up,
):
    channels, planes, cells, filters, samples = sizes
    inner = channels * 3
    group = (planes + 2) * inner
    wide = 3 * 3 * inner
    part_rows = 3 * inner
    lanes_of = lambda shape: lax.broadcasted_iota(jnp.int32, shape, 1)

    def compact(x):
        lane = lanes_of(x.shape)
        out = jnp.where(lane < part_rows, x, 0.0)
        for j in range(1, 3):
            here = jnp.logical_and(lane >= j * part_rows, lane < (j + 1) * part_rows)
            out = jnp.where(here, turned(x, j * (group - part_rows)), out)
        return out[:, :128]

    cots = cot_ref[...]
    gradient = jnp.zeros((filters, 256), F32)
    moment_out = jnp.zeros((filters, 128), F32)
    cross = jnp.zeros((filters, 128), F32)
    for part in range(PC):
        weight = weight_ref[part * filters:(part + 1) * filters, :]
        grad_down = lax.dot_general(weight, cots, CONTRACT, preferred_element_type=F32)
        weight = jnp.concatenate([weight, jnp.zeros((128 - filters, 128), BF16)], axis=0)
        grad_over = lax.dot_general(cots, weight, CONTRACT, preferred_element_type=F32)
        grad_down = grad_down.astype(BF16).astype(F32)
        grad_over = grad_over.astype(BF16).astype(F32)
        low_down = (LEAK_SLOPE * grad_down).astype(BF16).astype(F32)
        low_over = (LEAK_SLOPE * grad_over).astype(BF16).astype(F32)
        gap_down = grad_down - low_down
        gap_over = grad_over - low_over
        for sample in range(samples):
            slot = sample * PC + part
            gap = gap_down[:, sample:sample + 1]
            low = low_down[:, sample:sample + 1]
            across = gap_over[sample:sample + 1, :]
            gradient += gap * sums_ref[slot, :filters, :256]
            gradient += low * sums_ref[slot, filters:filters + 1, :256]
            moment_out += gap * sums_ref[slot, :filters, 256:] * across
            cross += low * (
                across * sums_ref[slot, filters:filters + 1, 256:]
                + (0.5 * cells) * low_over[sample:sample + 1, :]
            )
    lane = lanes_of(cross.shape)
    cross = jnp.where(lane < filters, cross, 0.0)
    tall = jnp.concatenate([cross, jnp.zeros((128 - filters, 128), F32)], axis=0)
    moment_out = jnp.where(lane < filters, moment_out, 0.0)
    moment_out += cross + jnp.transpose(tall)[:filters]

    blocks = jnp.zeros((part_rows, 512), F32)
    for plane in range(planes):
        start = plane * inner
        blocks += turned(gram_ref[start:start + part_rows, :], start)
    first = compact(blocks[:, :256])
    lane = lanes_of(first.shape)
    second = first + jnp.where(lane < part_rows, blocks[:, 256:384], 0.0)
    third = second - jnp.where(lane < part_rows, blocks[:, 384:], 0.0)
    turned_up[...] = jnp.zeros_like(turned_up)
    turned_up[0:part_rows, :] = first
    turned_up[...] = jnp.transpose(turned_up[...])
    held[...] = jnp.zeros_like(held)
    held[0:part_rows, :] = first
    above = turned_up[part_rows:2 * part_rows, :]
    row = jnp.where(lane < part_rows, above, pltpu.roll(second, part_rows, 1))
    held[part_rows:2 * part_rows, :] = jnp.where(lane < wide, row, 0.0)
    row = jnp.where(
        lane < 2 * part_rows,
        pltpu.roll(above, part_rows, 1),
        pltpu.roll(third, 2 * part_rows, 1),
    )
    row = jnp.where(lane < part_rows, turned_up[2 * part_rows:wide, :], row)
    held[2 * part_rows:wide, :] = jnp.where(lane < wide, row, 0.0)
    moment_in = held[...]
    gradient = compact(gradient)
    packed = jnp.concatenate(
        [
            moment_in[:, :64],
            moment_in[64:, 64:],
            gradient[:, :64],
            gradient[:, 64:],
            moment_out[:, :64],
        ],
        axis=0,
    )
    groups = sent_ref.shape[0]
    share = packed.shape[0] // groups
    sent_ref[:, 0:share, :] = in_halves(packed).reshape(groups, share, 128)
    feats = jnp.transpose(pool_ref[...])[:samples]
    own = own_ref[...].astype(F32)
    own = jnp.concatenate([own[:, :64], own[:, 64:], jnp.zeros((samples - 2, 64), F32)], axis=0)
    both = jnp.concatenate([feats, own], axis=1).astype(BF16)
    sent_ref[:, share:, :] = jnp.broadcast_to(both[None], (groups, samples, 128))


def conv_moments(sizes, sums, weight, cot_group, own, groups):
    samples = sizes[-1]
    rows = 256 // groups + samples
    vmem = pl.BlockSpec(memory_space=pltpu.VMEM)
    return pl.pallas_call(
        functools.partial(moments_body, sizes),
        in_specs=[vmem] * 6,
        out_specs=vmem,
        out_shape=jax.ShapeDtypeStruct((groups, rows, 128), BF16),
        scratch_shapes=[pltpu.VMEM((ROWS_IN, 128), F32), pltpu.VMEM((128, 128), F32)],
        compiler_params=pltpu.CompilerParams(vmem_limit_bytes=16 * 1024 * 1024),
    )(*sums, weight, cot_group, own)


def in_halves(x):
    high = x.astype(BF16)
    low = (x - high.astype(F32)).astype(BF16)
    return jnp.concatenate([high, low], axis=1)


def from_halves(x):
    wide = x.astype(F32)
    return wide[..., :64] + wide[..., 64:]


def middle_body(core_ref, got_ref, sent_ref):
    depth, cores, rows, _ = got_ref.shape
    share = rows - 8
    chunk = jnp.sum(from_halves(got_ref[:, 0, 0:share, :]), axis=0)
    for core in range(1, cores):
        chunk += jnp.sum(from_halves(got_ref[:, core, 0:share, :]), axis=0)
    wide = got_ref[:, core_ref[0], share:, :].astype(F32)
    pairs = depth // 2
    feats = wide[:, :, :64]
    feats = jnp.concatenate([feats[:pairs], feats[pairs:]], axis=2).reshape(pairs * 8, 128)
    cots = jnp.concatenate([wide[:, 0, 64:], wide[:, 1, 64:]], axis=1)
    feats = feats.astype(BF16)
    cots = cots.astype(BF16)
    chunk = in_halves(chunk)
    for peer in range(sent_ref.shape[0]):
        sent_ref[peer, 0:share, :] = chunk
        sent_ref[peer, share:share + pairs * 8, :] = feats
        sent_ref[peer, share + pairs * 8:, :] = cots


def middle(core, got, peers):
    depth, _, rows, lanes = got.shape
    vmem = pl.BlockSpec(memory_space=pltpu.VMEM)
    return pl.pallas_call(
        middle_body,
        in_specs=[pl.BlockSpec(memory_space=pltpu.SMEM), vmem],
        out_specs=vmem,
        out_shape=jax.ShapeDtypeStruct((peers, rows - 8 + depth * 5, lanes), BF16),
        compiler_params=pltpu.CompilerParams(vmem_limit_bytes=8 * 1024 * 1024),
    )(core, got)


def spread_body(got_ref, sent_ref):
    chunk = jnp.sum(from_halves(got_ref[...]), axis=0)
    sent_ref[...] = jnp.broadcast_to(in_halves(chunk)[None], sent_ref.shape)


def spread(got, groups):
    peers, _, lanes = got.shape
    share = 256 // groups
    return pl.pallas_call(
        spread_body,
        grid=(1,),
        in_specs=[pl.BlockSpec((peers, share, lanes), lambda i: (0, 0, 0))],
        out_specs=pl.BlockSpec((groups, share, lanes), lambda i: (0, 0, 0)),
        out_shape=jax.ShapeDtypeStruct((groups, share, lanes), BF16),
        compiler_params=pltpu.CompilerParams(vmem_limit_bytes=8 * 1024 * 1024),
    )(got)


def parts_of(x):
    high = x.astype(BF16)
    return high, (x - high.astype(F32)).astype(BF16)


def split_dot(a, b):
    a_high, a_low = parts_of(a)
    b_high, b_low = parts_of(b)
    return jnp.dot(
        jnp.concatenate([a_high, a_high, a_low], axis=1),
        jnp.concatenate([b_high, b_low, b_high], axis=0),
        preferred_element_type=F32,
    )


def square_and_apply(left, held, last):
    order = left.shape[1]
    if last:
        both = held
    else:
        both = jnp.concatenate([left, held], axis=1)
    if both.shape[0] < order:
        rest = jnp.zeros((order - both.shape[0], both.shape[1]), F32)
        both = jnp.concatenate([both, rest], axis=0)
    product = split_dot(left, both)
    if last:
        return left, held + product
    return product[:, :order], held + product[:, order:]


def square_and_extend(inverse, right, last):
    if last:
        return inverse + split_dot(inverse, right), right
    order = right.shape[0]
    product = split_dot(jnp.concatenate([inverse, right], axis=0), right)
    return inverse + product[:order], product[order:]


def two_sided(left, held, right):
    order = right.shape[0]
    inverse = jnp.where(unit(order), 1.0, 0.0) + right
    right = split_dot(right, right)
    for step in range(NS_STEPS):
        left, held = square_and_apply(left, held, step == NS_STEPS - 1)
        if step > 0:
            inverse, right = square_and_extend(inverse, right, step == NS_STEPS - 1)
    return split_dot(held, inverse)


def unit(order):
    row = lax.broadcasted_iota(jnp.int32, (order, order), 0)
    column = lax.broadcasted_iota(jnp.int32, (order, order), 1)
    return row == column


def scalar_sum(x):
    return jnp.sum(jnp.sum(x, axis=0, keepdims=True), axis=1, keepdims=True)


def residual(factor, order):
    size = factor.shape[0]
    eye = unit(size)
    trace = scalar_sum(jnp.where(eye, factor, 0.0))
    damping = DAMPING * trace / order
    sums = jnp.sum(jnp.abs(factor), axis=0, keepdims=True) + damping
    bound = jnp.max(sums, axis=1, keepdims=True)
    inside = lax.broadcasted_iota(jnp.int32, (size, size), 0) < order
    start = jnp.where(jnp.logical_and(eye, inside), 1.0 - damping / bound, 0.0)
    return start - factor / bound, bound


def dense_kernel_body(
    depth, spaces, place_ref, own_ref, other_ref, delta_ref, whole, cots, every,
):
    parts = own_ref.shape[0] // spaces
    width = 64
    block = depth * 8
    half = block // 2
    share = own_ref.shape[1] - other_ref.shape[1]
    count = parts * 2 * block
    lower = place_ref[1] == 0

    def both_cores(index):
        own = own_ref[index].astype(F32)[share:]
        other = other_ref[index].astype(F32)
        return jnp.where(lower, own, other), jnp.where(lower, other, own)

    def slab_of(index):
        pieces = []
        for part in range(parts):
            for rows in both_cores(part * spaces + index):
                pieces += [rows[:half, :width], rows[:half, width:]]
        return jnp.concatenate(pieces, axis=0)

    for slab in range(0, spaces, 2):
        pair = jnp.concatenate([slab_of(slab), slab_of(slab + 1)], axis=1)
        whole[:, slab * width:(slab + 2) * width] = pair.astype(BF16)
    for part in range(parts):
        for slab in range(spaces):
            for core, rows in enumerate(both_cores(part * spaces + slab)):
                first = (part * 2 + core) * block + slab
                cots[pl.ds(first, depth, stride=spaces), :] = rows[half:]
    cot_wide = cots[...]
    cot = cot_wide.astype(BF16)
    feats = whole[...]
    scale = 1.0 / count
    gram = lax.dot_general(feats, feats, CONTRACT, preferred_element_type=F32) * scale
    dense_in = lax.dot_general(feats, feats, LEADING, preferred_element_type=F32) * scale
    dense_out = lax.dot_general(cot, cot, LEADING, preferred_element_type=F32) * scale
    order = spaces * width
    eye = unit(count)
    damping = DAMPING * scalar_sum(jnp.where(eye, gram, 0.0)) / order
    sums = jnp.sum(jnp.abs(dense_in), axis=0, keepdims=True) + damping
    bound = jnp.max(sums, axis=1, keepdims=True)
    left = jnp.where(eye, 1.0 - damping / bound, 0.0) - gram / bound
    right, bound_out = residual(dense_out, dense_out.shape[0])
    held = two_sided(left, cot_wide * (scale / bound / bound_out), right)
    total = scalar_sum(held * split_dot(gram, cot_wide))
    mine = slab_of(place_ref[0])
    source = lax.broadcasted_iota(jnp.int32, (width, width), 0)
    target = lax.broadcasted_iota(jnp.int32, (width, width), 1)
    spot = (target % PC) * (width // PC) + target // PC
    pick = jnp.where(source == spot, 1.0, 0.0).astype(BF16)
    mine = jnp.dot(mine.astype(BF16), pick, preferred_element_type=F32).astype(BF16)
    high, low = parts_of(held)
    every[...] = lax.dot_general(
        jnp.concatenate([high, low], axis=0),
        jnp.concatenate([mine, mine], axis=0),
        LEADING,
        preferred_element_type=F32,
    )
    share = delta_ref.shape[0] - 8
    first = place_ref[2] * share // 8 * 8
    window = every[pl.ds(pl.multiple_of(first, 8), 8), :]
    delta_ref[0:share, :] = jnp.where(place_ref[2] % 2 == 0, window[:share], window[share:])
    delta_ref[share:, :] = jnp.broadcast_to(total, (8, width))


def dense_delta(place, own, other, depth, spaces, outputs):
    count = depth * 16 * (own.shape[0] // spaces)
    vmem = pl.BlockSpec(memory_space=pltpu.VMEM)
    return pl.pallas_call(
        functools.partial(dense_kernel_body, depth, spaces),
        in_specs=[pl.BlockSpec(memory_space=pltpu.SMEM), vmem, vmem],
        out_specs=vmem,
        out_shape=jax.ShapeDtypeStruct((4 + 8, 64), F32),
        scratch_shapes=[
            pltpu.VMEM((count, spaces * 64), BF16),
            pltpu.VMEM((count, outputs), F32),
            pltpu.VMEM((outputs, 64), F32),
        ],
        compiler_params=pltpu.CompilerParams(vmem_limit_bytes=48 * 1024 * 1024),
    )(place, own, other)


def final_kernel_body(
    filters, patch_rows, cells, got_ref, delta_ref, order_ref,
    step_conv_ref, step_dense_ref,
):
    scale = 1.0 / cells
    moments = from_halves(got_ref[...]).reshape(-1, 64)
    pad = jnp.zeros((128 - ROWS_IN, 64), F32)
    lower = jnp.concatenate([moments[64:ROWS_IN], pad], axis=0)
    corner = jnp.concatenate([moments[ROWS_IN:2 * ROWS_IN - 64], pad], axis=0)
    upper = jnp.concatenate([moments[0:64], jnp.transpose(lower)], axis=1)
    lower = jnp.concatenate([lower, corner], axis=1)
    conv_in = jnp.concatenate([upper, lower], axis=0) * scale
    first = 2 * ROWS_IN - 64
    conv_grad = jnp.concatenate(
        [moments[first:first + filters], moments[first + filters:first + 2 * filters]],
        axis=1,
    ) * scale
    conv_out = moments[first + 2 * filters:first + 3 * filters]
    conv_out = jnp.concatenate([conv_out, jnp.zeros((filters, 64), F32)], axis=1)
    conv_out = jnp.concatenate([conv_out, jnp.zeros((128 - filters, 128), F32)], axis=0) * scale
    right, bound_in = residual(conv_in, patch_rows)
    left, bound_out = residual(conv_out, filters)
    held = two_sided(left[0:filters], conv_grad / bound_in / bound_out, right)
    total = scalar_sum(held * conv_grad) + delta_ref[4:5, 0:1]
    scaling = jnp.minimum(1.0, jnp.sqrt(KL_BOUND / (LEARN_RATE * LEARN_RATE * total)))
    moved = split_dot(held, order_ref[...])
    step_conv_ref[...] = scaling * moved[:, 0:patch_rows]
    step_dense_ref[...] = scaling * delta_ref[0:4, :]


def final_steps(moments, delta, order, filters, patch_rows, cells):
    vmem = pl.BlockSpec(memory_space=pltpu.VMEM)
    return pl.pallas_call(
        functools.partial(final_kernel_body, filters, patch_rows, cells),
        in_specs=[vmem] * 3,
        out_specs=[vmem] * 2,
        out_shape=[
            jax.ShapeDtypeStruct((filters, patch_rows), F32),
            jax.ShapeDtypeStruct((4, delta.shape[1]), F32),
        ],
        compiler_params=pltpu.CompilerParams(vmem_limit_bytes=32 * 1024 * 1024),
    )(moments, delta, order)


def column_order(channels):
    row = lax.broadcasted_iota(jnp.int32, (128, 128), 0)
    column = lax.broadcasted_iota(jnp.int32, (128, 128), 1)
    channel, i, j, k = column // 27, column // 9 % 3, column // 3 % 3, column % 3
    source = ((j * 3 + i) * channels + channel) * 3 + k
    return jnp.where(jnp.logical_and(row == source, column < 27 * channels), 1.0, 0.0)


def on_device(volume, conv_kernel, dense_weight, cotangent):
    spaces = lax.axis_size(SPACE)
    groups = lax.axis_size(DP)
    column = lax.axis_size(COLUMN)
    samples, channels, planes, height, length = volume.shape
    filters, patch_rows = conv_kernel.shape
    slab = filters * PC

    up = [(i, i + 1) for i in range(spaces - 1)]
    down = [(j, i) for i, j in up]
    before = lax.ppermute(volume[:, :, planes - 1:], SPACE, up)
    after = lax.ppermute(volume[:, :, :1], SPACE, down)
    cot_group = gather_from(cotangent[0], SPACE, spaces)

    place = lax.axis_index(SPACE)
    weight = lax.dynamic_slice_in_dim(dense_weight, place * slab, slab, 0)
    weight = weight.reshape(filters, PC, -1).transpose(1, 0, 2).reshape(slab, -1)

    sums = conv_sums(volume, before, after, conv_kernel)
    sizes = (channels, planes, planes * height * length // PC, filters, samples)
    sent = conv_moments(sizes, sums, weight, cot_group, cotangent, column)
    peers = spaces * groups // column
    core = lax.axis_index("core")
    got = exchange(sent, COLUMN).reshape(column // 2, 2, -1, 128)
    got = exchange(middle(core.reshape(1), got, peers), PLANE)
    reduced = exchange(spread(got, column), COLUMN)
    other = lax.ppermute(got[:, 256 // column:], "core", [(0, 1), (1, 0)])
    places = jnp.stack([place, core, lax.axis_index(DP)])
    delta = dense_delta(places, got, other, column // 2, spaces, cotangent.shape[1])
    cells = samples * groups * planes * spaces * height * length
    step_conv, step_dense = final_steps(
        reduced, delta, column_order(channels), filters, patch_rows, cells
    )
    return step_conv, step_dense.T


def solution(mesh):
    fine = jax.sharding.Mesh(mesh.devices.reshape(-1, 2, 2, 2, 4), ("z", "xh", "core", "xl", "y"))
    placed = (P(DP, None, SPACE, None, None), P(), P(), P(DP + SPACE, None))
    return jax.shard_map(
        on_device, mesh=fine, in_specs=placed, out_specs=(P(), P(SPACE, DP)), check_vma=False
    )
```

```python
import functools

import jax
import jax.numpy as jnp
from jax import lax
from jax.experimental import pallas as pl
from jax.experimental.pallas import tpu as pltpu
from jax.sharding import PartitionSpec as P


PC = 2
NS_STEPS = 8

LEAK_SLOPE = 0.3
DAMPING = 0.1
KL_BOUND = 0.0001
LEARN_RATE = 0.01
CONTRACT = (((1,), (1,)), ((), ()))
LEADING = (((0,), (0,)), ((), ()))
DP = ("z", "xh", "core")
SPACE = ("xl", "y")
COLUMN = ("z", "core")
PLANE = ("xh", "xl", "y")
F32 = jnp.float32
BF16 = jnp.bfloat16
ROWS_IN = 112


def exchange(x, axes):
    return lax.all_to_all(x, axes, split_axis=0, concat_axis=0, tiled=True)


def gather_from(x, axes, peers):
    return exchange(jnp.broadcast_to(x[None], (peers,) + x.shape), axes)


def turned(x, by):
    return pltpu.roll(x, x.shape[1] - by, 1) if by else x


def conv_kernel_body(
    sizes, vol_ref, before_ref, after_ref, kernel_ref, pool_ref, sums_ref, gram_ref,
    shift_a, shift_b, stack_a, stack_b, wide_a, wide_b, edges, bands_ref, taken, done,
):
    channels, planes, height, length, filters, samples = sizes
    rim = planes + 2
    group = rim * channels * 3
    rows = 3 * group
    half = height * length // PC
    top = planes * filters
    base = top + 16
    step = pl.program_id(0)

    def build(sample, shifted, stacked):
        lane = lax.broadcasted_iota(jnp.int32, (height, length), 1)
        for plane in range(rim):
            for channel in range(channels):
                if plane == 0:
                    value = before_ref[sample, channel, 0]
                elif plane == rim - 1:
                    value = after_ref[sample, channel, 0]
                else:
                    value = vol_ref[sample, channel, plane - 1]
                value = value.astype(F32)
                moved = (
                    jnp.where(lane == 0, 0.0, pltpu.roll(value, 1, 1)),
                    value,
                    jnp.where(lane == length - 1, 0.0, pltpu.roll(value, length - 1, 1)),
                )
                for k in range(3):
                    row = group + (plane * channels + channel) * 3 + k
                    shifted[pl.ds(row, height, stride=group), :] = moved[k]
        for y in range(height):
            stacked[base:, y * length:(y + 1) * length] = shifted[
                y * group:y * group + rows, :
            ].astype(BF16)

    def consume(sample, stacked, wide):
        slot = sample * PC
        pooled = []
        for part in range(PC):
            total = jnp.zeros((filters, 128), F32)
            for piece in range(2):
                first = part * half + piece * (half // 2)
                lanes = slice(first, first + half // 2)
                pre = jnp.dot(bands_ref[...], stacked[base:, lanes], preferred_element_type=F32)
                stacked[0:top, lanes] = jnp.where(pre > 0, 1.0, 0.0).astype(BF16)
                active = jnp.where(pre > 0, pre, LEAK_SLOPE * pre)
                for plane in range(planes):
                    for at in range(0, half // 2, 128):
                        total += active[plane * filters:(plane + 1) * filters, at:at + 128]
            pooled.append(jnp.sum(total, axis=1, keepdims=True))
            lanes = slice(part * half, (part + 1) * half)
            gram = lax.dot_general(
                stacked[:base + group, lanes], stacked[base:, lanes], CONTRACT,
                preferred_element_type=F32,
            )
            wide[part, :, :rows] = gram[:top + 8]
            gram_ref[:, :rows] += gram[base:]
            square = lax.dot_general(
                stacked[:base, lanes], stacked[:top, lanes], CONTRACT,
                preferred_element_type=F32,
            )
            for first, last in ((0, filters), (top, top + 8)):
                patch = jnp.zeros((last - first, 256), F32)
                mask = jnp.zeros((last - first, top), F32)
                for plane in range(planes):
                    at = slice(first, last)
                    if first == 0:
                        at = slice(plane * filters, (plane + 1) * filters)
                    patch += turned(wide[part, at, :], plane * channels * 3)
                    mask += turned(square[at], plane * filters)
                to = slice(0, filters) if first == 0 else slice(filters, filters + 8)
                sums_ref[slot + part, to, :256] = patch
                sums_ref[slot + part, to, 256:] = mask
        spot = pl.ds(pl.multiple_of(sample * length, length), length)
        for side, y in ((0, height - 1), (1, 0)):
            edges[side, :, spot] = stacked[
                base + group:base + 2 * group, y * length:(y + 1) * length
            ]
        pooled = jnp.concatenate(pooled, axis=0) * (1.0 / (planes * half))
        spot = lax.broadcasted_iota(jnp.int32, pool_ref.shape, 1)
        pool_ref[...] = jnp.where(spot == sample, pooled, pool_ref[...])

    @pl.when(step == 0)
    def _():
        fetch = pltpu.make_async_copy(kernel_ref, taken, done)
        fetch.start()
        blank = jnp.zeros((group, length), F32)
        for shifted in (shift_a, shift_b):
            shifted[0:group, :] = blank
            shifted[(height + 1) * group:, :] = blank
        ones = jnp.ones((16, height * length), BF16)
        stack_a[top:base, :] = ones
        stack_b[top:base, :] = ones
        gram_ref[...] = jnp.zeros_like(gram_ref)
        pool_ref[...] = jnp.zeros_like(pool_ref)
        build(0, shift_a, stack_a)
        at = lax.broadcasted_iota(jnp.int32, (1, 256), 1)
        j, rest = at // group, at % group
        inner = channels * 3
        i, channel, k = rest // inner, rest % inner // 3, rest % 3
        used = jnp.logical_and(rest < 3 * inner, at < rows)
        source = jnp.where(used, channel * 27 + i * 9 + j * 3 + k, -1)
        row = lax.broadcasted_iota(jnp.int32, (kernel_ref.shape[1], 256), 0)
        pick = jnp.where(row == source, 1.0, 0.0).astype(BF16)
        fetch.wait()
        band = jnp.dot(taken[...], pick, preferred_element_type=F32)
        bands_ref[...] = jnp.concatenate(
            [band] + [pltpu.roll(band, plane * inner, 1) for plane in range(1, planes)], axis=0
        )[:, :rows].astype(BF16)

    build(2 * step + 1, shift_b, stack_b)
    consume(2 * step, stack_a, wide_a)
    build(jnp.minimum(2 * step + 2, samples - 1), shift_a, stack_a)
    consume(2 * step + 1, stack_b, wide_b)

    @pl.when(step == pl.num_programs(0) - 1)
    def _():
        for side in range(2):
            gram_ref[:, 256 + side * 128:256 + side * 128 + group] = lax.dot_general(
                edges[side], edges[side], CONTRACT, preferred_element_type=F32
            )


def conv_sums(volume, before, after, conv_kernel):
    samples, channels, planes, height, length = volume.shape
    filters = conv_kernel.shape[0]
    group = (planes + 2) * channels * 3
    top = planes * filters
    stack = top + 16 + 3 * group
    sizes = (channels, planes, height, length, filters, samples)
    vmem = pl.BlockSpec(memory_space=pltpu.VMEM)
    return pl.pallas_call(
        functools.partial(conv_kernel_body, sizes),
        grid=(samples // 2,),
        in_specs=[vmem] * 3 + [pl.BlockSpec(memory_space=pltpu.HBM)],
        out_specs=[vmem] * 3,
        out_shape=[
            jax.ShapeDtypeStruct((filters * PC, 128), F32),
            jax.ShapeDtypeStruct((samples * PC, filters + 8, 256 + top), F32),
            jax.ShapeDtypeStruct((group, 512), F32),
        ],
        scratch_shapes=[
            pltpu.VMEM(((height + 2) * group, length), F32),
            pltpu.VMEM(((height + 2) * group, length), F32),
            pltpu.VMEM((stack, height * length), BF16),
            pltpu.VMEM((stack, height * length), BF16),
            pltpu.VMEM((PC, top + 8, 256), F32),
            pltpu.VMEM((PC, top + 8, 256), F32),
            pltpu.VMEM((2, group, samples * length), BF16),
            pltpu.VMEM((top, 3 * group), BF16),
            pltpu.VMEM(conv_kernel.shape, BF16),
            pltpu.SemaphoreType.DMA(()),
        ],
        compiler_params=pltpu.CompilerParams(vmem_limit_bytes=24 * 1024 * 1024),
    )(volume, before, after, pltpu.with_memory_space_constraint(conv_kernel, pltpu.HBM))


def moments_body(
    sizes, pool_ref, sums_ref, gram_ref, weight_ref, cot_ref, own_ref, sent_ref, held, turned_up,
):
    channels, planes, cells, filters, samples = sizes
    inner = channels * 3
    group = (planes + 2) * inner
    wide = 3 * 3 * inner
    part_rows = 3 * inner
    lanes_of = lambda shape: lax.broadcasted_iota(jnp.int32, shape, 1)

    def compact(x):
        lane = lanes_of(x.shape)
        out = jnp.where(lane < part_rows, x, 0.0)
        for j in range(1, 3):
            here = jnp.logical_and(lane >= j * part_rows, lane < (j + 1) * part_rows)
            out = jnp.where(here, turned(x, j * (group - part_rows)), out)
        return out[:, :128]

    cots = cot_ref[...]
    gradient = jnp.zeros((filters, 256), F32)
    moment_out = jnp.zeros((filters, 128), F32)
    cross = jnp.zeros((filters, 128), F32)
    for part in range(PC):
        weight = weight_ref[part * filters:(part + 1) * filters, :]
        grad_down = lax.dot_general(weight, cots, CONTRACT, preferred_element_type=F32)
        weight = jnp.concatenate([weight, jnp.zeros((128 - filters, 128), BF16)], axis=0)
        grad_over = lax.dot_general(cots, weight, CONTRACT, preferred_element_type=F32)
        grad_down = grad_down.astype(BF16).astype(F32)
        grad_over = grad_over.astype(BF16).astype(F32)
        low_down = (LEAK_SLOPE * grad_down).astype(BF16).astype(F32)
        low_over = (LEAK_SLOPE * grad_over).astype(BF16).astype(F32)
        gap_down = grad_down - low_down
        gap_over = grad_over - low_over
        for sample in range(samples):
            slot = sample * PC + part
            gap = gap_down[:, sample:sample + 1]
            low = low_down[:, sample:sample + 1]
            across = gap_over[sample:sample + 1, :]
            gradient += gap * sums_ref[slot, :filters, :256]
            gradient += low * sums_ref[slot, filters:filters + 1, :256]
            moment_out += gap * sums_ref[slot, :filters, 256:] * across
            cross += low * (
                across * sums_ref[slot, filters:filters + 1, 256:]
                + (0.5 * cells) * low_over[sample:sample + 1, :]
            )
    lane = lanes_of(cross.shape)
    cross = jnp.where(lane < filters, cross, 0.0)
    tall = jnp.concatenate([cross, jnp.zeros((128 - filters, 128), F32)], axis=0)
    moment_out = jnp.where(lane < filters, moment_out, 0.0)
    moment_out += cross + jnp.transpose(tall)[:filters]

    blocks = jnp.zeros((part_rows, 512), F32)
    for plane in range(planes):
        start = plane * inner
        blocks += turned(gram_ref[start:start + part_rows, :], start)
    first = compact(blocks[:, :256])
    lane = lanes_of(first.shape)
    second = first + jnp.where(lane < part_rows, blocks[:, 256:384], 0.0)
    third = second - jnp.where(lane < part_rows, blocks[:, 384:], 0.0)
    turned_up[...] = jnp.zeros_like(turned_up)
    turned_up[0:part_rows, :] = first
    turned_up[...] = jnp.transpose(turned_up[...])
    held[...] = jnp.zeros_like(held)
    held[0:part_rows, :] = first
    above = turned_up[part_rows:2 * part_rows, :]
    row = jnp.where(lane < part_rows, above, pltpu.roll(second, part_rows, 1))
    held[part_rows:2 * part_rows, :] = jnp.where(lane < wide, row, 0.0)
    row = jnp.where(
        lane < 2 * part_rows,
        pltpu.roll(above, part_rows, 1),
        pltpu.roll(third, 2 * part_rows, 1),
    )
    row = jnp.where(lane < part_rows, turned_up[2 * part_rows:wide, :], row)
    held[2 * part_rows:wide, :] = jnp.where(lane < wide, row, 0.0)
    moment_in = held[...]
    gradient = compact(gradient)
    packed = jnp.concatenate(
        [
            moment_in[:, :64],
            moment_in[64:, 64:],
            gradient[:, :64],
            gradient[:, 64:],
            moment_out[:, :64],
        ],
        axis=0,
    )
    groups = sent_ref.shape[0]
    share = packed.shape[0] // groups
    sent_ref[:, 0:share, :] = in_halves(packed).reshape(groups, share, 128)
    feats = jnp.transpose(pool_ref[...])[:samples]
    own = own_ref[...].astype(F32)
    own = jnp.concatenate([own[:, :64], own[:, 64:], jnp.zeros((samples - 2, 64), F32)], axis=0)
    both = jnp.concatenate([feats, own], axis=1).astype(BF16)
    sent_ref[:, share:, :] = jnp.broadcast_to(both[None], (groups, samples, 128))


def conv_moments(sizes, sums, weight, cot_group, own, groups):
    samples = sizes[-1]
    rows = 256 // groups + samples
    vmem = pl.BlockSpec(memory_space=pltpu.VMEM)
    return pl.pallas_call(
        functools.partial(moments_body, sizes),
        in_specs=[vmem] * 6,
        out_specs=vmem,
        out_shape=jax.ShapeDtypeStruct((groups, rows, 128), BF16),
        scratch_shapes=[pltpu.VMEM((ROWS_IN, 128), F32), pltpu.VMEM((128, 128), F32)],
        compiler_params=pltpu.CompilerParams(vmem_limit_bytes=16 * 1024 * 1024),
    )(*sums, weight, cot_group, own)


def in_halves(x):
    high = x.astype(BF16)
    low = (x - high.astype(F32)).astype(BF16)
    return jnp.concatenate([high, low], axis=1)


def from_halves(x):
    wide = x.astype(F32)
    return wide[..., :64] + wide[..., 64:]


def middle_body(core_ref, got_ref, sent_ref):
    depth, cores, rows, _ = got_ref.shape
    share = rows - 8
    chunk = jnp.sum(from_halves(got_ref[:, 0, 0:share, :]), axis=0)
    for core in range(1, cores):
        chunk += jnp.sum(from_halves(got_ref[:, core, 0:share, :]), axis=0)
    upper = core_ref[...] > 0.5
    wide = jnp.where(
        upper[None], got_ref[:, 1, share:, :].astype(F32), got_ref[:, 0, share:, :].astype(F32)
    )
    pairs = depth // 2
    feats = wide[:, :, :64]
    feats = jnp.concatenate([feats[:pairs], feats[pairs:]], axis=2).reshape(pairs * 8, 128)
    cots = jnp.concatenate([wide[:, 0, 64:], wide[:, 1, 64:]], axis=1)
    feats = feats.astype(BF16)
    cots = cots.astype(BF16)
    chunk = in_halves(chunk)
    for peer in range(sent_ref.shape[0]):
        sent_ref[peer, 0:share, :] = chunk
        sent_ref[peer, share:share + pairs * 8, :] = feats
        sent_ref[peer, share + pairs * 8:, :] = cots


def middle(core, got, peers):
    depth, _, rows, lanes = got.shape
    vmem = pl.BlockSpec(memory_space=pltpu.VMEM)
    return pl.pallas_call(
        middle_body,
        in_specs=[vmem, vmem],
        out_specs=vmem,
        out_shape=jax.ShapeDtypeStruct((peers, rows - 8 + depth * 5, lanes), BF16),
        compiler_params=pltpu.CompilerParams(vmem_limit_bytes=8 * 1024 * 1024),
    )(core, got)


def spread_body(got_ref, sent_ref):
    chunk = jnp.sum(from_halves(got_ref[...]), axis=0)
    sent_ref[...] = jnp.broadcast_to(in_halves(chunk)[None], sent_ref.shape)


def spread(got, groups):
    peers, _, lanes = got.shape
    share = 256 // groups
    return pl.pallas_call(
        spread_body,
        grid=(1,),
        in_specs=[pl.BlockSpec((peers, share, lanes), lambda i: (0, 0, 0))],
        out_specs=pl.BlockSpec((groups, share, lanes), lambda i: (0, 0, 0)),
        out_shape=jax.ShapeDtypeStruct((groups, share, lanes), BF16),
        compiler_params=pltpu.CompilerParams(vmem_limit_bytes=8 * 1024 * 1024),
    )(got)


def parts_of(x):
    high = x.astype(BF16)
    return high, (x - high.astype(F32)).astype(BF16)


def split_dot(a, b):
    a_high, a_low = parts_of(a)
    b_high, b_low = parts_of(b)
    return jnp.dot(
        jnp.concatenate([a_high, a_high, a_low], axis=1),
        jnp.concatenate([b_high, b_low, b_high], axis=0),
        preferred_element_type=F32,
    )


def square_and_apply(left, held, last):
    order = left.shape[1]
    if last:
        both = held
    else:
        both = jnp.concatenate([left, held], axis=1)
    if both.shape[0] < order:
        rest = jnp.zeros((order - both.shape[0], both.shape[1]), F32)
        both = jnp.concatenate([both, rest], axis=0)
    product = split_dot(left, both)
    if last:
        return left, held + product
    return product[:, :order], held + product[:, order:]


def square_and_extend(inverse, right, last):
    if last:
        return inverse + split_dot(inverse, right), right
    order = right.shape[0]
    product = split_dot(jnp.concatenate([inverse, right], axis=0), right)
    return inverse + product[:order], product[order:]


def two_sided(left, held, right):
    order = right.shape[0]
    inverse = jnp.where(unit(order), 1.0, 0.0) + right
    right = split_dot(right, right)
    for step in range(NS_STEPS):
        left, held = square_and_apply(left, held, step == NS_STEPS - 1)
        if step > 0:
            inverse, right = square_and_extend(inverse, right, step == NS_STEPS - 1)
    return split_dot(held, inverse)


def unit(order):
    row = lax.broadcasted_iota(jnp.int32, (order, order), 0)
    column = lax.broadcasted_iota(jnp.int32, (order, order), 1)
    return row == column


def scalar_sum(x):
    return jnp.sum(jnp.sum(x, axis=0, keepdims=True), axis=1, keepdims=True)


def residual(factor, order):
    size = factor.shape[0]
    eye = unit(size)
    trace = scalar_sum(jnp.where(eye, factor, 0.0))
    damping = DAMPING * trace / order
    sums = jnp.sum(jnp.abs(factor), axis=0, keepdims=True) + damping
    bound = jnp.max(sums, axis=1, keepdims=True)
    inside = lax.broadcasted_iota(jnp.int32, (size, size), 0) < order
    start = jnp.where(jnp.logical_and(eye, inside), 1.0 - damping / bound, 0.0)
    return start - factor / bound, bound


def dense_kernel_body(
    depth, spaces, place_ref, own_ref, other_ref, delta_ref, whole, cots, every,
):
    parts = own_ref.shape[0] // spaces
    width = 64
    block = depth * 8
    half = block // 2
    share = own_ref.shape[1] - other_ref.shape[1]
    count = parts * 2 * block
    lower = place_ref[1] == 0

    def both_cores(index):
        own = own_ref[index].astype(F32)[share:]
        other = other_ref[index].astype(F32)
        return jnp.where(lower, own, other), jnp.where(lower, other, own)

    def slab_of(index):
        pieces = []
        for part in range(parts):
            for rows in both_cores(part * spaces + index):
                pieces += [rows[:half, :width], rows[:half, width:]]
        return jnp.concatenate(pieces, axis=0)

    for slab in range(0, spaces, 2):
        pair = jnp.concatenate([slab_of(slab), slab_of(slab + 1)], axis=1)
        whole[:, slab * width:(slab + 2) * width] = pair.astype(BF16)
    for part in range(parts):
        for slab in range(spaces):
            for core, rows in enumerate(both_cores(part * spaces + slab)):
                first = (part * 2 + core) * block + slab
                cots[pl.ds(first, depth, stride=spaces), :] = rows[half:]
    cot_wide = cots[...]
    cot = cot_wide.astype(BF16)
    feats = whole[...]
    scale = 1.0 / count
    gram = lax.dot_general(feats, feats, CONTRACT, preferred_element_type=F32) * scale
    dense_in = lax.dot_general(feats, feats, LEADING, preferred_element_type=F32) * scale
    dense_out = lax.dot_general(cot, cot, LEADING, preferred_element_type=F32) * scale
    order = spaces * width
    eye = unit(count)
    damping = DAMPING * scalar_sum(jnp.where(eye, gram, 0.0)) / order
    sums = jnp.sum(jnp.abs(dense_in), axis=0, keepdims=True) + damping
    bound = jnp.max(sums, axis=1, keepdims=True)
    left = jnp.where(eye, 1.0 - damping / bound, 0.0) - gram / bound
    right, bound_out = residual(dense_out, dense_out.shape[0])
    held = two_sided(left, cot_wide * (scale / bound / bound_out), right)
    total = scalar_sum(held * split_dot(gram, cot_wide))
    mine = slab_of(place_ref[0])
    source = lax.broadcasted_iota(jnp.int32, (width, width), 0)
    target = lax.broadcasted_iota(jnp.int32, (width, width), 1)
    spot = (target % PC) * (width // PC) + target // PC
    pick = jnp.where(source == spot, 1.0, 0.0).astype(BF16)
    mine = jnp.dot(mine.astype(BF16), pick, preferred_element_type=F32).astype(BF16)
    high, low = parts_of(held)
    every[...] = lax.dot_general(
        jnp.concatenate([high, low], axis=0),
        jnp.concatenate([mine, mine], axis=0),
        LEADING,
        preferred_element_type=F32,
    )
    share = delta_ref.shape[0] - 8
    first = place_ref[2] * share // 8 * 8
    window = every[pl.ds(pl.multiple_of(first, 8), 8), :]
    delta_ref[0:share, :] = jnp.where(place_ref[2] % 2 == 0, window[:share], window[share:])
    delta_ref[share:, :] = jnp.broadcast_to(total, (8, width))


def dense_delta(place, own, other, depth, spaces, outputs):
    count = depth * 16 * (own.shape[0] // spaces)
    vmem = pl.BlockSpec(memory_space=pltpu.VMEM)
    return pl.pallas_call(
        functools.partial(dense_kernel_body, depth, spaces),
        in_specs=[pl.BlockSpec(memory_space=pltpu.SMEM), vmem, vmem],
        out_specs=vmem,
        out_shape=jax.ShapeDtypeStruct((4 + 8, 64), F32),
        scratch_shapes=[
            pltpu.VMEM((count, spaces * 64), BF16),
            pltpu.VMEM((count, outputs), F32),
            pltpu.VMEM((outputs, 64), F32),
        ],
        compiler_params=pltpu.CompilerParams(vmem_limit_bytes=48 * 1024 * 1024),
    )(place, own, other)


def final_kernel_body(
    filters, patch_rows, cells, got_ref, delta_ref, order_ref,
    step_conv_ref, step_dense_ref,
):
    scale = 1.0 / cells
    moments = from_halves(got_ref[...]).reshape(-1, 64)
    pad = jnp.zeros((128 - ROWS_IN, 64), F32)
    lower = jnp.concatenate([moments[64:ROWS_IN], pad], axis=0)
    corner = jnp.concatenate([moments[ROWS_IN:2 * ROWS_IN - 64], pad], axis=0)
    upper = jnp.concatenate([moments[0:64], jnp.transpose(lower)], axis=1)
    lower = jnp.concatenate([lower, corner], axis=1)
    conv_in = jnp.concatenate([upper, lower], axis=0) * scale
    first = 2 * ROWS_IN - 64
    conv_grad = jnp.concatenate(
        [moments[first:first + filters], moments[first + filters:first + 2 * filters]],
        axis=1,
    ) * scale
    conv_out = moments[first + 2 * filters:first + 3 * filters]
    conv_out = jnp.concatenate([conv_out, jnp.zeros((filters, 64), F32)], axis=1)
    conv_out = jnp.concatenate([conv_out, jnp.zeros((128 - filters, 128), F32)], axis=0) * scale
    right, bound_in = residual(conv_in, patch_rows)
    left, bound_out = residual(conv_out, filters)
    held = two_sided(left[0:filters], conv_grad / bound_in / bound_out, right)
    total = scalar_sum(held * conv_grad) + delta_ref[4:5, 0:1]
    scaling = jnp.minimum(1.0, jnp.sqrt(KL_BOUND / (LEARN_RATE * LEARN_RATE * total)))
    moved = split_dot(held, order_ref[...])
    step_conv_ref[...] = scaling * moved[:, 0:patch_rows]
    step_dense_ref[...] = scaling * delta_ref[0:4, :]


def final_steps(moments, delta, order, filters, patch_rows, cells):
    vmem = pl.BlockSpec(memory_space=pltpu.VMEM)
    return pl.pallas_call(
        functools.partial(final_kernel_body, filters, patch_rows, cells),
        in_specs=[vmem] * 3,
        out_specs=[vmem] * 2,
        out_shape=[
            jax.ShapeDtypeStruct((filters, patch_rows), F32),
            jax.ShapeDtypeStruct((4, delta.shape[1]), F32),
        ],
        compiler_params=pltpu.CompilerParams(vmem_limit_bytes=32 * 1024 * 1024),
    )(moments, delta, order)


def column_order(channels):
    row = lax.broadcasted_iota(jnp.int32, (128, 128), 0)
    column = lax.broadcasted_iota(jnp.int32, (128, 128), 1)
    channel, i, j, k = column // 27, column // 9 % 3, column // 3 % 3, column % 3
    source = ((j * 3 + i) * channels + channel) * 3 + k
    return jnp.where(jnp.logical_and(row == source, column < 27 * channels), 1.0, 0.0)


def on_device(volume, conv_kernel, dense_weight, cotangent):
    spaces = lax.axis_size(SPACE)
    groups = lax.axis_size(DP)
    column = lax.axis_size(COLUMN)
    samples, channels, planes, height, length = volume.shape
    filters, patch_rows = conv_kernel.shape
    slab = filters * PC

    up = [(i, i + 1) for i in range(spaces - 1)]
    down = [(j, i) for i, j in up]
    before = lax.ppermute(volume[:, :, planes - 1:], SPACE, up)
    after = lax.ppermute(volume[:, :, :1], SPACE, down)
    cot_group = gather_from(cotangent[0], SPACE, spaces)

    place = lax.axis_index(SPACE)
    weight = lax.dynamic_slice_in_dim(dense_weight, place * slab, slab, 0)
    weight = weight.reshape(filters, PC, -1).transpose(1, 0, 2).reshape(slab, -1)

    sums = conv_sums(volume, before, after, conv_kernel)
    sizes = (channels, planes, planes * height * length // PC, filters, samples)
    sent = conv_moments(sizes, sums, weight, cot_group, cotangent, column)
    peers = spaces * groups // column
    core = lax.axis_index("core")
    got = exchange(sent, COLUMN).reshape(column // 2, 2, -1, 128)
    got = exchange(middle(jnp.broadcast_to(core.astype(F32), (8, 128)), got, peers), PLANE)
    reduced = exchange(spread(got, column), COLUMN)
    other = lax.ppermute(got[:, 256 // column:], "core", [(0, 1), (1, 0)])
    places = jnp.stack([place, core, lax.axis_index(DP)])
    delta = dense_delta(places, got, other, column // 2, spaces, cotangent.shape[1])
    cells = samples * groups * planes * spaces * height * length
    step_conv, step_dense = final_steps(
        reduced, delta, column_order(channels), filters, patch_rows, cells
    )
    return step_conv, step_dense.T


def solution(mesh):
    fine = jax.sharding.Mesh(mesh.devices.reshape(-1, 2, 2, 2, 4), ("z", "xh", "core", "xl", "y"))
    placed = (P(DP, None, SPACE, None, None), P(), P(), P(DP + SPACE, None))
    return jax.shard_map(
        on_device, mesh=fine, in_specs=placed, out_specs=(P(), P(SPACE, DP)), check_vma=False
    )
```

```python
import functools

import jax
import jax.numpy as jnp
from jax import lax
from jax.experimental import pallas as pl
from jax.experimental.pallas import tpu as pltpu
from jax.sharding import PartitionSpec as P


PC = 2
NS_STEPS = 8

LEAK_SLOPE = 0.3
DAMPING = 0.1
KL_BOUND = 0.0001
LEARN_RATE = 0.01
CONTRACT = (((1,), (1,)), ((), ()))
LEADING = (((0,), (0,)), ((), ()))
DP = ("z", "xh", "core")
SPACE = ("xl", "y")
COLUMN = ("z", "core")
PLANE = ("xh", "xl", "y")
F32 = jnp.float32
BF16 = jnp.bfloat16
ROWS_IN = 112


def exchange(x, axes):
    return lax.all_to_all(x, axes, split_axis=0, concat_axis=0, tiled=True)


def gather_from(x, axes, peers):
    return exchange(jnp.broadcast_to(x[None], (peers,) + x.shape), axes)


def turned(x, by):
    return pltpu.roll(x, x.shape[1] - by, 1) if by else x


def conv_kernel_body(
    sizes, vol_ref, before_ref, after_ref, bands_ref, pool_ref, sums_ref, gram_ref,
    shift_a, shift_b, stack_a, stack_b, wide_a, wide_b, edges,
):
    channels, planes, height, length, filters, samples = sizes
    rim = planes + 2
    group = rim * channels * 3
    rows = 3 * group
    half = height * length // PC
    top = planes * filters
    base = top + 16
    step = pl.program_id(0)

    def build(sample, shifted, stacked):
        lane = lax.broadcasted_iota(jnp.int32, (height, length), 1)
        for plane in range(rim):
            for channel in range(channels):
                if plane == 0:
                    value = before_ref[sample, channel, 0]
                elif plane == rim - 1:
                    value = after_ref[sample, channel, 0]
                else:
                    value = vol_ref[sample, channel, plane - 1]
                value = value.astype(F32)
                moved = (
                    jnp.where(lane == 0, 0.0, pltpu.roll(value, 1, 1)),
                    value,
                    jnp.where(lane == length - 1, 0.0, pltpu.roll(value, length - 1, 1)),
                )
                for k in range(3):
                    row = group + (plane * channels + channel) * 3 + k
                    shifted[pl.ds(row, height, stride=group), :] = moved[k]
        for y in range(height):
            stacked[base:, y * length:(y + 1) * length] = shifted[
                y * group:y * group + rows, :
            ].astype(BF16)

    def consume(sample, stacked, wide):
        slot = sample * PC
        pooled = []
        for part in range(PC):
            total = jnp.zeros((filters, 128), F32)
            for piece in range(2):
                first = part * half + piece * (half // 2)
                lanes = slice(first, first + half // 2)
                pre = jnp.dot(bands_ref[...], stacked[base:, lanes], preferred_element_type=F32)
                stacked[0:top, lanes] = jnp.where(pre > 0, 1.0, 0.0).astype(BF16)
                active = jnp.where(pre > 0, pre, LEAK_SLOPE * pre)
                for plane in range(planes):
                    for at in range(0, half // 2, 128):
                        total += active[plane * filters:(plane + 1) * filters, at:at + 128]
            pooled.append(jnp.sum(total, axis=1, keepdims=True))
            lanes = slice(part * half, (part + 1) * half)
            gram = lax.dot_general(
                stacked[:base + group, lanes], stacked[base:, lanes], CONTRACT,
                preferred_element_type=F32,
            )
            wide[part, :, :rows] = gram[:top + 8]
            gram_ref[:, :rows] += gram[base:]
            square = lax.dot_general(
                stacked[:base, lanes], stacked[:top, lanes], CONTRACT,
                preferred_element_type=F32,
            )
            for first, last in ((0, filters), (top, top + 8)):
                patch = jnp.zeros((last - first, 256), F32)
                mask = jnp.zeros((last - first, top), F32)
                for plane in range(planes):
                    at = slice(first, last)
                    if first == 0:
                        at = slice(plane * filters, (plane + 1) * filters)
                    patch += turned(wide[part, at, :], plane * channels * 3)
                    mask += turned(square[at], plane * filters)
                to = slice(0, filters) if first == 0 else slice(filters, filters + 8)
                sums_ref[slot + part, to, :256] = patch
                sums_ref[slot + part, to, 256:] = mask
        spot = pl.ds(pl.multiple_of(sample * length, length), length)
        for side, y in ((0, height - 1), (1, 0)):
            edges[side, :, spot] = stacked[
                base + group:base + 2 * group, y * length:(y + 1) * length
            ]
        pooled = jnp.concatenate(pooled, axis=0) * (1.0 / (planes * half))
        spot = lax.broadcasted_iota(jnp.int32, pool_ref.shape, 1)
        pool_ref[...] = jnp.where(spot == sample, pooled, pool_ref[...])

    @pl.when(step == 0)
    def _():
        blank = jnp.zeros((group, length), F32)
        for shifted in (shift_a, shift_b):
            shifted[0:group, :] = blank
            shifted[(height + 1) * group:, :] = blank
        ones = jnp.ones((16, height * length), BF16)
        stack_a[top:base, :] = ones
        stack_b[top:base, :] = ones
        gram_ref[...] = jnp.zeros_like(gram_ref)
        pool_ref[...] = jnp.zeros_like(pool_ref)
        build(0, shift_a, stack_a)

    build(2 * step + 1, shift_b, stack_b)
    consume(2 * step, stack_a, wide_a)
    build(jnp.minimum(2 * step + 2, samples - 1), shift_a, stack_a)
    consume(2 * step + 1, stack_b, wide_b)

    @pl.when(step == pl.num_programs(0) - 1)
    def _():
        for side in range(2):
            gram_ref[:, 256 + side * 128:256 + side * 128 + group] = lax.dot_general(
                edges[side], edges[side], CONTRACT, preferred_element_type=F32
            )


def conv_sums(volume, before, after, bands, filters):
    samples, channels, planes, height, length = volume.shape
    group = (planes + 2) * channels * 3
    top = planes * filters
    stack = top + 16 + 3 * group
    sizes = (channels, planes, height, length, filters, samples)
    vmem = pl.BlockSpec(memory_space=pltpu.VMEM)
    return pl.pallas_call(
        functools.partial(conv_kernel_body, sizes),
        grid=(samples // 2,),
        in_specs=[vmem] * 4,
        out_specs=[vmem] * 3,
        out_shape=[
            jax.ShapeDtypeStruct((filters * PC, 128), F32),
            jax.ShapeDtypeStruct((samples * PC, filters + 8, 256 + top), F32),
            jax.ShapeDtypeStruct((group, 512), F32),
        ],
        scratch_shapes=[
            pltpu.VMEM(((height + 2) * group, length), F32),
            pltpu.VMEM(((height + 2) * group, length), F32),
            pltpu.VMEM((stack, height * length), BF16),
            pltpu.VMEM((stack, height * length), BF16),
            pltpu.VMEM((PC, top + 8, 256), F32),
            pltpu.VMEM((PC, top + 8, 256), F32),
            pltpu.VMEM((2, group, samples * length), BF16),
        ],
        compiler_params=pltpu.CompilerParams(vmem_limit_bytes=24 * 1024 * 1024),
    )(volume, before, after, bands)


def moments_body(
    sizes, pool_ref, sums_ref, gram_ref, weight_ref, cot_ref, own_ref, sent_ref, held, turned_up,
):
    channels, planes, cells, filters, samples = sizes
    inner = channels * 3
    group = (planes + 2) * inner
    wide = 3 * 3 * inner
    part_rows = 3 * inner
    lanes_of = lambda shape: lax.broadcasted_iota(jnp.int32, shape, 1)

    def compact(x):
        lane = lanes_of(x.shape)
        out = jnp.where(lane < part_rows, x, 0.0)
        for j in range(1, 3):
            here = jnp.logical_and(lane >= j * part_rows, lane < (j + 1) * part_rows)
            out = jnp.where(here, turned(x, j * (group - part_rows)), out)
        return out[:, :128]

    cots = cot_ref[...]
    gradient = jnp.zeros((filters, 256), F32)
    moment_out = jnp.zeros((filters, 128), F32)
    cross = jnp.zeros((filters, 128), F32)
    for part in range(PC):
        weight = weight_ref[part * filters:(part + 1) * filters, :]
        grad_down = lax.dot_general(weight, cots, CONTRACT, preferred_element_type=F32)
        weight = jnp.concatenate([weight, jnp.zeros((128 - filters, 128), BF16)], axis=0)
        grad_over = lax.dot_general(cots, weight, CONTRACT, preferred_element_type=F32)
        grad_down = grad_down.astype(BF16).astype(F32)
        grad_over = grad_over.astype(BF16).astype(F32)
        low_down = (LEAK_SLOPE * grad_down).astype(BF16).astype(F32)
        low_over = (LEAK_SLOPE * grad_over).astype(BF16).astype(F32)
        gap_down = grad_down - low_down
        gap_over = grad_over - low_over
        for sample in range(samples):
            slot = sample * PC + part
            gap = gap_down[:, sample:sample + 1]
            low = low_down[:, sample:sample + 1]
            across = gap_over[sample:sample + 1, :]
            gradient += gap * sums_ref[slot, :filters, :256]
            gradient += low * sums_ref[slot, filters:filters + 1, :256]
            moment_out += gap * sums_ref[slot, :filters, 256:] * across
            cross += low * (
                across * sums_ref[slot, filters:filters + 1, 256:]
                + (0.5 * cells) * low_over[sample:sample + 1, :]
            )
    lane = lanes_of(cross.shape)
    cross = jnp.where(lane < filters, cross, 0.0)
    tall = jnp.concatenate([cross, jnp.zeros((128 - filters, 128), F32)], axis=0)
    moment_out = jnp.where(lane < filters, moment_out, 0.0)
    moment_out += cross + jnp.transpose(tall)[:filters]

    blocks = jnp.zeros((part_rows, 512), F32)
    for plane in range(planes):
        start = plane * inner
        blocks += turned(gram_ref[start:start + part_rows, :], start)
    first = compact(blocks[:, :256])
    lane = lanes_of(first.shape)
    second = first + jnp.where(lane < part_rows, blocks[:, 256:384], 0.0)
    third = second - jnp.where(lane < part_rows, blocks[:, 384:], 0.0)
    turned_up[...] = jnp.zeros_like(turned_up)
    turned_up[0:part_rows, :] = first
    turned_up[...] = jnp.transpose(turned_up[...])
    held[...] = jnp.zeros_like(held)
    held[0:part_rows, :] = first
    above = turned_up[part_rows:2 * part_rows, :]
    row = jnp.where(lane < part_rows, above, pltpu.roll(second, part_rows, 1))
    held[part_rows:2 * part_rows, :] = jnp.where(lane < wide, row, 0.0)
    row = jnp.where(
        lane < 2 * part_rows,
        pltpu.roll(above, part_rows, 1),
        pltpu.roll(third, 2 * part_rows, 1),
    )
    row = jnp.where(lane < part_rows, turned_up[2 * part_rows:wide, :], row)
    held[2 * part_rows:wide, :] = jnp.where(lane < wide, row, 0.0)
    moment_in = held[...]
    gradient = compact(gradient)
    packed = jnp.concatenate(
        [
            moment_in[:, :64],
            moment_in[64:, 64:],
            gradient[:, :64],
            gradient[:, 64:],
            moment_out[:, :64],
        ],
        axis=0,
    )
    groups = sent_ref.shape[0]
    share = packed.shape[0] // groups
    sent_ref[:, 0:share, :] = in_halves(packed).reshape(groups, share, 128)
    feats = jnp.transpose(pool_ref[...])[:samples]
    own = own_ref[...].astype(F32)
    own = jnp.concatenate([own[:, :64], own[:, 64:], jnp.zeros((samples - 2, 64), F32)], axis=0)
    both = jnp.concatenate([feats, own], axis=1).astype(BF16)
    sent_ref[:, share:, :] = jnp.broadcast_to(both[None], (groups, samples, 128))


def conv_moments(sizes, sums, weight, cot_group, own, groups):
    samples = sizes[-1]
    rows = 256 // groups + samples
    vmem = pl.BlockSpec(memory_space=pltpu.VMEM)
    return pl.pallas_call(
        functools.partial(moments_body, sizes),
        in_specs=[vmem] * 6,
        out_specs=vmem,
        out_shape=jax.ShapeDtypeStruct((groups, rows, 128), BF16),
        scratch_shapes=[pltpu.VMEM((ROWS_IN, 128), F32), pltpu.VMEM((128, 128), F32)],
        compiler_params=pltpu.CompilerParams(vmem_limit_bytes=16 * 1024 * 1024),
    )(*sums, weight, cot_group, own)


def in_halves(x):
    high = x.astype(BF16)
    low = (x - high.astype(F32)).astype(BF16)
    return jnp.concatenate([high, low], axis=1)


def from_halves(x):
    wide = x.astype(F32)
    return wide[..., :64] + wide[..., 64:]


def middle_body(core_ref, got_ref, sent_ref):
    depth, cores, rows, _ = got_ref.shape
    share = rows - 8
    chunk = jnp.sum(from_halves(got_ref[:, 0, 0:share, :]), axis=0)
    for core in range(1, cores):
        chunk += jnp.sum(from_halves(got_ref[:, core, 0:share, :]), axis=0)
    upper = core_ref[...] > 0.5
    wide = jnp.where(
        upper[None], got_ref[:, 1, share:, :].astype(F32), got_ref[:, 0, share:, :].astype(F32)
    )
    pairs = depth // 2
    feats = wide[:, :, :64]
    feats = jnp.concatenate([feats[:pairs], feats[pairs:]], axis=2).reshape(pairs * 8, 128)
    cots = jnp.concatenate([wide[:, 0, 64:], wide[:, 1, 64:]], axis=1)
    feats = feats.astype(BF16)
    cots = cots.astype(BF16)
    chunk = in_halves(chunk)
    for peer in range(sent_ref.shape[0]):
        sent_ref[peer, 0:share, :] = chunk
        sent_ref[peer, share:share + pairs * 8, :] = feats
        sent_ref[peer, share + pairs * 8:, :] = cots


def middle(core, got, peers):
    depth, _, rows, lanes = got.shape
    vmem = pl.BlockSpec(memory_space=pltpu.VMEM)
    return pl.pallas_call(
        middle_body,
        in_specs=[vmem, vmem],
        out_specs=vmem,
        out_shape=jax.ShapeDtypeStruct((peers, rows - 8 + depth * 5, lanes), BF16),
        compiler_params=pltpu.CompilerParams(vmem_limit_bytes=8 * 1024 * 1024),
    )(core, got)


def spread_body(got_ref, sent_ref):
    chunk = jnp.sum(from_halves(got_ref[...]), axis=0)
    sent_ref[...] = jnp.broadcast_to(in_halves(chunk)[None], sent_ref.shape)


def spread(got, groups):
    peers, _, lanes = got.shape
    share = 256 // groups
    return pl.pallas_call(
        spread_body,
        grid=(1,),
        in_specs=[pl.BlockSpec((peers, share, lanes), lambda i: (0, 0, 0))],
        out_specs=pl.BlockSpec((groups, share, lanes), lambda i: (0, 0, 0)),
        out_shape=jax.ShapeDtypeStruct((groups, share, lanes), BF16),
        compiler_params=pltpu.CompilerParams(vmem_limit_bytes=8 * 1024 * 1024),
    )(got)


def parts_of(x):
    high = x.astype(BF16)
    return high, (x - high.astype(F32)).astype(BF16)


def split_dot(a, b):
    a_high, a_low = parts_of(a)
    b_high, b_low = parts_of(b)
    return jnp.dot(
        jnp.concatenate([a_high, a_high, a_low], axis=1),
        jnp.concatenate([b_high, b_low, b_high], axis=0),
        preferred_element_type=F32,
    )


def square_and_apply(left, held, last):
    order = left.shape[1]
    if last:
        both = held
    else:
        both = jnp.concatenate([left, held], axis=1)
    if both.shape[0] < order:
        rest = jnp.zeros((order - both.shape[0], both.shape[1]), F32)
        both = jnp.concatenate([both, rest], axis=0)
    product = split_dot(left, both)
    if last:
        return left, held + product
    return product[:, :order], held + product[:, order:]


def square_and_extend(inverse, right, last):
    if last:
        return inverse + split_dot(inverse, right), right
    order = right.shape[0]
    product = split_dot(jnp.concatenate([inverse, right], axis=0), right)
    return inverse + product[:order], product[order:]


def two_sided(left, held, right):
    order = right.shape[0]
    inverse = jnp.where(unit(order), 1.0, 0.0) + right
    right = split_dot(right, right)
    for step in range(NS_STEPS):
        left, held = square_and_apply(left, held, step == NS_STEPS - 1)
        if step > 0:
            inverse, right = square_and_extend(inverse, right, step == NS_STEPS - 1)
    return split_dot(held, inverse)


def unit(order):
    row = lax.broadcasted_iota(jnp.int32, (order, order), 0)
    column = lax.broadcasted_iota(jnp.int32, (order, order), 1)
    return row == column


def scalar_sum(x):
    return jnp.sum(jnp.sum(x, axis=0, keepdims=True), axis=1, keepdims=True)


def residual(factor, order):
    size = factor.shape[0]
    eye = unit(size)
    trace = scalar_sum(jnp.where(eye, factor, 0.0))
    damping = DAMPING * trace / order
    sums = jnp.sum(jnp.abs(factor), axis=0, keepdims=True) + damping
    bound = jnp.max(sums, axis=1, keepdims=True)
    inside = lax.broadcasted_iota(jnp.int32, (size, size), 0) < order
    start = jnp.where(jnp.logical_and(eye, inside), 1.0 - damping / bound, 0.0)
    return start - factor / bound, bound


def dense_kernel_body(
    depth, spaces, place_ref, own_ref, other_ref, delta_ref, whole, cots, every,
):
    parts = own_ref.shape[0] // spaces
    width = 64
    block = depth * 8
    half = block // 2
    share = own_ref.shape[1] - other_ref.shape[1]
    count = parts * 2 * block
    lower = place_ref[1] == 0

    def both_cores(index):
        own = own_ref[index].astype(F32)[share:]
        other = other_ref[index].astype(F32)
        return jnp.where(lower, own, other), jnp.where(lower, other, own)

    def slab_of(index):
        pieces = []
        for part in range(parts):
            for rows in both_cores(part * spaces + index):
                pieces += [rows[:half, :width], rows[:half, width:]]
        return jnp.concatenate(pieces, axis=0)

    for slab in range(0, spaces, 2):
        pair = jnp.concatenate([slab_of(slab), slab_of(slab + 1)], axis=1)
        whole[:, slab * width:(slab + 2) * width] = pair.astype(BF16)
    for part in range(parts):
        for slab in range(spaces):
            for core, rows in enumerate(both_cores(part * spaces + slab)):
                first = (part * 2 + core) * block + slab
                cots[pl.ds(first, depth, stride=spaces), :] = rows[half:]
    cot_wide = cots[...]
    cot = cot_wide.astype(BF16)
    feats = whole[...]
    scale = 1.0 / count
    gram = lax.dot_general(feats, feats, CONTRACT, preferred_element_type=F32) * scale
    dense_in = lax.dot_general(feats, feats, LEADING, preferred_element_type=F32) * scale
    dense_out = lax.dot_general(cot, cot, LEADING, preferred_element_type=F32) * scale
    order = spaces * width
    eye = unit(count)
    damping = DAMPING * scalar_sum(jnp.where(eye, gram, 0.0)) / order
    sums = jnp.sum(jnp.abs(dense_in), axis=0, keepdims=True) + damping
    bound = jnp.max(sums, axis=1, keepdims=True)
    left = jnp.where(eye, 1.0 - damping / bound, 0.0) - gram / bound
    right, bound_out = residual(dense_out, dense_out.shape[0])
    held = two_sided(left, cot_wide * (scale / bound / bound_out), right)
    total = scalar_sum(held * split_dot(gram, cot_wide))
    mine = slab_of(place_ref[0])
    source = lax.broadcasted_iota(jnp.int32, (width, width), 0)
    target = lax.broadcasted_iota(jnp.int32, (width, width), 1)
    spot = (target % PC) * (width // PC) + target // PC
    pick = jnp.where(source == spot, 1.0, 0.0).astype(BF16)
    mine = jnp.dot(mine.astype(BF16), pick, preferred_element_type=F32).astype(BF16)
    high, low = parts_of(held)
    every[...] = lax.dot_general(
        jnp.concatenate([high, low], axis=0),
        jnp.concatenate([mine, mine], axis=0),
        LEADING,
        preferred_element_type=F32,
    )
    share = delta_ref.shape[0] - 8
    first = place_ref[2] * share // 8 * 8
    window = every[pl.ds(pl.multiple_of(first, 8), 8), :]
    delta_ref[0:share, :] = jnp.where(place_ref[2] % 2 == 0, window[:share], window[share:])
    delta_ref[share:, :] = jnp.broadcast_to(total, (8, width))


def dense_delta(place, own, other, depth, spaces, outputs):
    count = depth * 16 * (own.shape[0] // spaces)
    vmem = pl.BlockSpec(memory_space=pltpu.VMEM)
    return pl.pallas_call(
        functools.partial(dense_kernel_body, depth, spaces),
        in_specs=[pl.BlockSpec(memory_space=pltpu.SMEM), vmem, vmem],
        out_specs=vmem,
        out_shape=jax.ShapeDtypeStruct((4 + 8, 64), F32),
        scratch_shapes=[
            pltpu.VMEM((count, spaces * 64), BF16),
            pltpu.VMEM((count, outputs), F32),
            pltpu.VMEM((outputs, 64), F32),
        ],
        compiler_params=pltpu.CompilerParams(vmem_limit_bytes=48 * 1024 * 1024),
    )(place, own, other)


def final_kernel_body(
    filters, patch_rows, cells, got_ref, delta_ref, order_ref,
    step_conv_ref, step_dense_ref,
):
    scale = 1.0 / cells
    moments = from_halves(got_ref[...]).reshape(-1, 64)
    pad = jnp.zeros((128 - ROWS_IN, 64), F32)
    lower = jnp.concatenate([moments[64:ROWS_IN], pad], axis=0)
    corner = jnp.concatenate([moments[ROWS_IN:2 * ROWS_IN - 64], pad], axis=0)
    upper = jnp.concatenate([moments[0:64], jnp.transpose(lower)], axis=1)
    lower = jnp.concatenate([lower, corner], axis=1)
    conv_in = jnp.concatenate([upper, lower], axis=0) * scale
    first = 2 * ROWS_IN - 64
    conv_grad = jnp.concatenate(
        [moments[first:first + filters], moments[first + filters:first + 2 * filters]],
        axis=1,
    ) * scale
    conv_out = moments[first + 2 * filters:first + 3 * filters]
    conv_out = jnp.concatenate([conv_out, jnp.zeros((filters, 64), F32)], axis=1)
    conv_out = jnp.concatenate([conv_out, jnp.zeros((128 - filters, 128), F32)], axis=0) * scale
    right, bound_in = residual(conv_in, patch_rows)
    left, bound_out = residual(conv_out, filters)
    held = two_sided(left[0:filters], conv_grad / bound_in / bound_out, right)
    total = scalar_sum(held * conv_grad) + delta_ref[4:5, 0:1]
    scaling = jnp.minimum(1.0, jnp.sqrt(KL_BOUND / (LEARN_RATE * LEARN_RATE * total)))
    moved = split_dot(held, order_ref[...])
    step_conv_ref[...] = scaling * moved[:, 0:patch_rows]
    step_dense_ref[...] = scaling * delta_ref[0:4, :]


def final_steps(moments, delta, order, filters, patch_rows, cells):
    vmem = pl.BlockSpec(memory_space=pltpu.VMEM)
    return pl.pallas_call(
        functools.partial(final_kernel_body, filters, patch_rows, cells),
        in_specs=[vmem] * 3,
        out_specs=[vmem] * 2,
        out_shape=[
            jax.ShapeDtypeStruct((filters, patch_rows), F32),
            jax.ShapeDtypeStruct((4, delta.shape[1]), F32),
        ],
        compiler_params=pltpu.CompilerParams(vmem_limit_bytes=32 * 1024 * 1024),
    )(moments, delta, order)


def column_order(channels):
    row = lax.broadcasted_iota(jnp.int32, (128, 128), 0)
    column = lax.broadcasted_iota(jnp.int32, (128, 128), 1)
    channel, i, j, k = column // 27, column // 9 % 3, column // 3 % 3, column % 3
    source = ((j * 3 + i) * channels + channel) * 3 + k
    return jnp.where(jnp.logical_and(row == source, column < 27 * channels), 1.0, 0.0)


def on_device(volume, conv_kernel, dense_weight, cotangent):
    spaces = lax.axis_size(SPACE)
    groups = lax.axis_size(DP)
    column = lax.axis_size(COLUMN)
    samples, channels, planes, height, length = volume.shape
    filters, patch_rows = conv_kernel.shape
    slab = filters * PC

    up = [(i, i + 1) for i in range(spaces - 1)]
    down = [(j, i) for i, j in up]
    before = lax.ppermute(volume[:, :, planes - 1:], SPACE, up)
    after = lax.ppermute(volume[:, :, :1], SPACE, down)
    mixed = conv_kernel.reshape(filters, channels, 3, 3, 3).transpose(0, 3, 2, 1, 4)
    mixed = mixed.reshape(filters, 3, channels * 9)
    inner = channels * 3
    spare = (planes - 1) * inner
    bands = jnp.concatenate(
        [
            jnp.pad(mixed, ((0, 0), (0, 0), (p * inner, spare - p * inner)))
            for p in range(planes)
        ],
        axis=0,
    ).reshape(planes * filters, -1)
    cot_group = gather_from(cotangent[0], SPACE, spaces)

    place = lax.axis_index(SPACE)
    weight = lax.dynamic_slice_in_dim(dense_weight, place * slab, slab, 0)
    weight = weight.reshape(filters, PC, -1).transpose(1, 0, 2).reshape(slab, -1)

    sums = conv_sums(volume, before, after, bands, filters)
    sizes = (channels, planes, planes * height * length // PC, filters, samples)
    sent = conv_moments(sizes, sums, weight, cot_group, cotangent, column)
    peers = spaces * groups // column
    core = lax.axis_index("core")
    got = exchange(sent, COLUMN).reshape(column // 2, 2, -1, 128)
    got = exchange(middle(jnp.broadcast_to(core.astype(F32), (8, 128)), got, peers), PLANE)
    reduced = exchange(spread(got, column), COLUMN)
    other = lax.ppermute(got[:, 256 // column:], "core", [(0, 1), (1, 0)])
    places = jnp.stack([place, core, lax.axis_index(DP)])
    delta = dense_delta(places, got, other, column // 2, spaces, cotangent.shape[1])
    cells = samples * groups * planes * spaces * height * length
    step_conv, step_dense = final_steps(
        reduced, delta, column_order(channels), filters, patch_rows, cells
    )
    return step_conv, step_dense.T


def solution(mesh):
    fine = jax.sharding.Mesh(mesh.devices.reshape(-1, 2, 2, 2, 4), ("z", "xh", "core", "xl", "y"))
    placed = (P(DP, None, SPACE, None, None), P(), P(), P(DP + SPACE, None))
    return jax.shard_map(
        on_device, mesh=fine, in_specs=placed, out_specs=(P(), P(SPACE, DP)), check_vma=False
    )
```

```python
import functools

import jax
import jax.numpy as jnp
from jax import lax
from jax.experimental import pallas as pl
from jax.experimental.pallas import tpu as pltpu
from jax.sharding import PartitionSpec as P


PC = 2
NS_STEPS = 8

LEAK_SLOPE = 0.3
DAMPING = 0.1
KL_BOUND = 0.0001
LEARN_RATE = 0.01
CONTRACT = (((1,), (1,)), ((), ()))
LEADING = (((0,), (0,)), ((), ()))
DP = ("z", "xh", "core")
SPACE = ("xl", "y")
COLUMN = ("z", "core")
PLANE = ("xh", "xl", "y")
F32 = jnp.float32
BF16 = jnp.bfloat16
ROWS_IN = 112


def exchange(x, axes):
    return lax.all_to_all(x, axes, split_axis=0, concat_axis=0, tiled=True)


def gather_from(x, axes, peers):
    return exchange(jnp.broadcast_to(x[None], (peers,) + x.shape), axes)


def turned(x, by):
    return pltpu.roll(x, x.shape[1] - by, 1) if by else x


def conv_kernel_body(
    sizes, vol_ref, before_ref, after_ref, bands_ref, pool_ref, sums_ref, gram_ref,
    shift_a, shift_b, stack_a, stack_b, wide_a, wide_b, edges,
):
    channels, planes, height, length, filters, samples = sizes
    rim = planes + 2
    group = rim * channels * 3
    rows = 3 * group
    half = height * length // PC
    top = planes * filters
    base = top + 16
    step = pl.program_id(0)

    def build(sample, shifted, stacked):
        lane = lax.broadcasted_iota(jnp.int32, (height, length), 1)
        for plane in range(rim):
            for channel in range(channels):
                if plane == 0:
                    value = before_ref[sample, channel, 0]
                elif plane == rim - 1:
                    value = after_ref[sample, channel, 0]
                else:
                    value = vol_ref[sample, channel, plane - 1]
                value = value.astype(F32)
                moved = (
                    jnp.where(lane == 0, 0.0, pltpu.roll(value, 1, 1)),
                    value,
                    jnp.where(lane == length - 1, 0.0, pltpu.roll(value, length - 1, 1)),
                )
                for k in range(3):
                    row = group + (plane * channels + channel) * 3 + k
                    shifted[pl.ds(row, height, stride=group), :] = moved[k]
        for y in range(height):
            stacked[base:, y * length:(y + 1) * length] = shifted[
                y * group:y * group + rows, :
            ].astype(BF16)

    def consume(sample, stacked, wide):
        slot = sample * PC
        pooled = []
        for part in range(PC):
            total = jnp.zeros((filters, 128), F32)
            for piece in range(2):
                first = part * half + piece * (half // 2)
                lanes = slice(first, first + half // 2)
                pre = jnp.dot(bands_ref[...], stacked[base:, lanes], preferred_element_type=F32)
                stacked[0:top, lanes] = jnp.where(pre > 0, 1.0, 0.0).astype(BF16)
                active = jnp.where(pre > 0, pre, LEAK_SLOPE * pre)
                for plane in range(planes):
                    for at in range(0, half // 2, 128):
                        total += active[plane * filters:(plane + 1) * filters, at:at + 128]
            pooled.append(jnp.sum(total, axis=1, keepdims=True))
            lanes = slice(part * half, (part + 1) * half)
            gram = lax.dot_general(
                stacked[:base + group, lanes], stacked[base:, lanes], CONTRACT,
                preferred_element_type=F32,
            )
            wide[part, :, :rows] = gram[:top + 8]
            gram_ref[:, :rows] += gram[base:]
            square = lax.dot_general(
                stacked[:base, lanes], stacked[:top, lanes], CONTRACT,
                preferred_element_type=F32,
            )
            for first, last in ((0, filters), (top, top + 8)):
                patch = jnp.zeros((last - first, 256), F32)
                mask = jnp.zeros((last - first, top), F32)
                for plane in range(planes):
                    at = slice(first, last)
                    if first == 0:
                        at = slice(plane * filters, (plane + 1) * filters)
                    patch += turned(wide[part, at, :], plane * channels * 3)
                    mask += turned(square[at], plane * filters)
                to = slice(0, filters) if first == 0 else slice(filters, filters + 8)
                sums_ref[slot + part, to, :256] = patch
                sums_ref[slot + part, to, 256:] = mask
        spot = pl.ds(pl.multiple_of(sample * length, length), length)
        for side, y in ((0, height - 1), (1, 0)):
            edges[side, :, spot] = stacked[
                base + group:base + 2 * group, y * length:(y + 1) * length
            ]
        pooled = jnp.concatenate(pooled, axis=0) * (1.0 / (planes * half))
        spot = lax.broadcasted_iota(jnp.int32, pool_ref.shape, 1)
        pool_ref[...] = jnp.where(spot == sample, pooled, pool_ref[...])

    @pl.when(step == 0)
    def _():
        blank = jnp.zeros((group, length), F32)
        for shifted in (shift_a, shift_b):
            shifted[0:group, :] = blank
            shifted[(height + 1) * group:, :] = blank
        ones = jnp.ones((16, height * length), BF16)
        stack_a[top:base, :] = ones
        stack_b[top:base, :] = ones
        gram_ref[...] = jnp.zeros_like(gram_ref)
        pool_ref[...] = jnp.zeros_like(pool_ref)
        build(0, shift_a, stack_a)

    build(2 * step + 1, shift_b, stack_b)
    consume(2 * step, stack_a, wide_a)
    build(jnp.minimum(2 * step + 2, samples - 1), shift_a, stack_a)
    consume(2 * step + 1, stack_b, wide_b)

    @pl.when(step == pl.num_programs(0) - 1)
    def _():
        for side in range(2):
            gram_ref[:, 256 + side * 128:256 + side * 128 + group] = lax.dot_general(
                edges[side], edges[side], CONTRACT, preferred_element_type=F32
            )


def conv_sums(volume, before, after, bands, filters):
    samples, channels, planes, height, length = volume.shape
    group = (planes + 2) * channels * 3
    top = planes * filters
    stack = top + 16 + 3 * group
    sizes = (channels, planes, height, length, filters, samples)
    vmem = pl.BlockSpec(memory_space=pltpu.VMEM)
    return pl.pallas_call(
        functools.partial(conv_kernel_body, sizes),
        grid=(samples // 2,),
        in_specs=[vmem] * 4,
        out_specs=[vmem] * 3,
        out_shape=[
            jax.ShapeDtypeStruct((filters * PC, 128), F32),
            jax.ShapeDtypeStruct((samples * PC, filters + 8, 256 + top), F32),
            jax.ShapeDtypeStruct((group, 512), F32),
        ],
        scratch_shapes=[
            pltpu.VMEM(((height + 2) * group, length), F32),
            pltpu.VMEM(((height + 2) * group, length), F32),
            pltpu.VMEM((stack, height * length), BF16),
            pltpu.VMEM((stack, height * length), BF16),
            pltpu.VMEM((PC, top + 8, 256), F32),
            pltpu.VMEM((PC, top + 8, 256), F32),
            pltpu.VMEM((2, group, samples * length), BF16),
        ],
        compiler_params=pltpu.CompilerParams(vmem_limit_bytes=24 * 1024 * 1024),
    )(volume, before, after, bands)


def moments_body(
    sizes, pool_ref, sums_ref, gram_ref, weight_ref, cot_ref, own_ref, sent_ref, held, turned_up,
):
    channels, planes, cells, filters, samples = sizes
    inner = channels * 3
    group = (planes + 2) * inner
    wide = 3 * 3 * inner
    part_rows = 3 * inner
    lanes_of = lambda shape: lax.broadcasted_iota(jnp.int32, shape, 1)

    def compact(x):
        lane = lanes_of(x.shape)
        out = jnp.where(lane < part_rows, x, 0.0)
        for j in range(1, 3):
            here = jnp.logical_and(lane >= j * part_rows, lane < (j + 1) * part_rows)
            out = jnp.where(here, turned(x, j * (group - part_rows)), out)
        return out[:, :128]

    cots = cot_ref[...]
    gradient = jnp.zeros((filters, 256), F32)
    moment_out = jnp.zeros((filters, 128), F32)
    cross = jnp.zeros((filters, 128), F32)
    for part in range(PC):
        weight = weight_ref[part * filters:(part + 1) * filters, :]
        grad_down = lax.dot_general(weight, cots, CONTRACT, preferred_element_type=F32)
        weight = jnp.concatenate([weight, jnp.zeros((128 - filters, 128), BF16)], axis=0)
        grad_over = lax.dot_general(cots, weight, CONTRACT, preferred_element_type=F32)
        grad_down = grad_down.astype(BF16).astype(F32)
        grad_over = grad_over.astype(BF16).astype(F32)
        low_down = (LEAK_SLOPE * grad_down).astype(BF16).astype(F32)
        low_over = (LEAK_SLOPE * grad_over).astype(BF16).astype(F32)
        gap_down = grad_down - low_down
        gap_over = grad_over - low_over
        for sample in range(samples):
            slot = sample * PC + part
            gap = gap_down[:, sample:sample + 1]
            low = low_down[:, sample:sample + 1]
            across = gap_over[sample:sample + 1, :]
            gradient += gap * sums_ref[slot, :filters, :256]
            gradient += low * sums_ref[slot, filters:filters + 1, :256]
            moment_out += gap * sums_ref[slot, :filters, 256:] * across
            cross += low * (
                across * sums_ref[slot, filters:filters + 1, 256:]
                + (0.5 * cells) * low_over[sample:sample + 1, :]
            )
    lane = lanes_of(cross.shape)
    cross = jnp.where(lane < filters, cross, 0.0)
    tall = jnp.concatenate([cross, jnp.zeros((128 - filters, 128), F32)], axis=0)
    moment_out = jnp.where(lane < filters, moment_out, 0.0)
    moment_out += cross + jnp.transpose(tall)[:filters]

    blocks = jnp.zeros((part_rows, 512), F32)
    for plane in range(planes):
        start = plane * inner
        blocks += turned(gram_ref[start:start + part_rows, :], start)
    first = compact(blocks[:, :256])
    lane = lanes_of(first.shape)
    second = first + jnp.where(lane < part_rows, blocks[:, 256:384], 0.0)
    third = second - jnp.where(lane < part_rows, blocks[:, 384:], 0.0)
    turned_up[...] = jnp.zeros_like(turned_up)
    turned_up[0:part_rows, :] = first
    turned_up[...] = jnp.transpose(turned_up[...])
    held[...] = jnp.zeros_like(held)
    held[0:part_rows, :] = first
    above = turned_up[part_rows:2 * part_rows, :]
    row = jnp.where(lane < part_rows, above, pltpu.roll(second, part_rows, 1))
    held[part_rows:2 * part_rows, :] = jnp.where(lane < wide, row, 0.0)
    row = jnp.where(
        lane < 2 * part_rows,
        pltpu.roll(above, part_rows, 1),
        pltpu.roll(third, 2 * part_rows, 1),
    )
    row = jnp.where(lane < part_rows, turned_up[2 * part_rows:wide, :], row)
    held[2 * part_rows:wide, :] = jnp.where(lane < wide, row, 0.0)
    moment_in = held[...]
    gradient = compact(gradient)
    packed = jnp.concatenate(
        [
            moment_in[:, :64],
            moment_in[64:, 64:],
            gradient[:, :64],
            gradient[:, 64:],
            moment_out[:, :64],
        ],
        axis=0,
    )
    groups = sent_ref.shape[0]
    share = packed.shape[0] // groups
    sent_ref[:, 0:share, :] = in_halves(packed).reshape(groups, share, 128)
    feats = jnp.transpose(pool_ref[...])[:samples]
    own = own_ref[...].astype(F32)
    own = jnp.concatenate([own[:, :64], own[:, 64:], jnp.zeros((samples - 2, 64), F32)], axis=0)
    both = jnp.concatenate([feats, own], axis=1).astype(BF16)
    sent_ref[:, share:, :] = jnp.broadcast_to(both[None], (groups, samples, 128))


def conv_moments(sizes, sums, weight, cot_group, own, groups):
    samples = sizes[-1]
    rows = 256 // groups + samples
    vmem = pl.BlockSpec(memory_space=pltpu.VMEM)
    return pl.pallas_call(
        functools.partial(moments_body, sizes),
        in_specs=[vmem] * 6,
        out_specs=vmem,
        out_shape=jax.ShapeDtypeStruct((groups, rows, 128), BF16),
        scratch_shapes=[pltpu.VMEM((ROWS_IN, 128), F32), pltpu.VMEM((128, 128), F32)],
        compiler_params=pltpu.CompilerParams(vmem_limit_bytes=16 * 1024 * 1024),
    )(*sums, weight, cot_group, own)


def in_halves(x):
    high = x.astype(BF16)
    low = (x - high.astype(F32)).astype(BF16)
    return jnp.concatenate([high, low], axis=1)


def from_halves(x):
    wide = x.astype(F32)
    return wide[..., :64] + wide[..., 64:]


def middle_body(core_ref, got_ref, sent_ref):
    depth, cores, rows, _ = got_ref.shape
    share = rows - 8
    chunk = jnp.sum(from_halves(got_ref[:, 0, 0:share, :]), axis=0)
    for core in range(1, cores):
        chunk += jnp.sum(from_halves(got_ref[:, core, 0:share, :]), axis=0)
    upper = core_ref[...] > 0.5
    wide = jnp.where(
        upper[None], got_ref[:, 1, share:, :].astype(F32), got_ref[:, 0, share:, :].astype(F32)
    )
    pairs = depth // 2
    feats = wide[:, :, :64]
    feats = jnp.concatenate([feats[:pairs], feats[pairs:]], axis=2).reshape(pairs * 8, 128)
    cots = jnp.concatenate([wide[:, 0, 64:], wide[:, 1, 64:]], axis=1)
    feats = feats.astype(BF16)
    cots = cots.astype(BF16)
    chunk = in_halves(chunk)
    for peer in range(sent_ref.shape[0]):
        sent_ref[peer, 0:share, :] = chunk
        sent_ref[peer, share:share + pairs * 8, :] = feats
        sent_ref[peer, share + pairs * 8:, :] = cots


def middle(core, got, peers):
    depth, _, rows, lanes = got.shape
    vmem = pl.BlockSpec(memory_space=pltpu.VMEM)
    return pl.pallas_call(
        middle_body,
        in_specs=[vmem, vmem],
        out_specs=vmem,
        out_shape=jax.ShapeDtypeStruct((peers, rows - 8 + depth * 5, lanes), BF16),
        compiler_params=pltpu.CompilerParams(vmem_limit_bytes=8 * 1024 * 1024),
    )(core, got)


def spread_body(got_ref, sent_ref):
    chunk = jnp.sum(from_halves(got_ref[...]), axis=0)
    sent_ref[...] = jnp.broadcast_to(in_halves(chunk)[None], sent_ref.shape)


def spread(got, groups):
    peers, _, lanes = got.shape
    share = 256 // groups
    return pl.pallas_call(
        spread_body,
        grid=(1,),
        in_specs=[pl.BlockSpec((peers, share, lanes), lambda i: (0, 0, 0))],
        out_specs=pl.BlockSpec((groups, share, lanes), lambda i: (0, 0, 0)),
        out_shape=jax.ShapeDtypeStruct((groups, share, lanes), BF16),
        compiler_params=pltpu.CompilerParams(vmem_limit_bytes=8 * 1024 * 1024),
    )(got)


def parts_of(x):
    high = x.astype(BF16)
    return high, (x - high.astype(F32)).astype(BF16)


def split_dot(a, b):
    a_high, a_low = parts_of(a)
    b_high, b_low = parts_of(b)
    return jnp.dot(
        jnp.concatenate([a_high, a_high, a_low], axis=1),
        jnp.concatenate([b_high, b_low, b_high], axis=0),
        preferred_element_type=F32,
    )


def square_and_apply(left, held, last):
    order = left.shape[1]
    if last:
        both = held
    else:
        both = jnp.concatenate([left, held], axis=1)
    if both.shape[0] < order:
        rest = jnp.zeros((order - both.shape[0], both.shape[1]), F32)
        both = jnp.concatenate([both, rest], axis=0)
    product = split_dot(left, both)
    if last:
        return left, held + product
    return product[:, :order], held + product[:, order:]


def square_and_extend(inverse, right, last):
    if last:
        return inverse + split_dot(inverse, right), right
    order = right.shape[0]
    product = split_dot(jnp.concatenate([inverse, right], axis=0), right)
    return inverse + product[:order], product[order:]


def two_sided(left, held, right):
    order = right.shape[0]
    inverse = jnp.where(unit(order), 1.0, 0.0) + right
    right = split_dot(right, right)
    for step in range(NS_STEPS):
        left, held = square_and_apply(left, held, step == NS_STEPS - 1)
        if step > 0:
            inverse, right = square_and_extend(inverse, right, step == NS_STEPS - 1)
    return split_dot(held, inverse)


def unit(order):
    row = lax.broadcasted_iota(jnp.int32, (order, order), 0)
    column = lax.broadcasted_iota(jnp.int32, (order, order), 1)
    return row == column


def scalar_sum(x):
    return jnp.sum(jnp.sum(x, axis=0, keepdims=True), axis=1, keepdims=True)


def residual(factor, order):
    size = factor.shape[0]
    eye = unit(size)
    trace = scalar_sum(jnp.where(eye, factor, 0.0))
    damping = DAMPING * trace / order
    sums = jnp.sum(jnp.abs(factor), axis=0, keepdims=True) + damping
    bound = jnp.max(sums, axis=1, keepdims=True)
    inside = lax.broadcasted_iota(jnp.int32, (size, size), 0) < order
    start = jnp.where(jnp.logical_and(eye, inside), 1.0 - damping / bound, 0.0)
    return start - factor / bound, bound


def dense_kernel_body(
    depth, spaces, place_ref, own_ref, other_ref, delta_ref, whole, cots, every,
):
    parts = own_ref.shape[0] // spaces
    width = 64
    block = depth * 8
    half = block // 2
    share = own_ref.shape[1] - other_ref.shape[1]
    count = parts * 2 * block
    lower = place_ref[1] == 0

    def both_cores(index):
        own = own_ref[index].astype(F32)[share:]
        other = other_ref[index].astype(F32)
        return jnp.where(lower, own, other), jnp.where(lower, other, own)

    def slab_of(index):
        pieces = []
        for part in range(parts):
            for rows in both_cores(part * spaces + index):
                pieces += [rows[:half, :width], rows[:half, width:]]
        return jnp.concatenate(pieces, axis=0)

    for slab in range(0, spaces, 2):
        pair = jnp.concatenate([slab_of(slab), slab_of(slab + 1)], axis=1)
        whole[:, slab * width:(slab + 2) * width] = pair.astype(BF16)
    for part in range(parts):
        for slab in range(spaces):
            for core, rows in enumerate(both_cores(part * spaces + slab)):
                first = (part * 2 + core) * block + slab
                cots[pl.ds(first, depth, stride=spaces), :] = rows[half:]
    cot_wide = cots[...]
    cot = cot_wide.astype(BF16)
    feats = whole[...]
    scale = 1.0 / count
    gram = lax.dot_general(feats, feats, CONTRACT, preferred_element_type=F32) * scale
    dense_in = lax.dot_general(feats, feats, LEADING, preferred_element_type=F32) * scale
    dense_out = lax.dot_general(cot, cot, LEADING, preferred_element_type=F32) * scale
    order = spaces * width
    eye = unit(count)
    damping = DAMPING * scalar_sum(jnp.where(eye, gram, 0.0)) / order
    sums = jnp.sum(jnp.abs(dense_in), axis=0, keepdims=True) + damping
    bound = jnp.max(sums, axis=1, keepdims=True)
    left = jnp.where(eye, 1.0 - damping / bound, 0.0) - gram / bound
    right, bound_out = residual(dense_out, dense_out.shape[0])
    held = two_sided(left, cot_wide * (scale / bound / bound_out), right)
    total = scalar_sum(held * split_dot(gram, cot_wide))
    mine = slab_of(place_ref[0])
    source = lax.broadcasted_iota(jnp.int32, (width, width), 0)
    target = lax.broadcasted_iota(jnp.int32, (width, width), 1)
    spot = (target % PC) * (width // PC) + target // PC
    pick = jnp.where(source == spot, 1.0, 0.0).astype(BF16)
    mine = jnp.dot(mine.astype(BF16), pick, preferred_element_type=F32).astype(BF16)
    high, low = parts_of(held)
    every[...] = lax.dot_general(
        jnp.concatenate([high, low], axis=0),
        jnp.concatenate([mine, mine], axis=0),
        LEADING,
        preferred_element_type=F32,
    )
    share = delta_ref.shape[0] - 8
    first = place_ref[2] * share // 8 * 8
    window = every[pl.ds(pl.multiple_of(first, 8), 8), :]
    delta_ref[0:share, :] = jnp.where(place_ref[2] % 2 == 0, window[:share], window[share:])
    delta_ref[share:, :] = jnp.broadcast_to(total, (8, width))


def dense_delta(place, own, other, depth, spaces, outputs):
    count = depth * 16 * (own.shape[0] // spaces)
    vmem = pl.BlockSpec(memory_space=pltpu.VMEM)
    return pl.pallas_call(
        functools.partial(dense_kernel_body, depth, spaces),
        in_specs=[pl.BlockSpec(memory_space=pltpu.SMEM), vmem, vmem],
        out_specs=vmem,
        out_shape=jax.ShapeDtypeStruct((4 + 8, 64), F32),
        scratch_shapes=[
            pltpu.VMEM((count, spaces * 64), BF16),
            pltpu.VMEM((count, outputs), F32),
            pltpu.VMEM((outputs, 64), F32),
        ],
        compiler_params=pltpu.CompilerParams(vmem_limit_bytes=48 * 1024 * 1024),
    )(place, own, other)


def final_kernel_body(
    filters, patch_rows, cells, got_ref, delta_ref, order_ref,
    step_conv_ref, step_dense_ref,
):
    scale = 1.0 / cells
    moments = from_halves(got_ref[...]).reshape(-1, 64)
    pad = jnp.zeros((128 - ROWS_IN, 64), F32)
    lower = jnp.concatenate([moments[64:ROWS_IN], pad], axis=0)
    corner = jnp.concatenate([moments[ROWS_IN:2 * ROWS_IN - 64], pad], axis=0)
    upper = jnp.concatenate([moments[0:64], jnp.transpose(lower)], axis=1)
    lower = jnp.concatenate([lower, corner], axis=1)
    conv_in = jnp.concatenate([upper, lower], axis=0) * scale
    first = 2 * ROWS_IN - 64
    conv_grad = jnp.concatenate(
        [moments[first:first + filters], moments[first + filters:first + 2 * filters]],
        axis=1,
    ) * scale
    conv_out = moments[first + 2 * filters:first + 3 * filters]
    conv_out = jnp.concatenate([conv_out, jnp.zeros((filters, 64), F32)], axis=1)
    conv_out = jnp.concatenate([conv_out, jnp.zeros((128 - filters, 128), F32)], axis=0) * scale
    right, bound_in = residual(conv_in, patch_rows)
    left, bound_out = residual(conv_out, filters)
    held = two_sided(left[0:filters], conv_grad / bound_in / bound_out, right)
    total = scalar_sum(held * conv_grad) + delta_ref[4:5, 0:1]
    scaling = jnp.minimum(1.0, jnp.sqrt(KL_BOUND / (LEARN_RATE * LEARN_RATE * total)))
    order = order_ref[...].astype(BF16)
    moved = jnp.dot(
        jnp.concatenate(parts_of(held), axis=1),
        jnp.concatenate([order, order], axis=0),
        preferred_element_type=F32,
    )
    step_conv_ref[...] = scaling * moved[:, 0:patch_rows]
    step_dense_ref[...] = scaling * delta_ref[0:4, :]


def final_steps(moments, delta, order, filters, patch_rows, cells):
    vmem = pl.BlockSpec(memory_space=pltpu.VMEM)
    return pl.pallas_call(
        functools.partial(final_kernel_body, filters, patch_rows, cells),
        in_specs=[vmem] * 3,
        out_specs=[vmem] * 2,
        out_shape=[
            jax.ShapeDtypeStruct((filters, patch_rows), F32),
            jax.ShapeDtypeStruct((4, delta.shape[1]), F32),
        ],
        compiler_params=pltpu.CompilerParams(vmem_limit_bytes=32 * 1024 * 1024),
    )(moments, delta, order)


def column_order(channels):
    row = lax.broadcasted_iota(jnp.int32, (128, 128), 0)
    column = lax.broadcasted_iota(jnp.int32, (128, 128), 1)
    channel, i, j, k = column // 27, column // 9 % 3, column // 3 % 3, column % 3
    source = ((j * 3 + i) * channels + channel) * 3 + k
    return jnp.where(jnp.logical_and(row == source, column < 27 * channels), 1.0, 0.0)


def on_device(volume, conv_kernel, dense_weight, cotangent):
    spaces = lax.axis_size(SPACE)
    groups = lax.axis_size(DP)
    column = lax.axis_size(COLUMN)
    samples, channels, planes, height, length = volume.shape
    filters, patch_rows = conv_kernel.shape
    slab = filters * PC

    up = [(i, i + 1) for i in range(spaces - 1)]
    down = [(j, i) for i, j in up]
    before = lax.ppermute(volume[:, :, planes - 1:], SPACE, up)
    after = lax.ppermute(volume[:, :, :1], SPACE, down)
    mixed = conv_kernel.reshape(filters, channels, 3, 3, 3).transpose(0, 3, 2, 1, 4)
    mixed = mixed.reshape(filters, 3, channels * 9)
    inner = channels * 3
    spare = (planes - 1) * inner
    bands = jnp.concatenate(
        [
            jnp.pad(mixed, ((0, 0), (0, 0), (p * inner, spare - p * inner)))
            for p in range(planes)
        ],
        axis=0,
    ).reshape(planes * filters, -1)
    cot_group = gather_from(cotangent[0], SPACE, spaces)

    place = lax.axis_index(SPACE)
    weight = lax.dynamic_slice_in_dim(dense_weight, place * slab, slab, 0)
    weight = weight.reshape(filters, PC, -1).transpose(1, 0, 2).reshape(slab, -1)

    sums = conv_sums(volume, before, after, bands, filters)
    sizes = (channels, planes, planes * height * length // PC, filters, samples)
    sent = conv_moments(sizes, sums, weight, cot_group, cotangent, column)
    peers = spaces * groups // column
    core = lax.axis_index("core")
    got = exchange(sent, COLUMN).reshape(column // 2, 2, -1, 128)
    got = exchange(middle(jnp.broadcast_to(core.astype(F32), (8, 128)), got, peers), PLANE)
    reduced = exchange(spread(got, column), COLUMN)
    other = lax.ppermute(got[:, 256 // column:], "core", [(0, 1), (1, 0)])
    places = jnp.stack([place, core, lax.axis_index(DP)])
    delta = dense_delta(places, got, other, column // 2, spaces, cotangent.shape[1])
    cells = samples * groups * planes * spaces * height * length
    step_conv, step_dense = final_steps(
        reduced, delta, column_order(channels), filters, patch_rows, cells
    )
    return step_conv, step_dense.T


def solution(mesh):
    fine = jax.sharding.Mesh(mesh.devices.reshape(-1, 2, 2, 2, 4), ("z", "xh", "core", "xl", "y"))
    placed = (P(DP, None, SPACE, None, None), P(), P(), P(DP + SPACE, None))
    return jax.shard_map(
        on_device, mesh=fine, in_specs=placed, out_specs=(P(), P(SPACE, DP)), check_vma=False
    )
```
